512 devices in a mesh: space: 64 (over x_lo, z, core), chan: 8 (over y, x_hi).
Axes of the slice: x: 4 (x_hi: 2, x_lo: 2; x = x_hi * 2 + x_lo), y: 4, z: 16, core: 2. Of those that a mesh axis runs over, the one named last changes fastest.
Arguments:
- volume: bfloat16 [64, 64, 48, 128], P('chan', 'space'), may hold values from -6 to 6
- weight: bfloat16 [64, 64, 3, 3, 3], P('chan'), may hold values from -0.15625 to 0.15625
- bias: float32 [64], P('chan'), may hold values from -3 to 3
- upstream: bfloat16 [64, 64, 48, 128], P('chan', 'space'), may hold values from -6 to 6
Outputs:
- activated: bfloat16 [64, 64, 48, 128], P('chan', 'space')
- input_grad: bfloat16 [64, 64, 48, 128], P('chan', 'space')
- weight_grad: float32 [64, 64, 3, 3, 3], P('chan')
- bias_grad: float32 [64], P('chan')
The draws below stay inside these ranges and needn't reach their ends.
All inputs are finite; a program needn't handle non-finite values.
Results may differ from the reference program's by a relative error of at most 0.008.
Values may be sent and summed in bfloat16 or wider, within the bound.
A program may use at most 64 MiB of HBM per device.

```python
import math
import jax
import jax.numpy as jnp
from jax import lax

CH = 64
HR = 48
WD = 128
DEPTH = 64


def levels(key, extent, split, least, top_value):
    loudness = 1.0
    for position, blocks in split:
        draws = jax.random.uniform(jax.random.fold_in(jax.random.fold_in(key, 6), position), (blocks,), jnp.float32, least / len(split), top_value / len(split))
        loudness = loudness * jnp.repeat(jnp.exp(draws), extent[position] // blocks).reshape((-1,) + (1,) * (len(extent) - 1 - position))
    return loudness


def bell_draw(own_key, shape, spread, bound, cuts=(), kind=jnp.bfloat16):
    loudness = levels(own_key, shape, cuts, -0.22, 0.18) if cuts else 1.0
    values = jax.random.normal(own_key, shape, jnp.float32) * spread * loudness
    return jnp.minimum(jnp.maximum(values, -bound), bound).astype(kind)


def setup_inputs(seed: int = 0) -> dict:
    key_of = jax.random.split(jax.random.key(seed), 5)
    volume = bell_draw(key_of[0], (CH, DEPTH, HR, WD), 1.0, 6.0, ((0, 8), (1, 64)))
    weight = bell_draw(key_of[1], (CH, CH, 3, 3, 3), (CH * 27) ** -0.5, 0.15625, ((0, 8),))
    bias = bell_draw(key_of[2], (CH,), 0.5, 3.0, ((0, 8),), jnp.float32)
    upstream = bell_draw(key_of[3], (CH, DEPTH, HR, WD), 1.0, 6.0, ((0, 8), (1, 64)))
    return dict(volume=volume, weight=weight, bias=bias, upstream=upstream)


leakage = 0.1

def convolve(lhs, rhs, padding):
    return lax.conv_general_dilated(lhs, rhs, (1, 1, 1), padding, dimension_numbers=('NCDHW', 'OIDHW', 'NCDHW'), preferred_element_type=jnp.float32)

def reference(volume, weight, bias, upstream):
    padding = [(1, 1), (1, 1), (1, 1)]
    preact = convolve(volume[None], weight, padding)[0] + bias[:, None, None, None].astype(jnp.float32)
    activated = (leakage * preact + (1.0 - leakage) * jax.nn.softplus(preact)).astype(jnp.bfloat16)
    delta = (upstream.astype(jnp.float32) * (leakage + (1.0 - leakage) * jax.nn.sigmoid(preact))).astype(jnp.bfloat16)
    flipped = jnp.transpose(weight, (1, 0, 2, 3, 4))[:, :, ::-1, ::-1, ::-1]
    input_grad = convolve(delta[None], flipped, padding)[0].astype(jnp.bfloat16)
    factor = 1.0 / math.sqrt(DEPTH * HR * WD)
    summed = convolve(volume[:, None], delta[:, None], padding)
    weight_grad = jnp.transpose(summed, (1, 0, 2, 3, 4)) * factor
    bias_grad = lax.optimization_barrier(jnp.sum(delta.astype(jnp.float32), axis=(1, 2, 3))) * factor
    return (activated, input_grad, weight_grad, bias_grad)
```

```python
import functools
import math

import jax
import jax.numpy as jnp
from jax import lax
from jax.experimental import pallas as pl
from jax.experimental.pallas import tpu as pltpu
from jax.sharding import PartitionSpec as P

MESH = pl.DeviceIdType.MESH
f32 = jnp.float32
bf16 = jnp.bfloat16
leakage = 0.1
LANES = 128
SHARE = 8


class Plan:
    def __init__(self, planes, ranks, rows, halves, blocks, factor):
        self.N = planes
        self.P = ranks
        self.R = rows // ranks
        self.H = rows
        self.C = SHARE * ranks
        self.X = halves
        self.B = blocks
        self.U = planes // (halves * blocks)
        self.M = self.U * self.X
        self.KW = 9 * self.C
        self.NJ = self.KW // LANES + 1
        self.KP = self.NJ * LANES
        self.T = -(-3 * self.NJ // self.M)
        self.factor = factor


def kernel(
    g, vol, up, wl, bias,
    act_o, ig_o, wg_o, bg_o,
    VS, VX, UX, WS, WG, XL, DX, DL, W1, W2, PRE, DB, ACT, ACR, IGS, IGR,
    GT, GS, GR, SB, Q1, Q2, FIN,
    v_s, v_r, u_s, u_r, w_s, w_r, p_s, p_r, d_s, d_r, a_s, a_r, i_s, i_r,
    g_s, g_r, q1_s, q1_r, q2_s, q2_r, q3_s, q3_r,
):
    N, Pn, R, C, M, B, U = g.N, g.P, g.R, g.C, g.M, g.B, g.U
    s = lax.axis_index("space")
    r = lax.axis_index("chan")
    span = B * U
    x_lo, within = s // span, s % span
    block, unit = within // U, within % U
    member = x_lo * U + unit
    pending = []

    def chan_peer(k):
        return lax.rem(r + k, Pn)

    def group_peer(k):
        m = lax.rem(member + k, M)
        return m, (m // U) * span + block * U + m % U

    def block_peer(k):
        b = lax.rem(block + k, B)
        return x_lo * span + b * U + unit

    def copy(src, dst, ssem, rsem, to_s, to_r):
        return pltpu.make_async_remote_copy(
            src_ref=src, dst_ref=dst, send_sem=ssem, recv_sem=rsem,
            device_id=(to_s, to_r), device_id_type=MESH,
        )

    def start(c):
        c.start()
        pending.append((None, c))

    around = [(ds, dr) for ds in (-1, 0, 1) for dr in (-1, 0, 1) if (ds, dr) != (0, 0)]

    def inside(ds, dr):
        ok = None
        for here, step, end in ((s, ds, N), (r, dr, Pn)):
            if step:
                near = here > 0 if step < 0 else here < end - 1
                ok = near if ok is None else jnp.logical_and(ok, near)
        return ok

    barrier = pltpu.get_barrier_semaphore()

    def greet(to_s, to_r):
        pl.semaphore_signal(barrier, inc=1, device_id=(to_s, to_r), device_id_type=MESH)

    for k in range(1, Pn):
        greet(s, chan_peer(k))
    for k in range(1, M):
        greet(group_peer(k)[1], r)
    for k in range(1, B):
        greet(block_peer(k), r)
    for ds, dr in around:
        pl.when(inside(ds, dr))(functools.partial(greet, s + ds, r + dr))
    wide_s = 1 + jnp.where(s > 0, 1, 0) + jnp.where(s < N - 1, 1, 0)
    wide_r = 1 + jnp.where(r > 0, 1, 0) + jnp.where(r < Pn - 1, 1, 0)

    tile = (SHARE, LANES)
    zero_tile = jnp.zeros(tile, bf16)
    VS[0] = zero_tile
    VS[g.H + 1] = zero_tile
    VS[pl.ds(1, g.H)] = vol[...]
    lane8 = lax.broadcasted_iota(jnp.int32, tile, 1)
    edge = g.KW % LANES
    last = pl.ds((g.NJ - 1) * LANES, LANES)
    WS[...] = wl[...]
    b0 = bias[...]
    hi = b0.astype(bf16).astype(f32)
    mid = (b0 - hi).astype(bf16).astype(f32)
    low = (b0 - hi - mid).astype(bf16).astype(f32)
    tail = wl[0, :, last].astype(f32)
    tail = jnp.where(lane8 == edge, hi, tail)
    tail = jnp.where(lane8 == edge + 1, mid, tail)
    tail = jnp.where(lane8 == edge + 2, low, tail)
    WS[0, :, last] = tail.astype(bf16)

    pl.semaphore_wait(barrier, (Pn - 1) + (M - 1) + (B - 1) + wide_s * wide_r - 1)

    vsend, wsend, usend = [], [], []
    for k in range(1, Pn):
        to = chan_peer(k)
        c = copy(VS.at[pl.ds(R * to, R + 2)], VX.at[1, :, r], v_s.at[k], v_r.at[k], s, to)
        start(c)
        vsend.append(c)
    for k in range(1, Pn):
        c = copy(WS, WG.at[r], w_s.at[k], w_r.at[k], s, chan_peer(k))
        start(c)
        wsend.append(c)
    for k in range(1, Pn):
        to = chan_peer(k)
        c = copy(up.at[pl.ds(R * to, R)], UX.at[r], u_s.at[k], u_r.at[k], s, to)
        start(c)
        usend.append(c)
    VX[1, :, r] = VS[pl.ds(R * r, R + 2)]
    UX[r] = up[pl.ds(R * r, R)]
    WG[r] = WS[...]

    def clear(ref, a):
        def body(i, _):
            ref[a, i] = jnp.zeros(ref.shape[2:], bf16)
            return 0
        lax.fori_loop(0, R + 2, body, 0)

    @pl.when(s == 0)
    def _():
        clear(VX, 0)
        clear(DX, 0)

    @pl.when(s == N - 1)
    def _():
        clear(VX, 2)
        clear(DX, 2)

    @pl.when(r == 0)
    def _():
        for a in range(3):
            DX[a, 0] = jnp.zeros((C, LANES), bf16)

    @pl.when(r == Pn - 1)
    def _():
        for a in range(3):
            DX[a, R + 1] = jnp.zeros((C, LANES), bf16)

    for c in vsend:
        c.wait_recv()

    down = copy(VX.at[1], VX.at[2], p_s.at[0], p_r.at[0], s - 1, r)
    upw = copy(VX.at[1], VX.at[0], p_s.at[1], p_r.at[1], s + 1, r)
    pl.when(s > 0)(down.start)
    pl.when(s < N - 1)(upw.start)
    pending.append((s > 0, down))
    pending.append((s < N - 1, upw))

    lane = lax.broadcasted_iota(jnp.int32, (C, LANES), 1)

    def spread(ref, out, a):
        def body(i, _):
            x = ref[a, i].astype(f32).reshape(C, LANES)
            at = pl.ds(pl.multiple_of(i * LANES, LANES), LANES)
            before = jnp.where(lane == 0, 0.0, pltpu.roll(x, 1, 1))
            after = jnp.where(lane == LANES - 1, 0.0, pltpu.roll(x, LANES - 1, 1))
            out[pl.ds((3 * a) * C, C), at] = before.astype(bf16)
            out[pl.ds((3 * a + 1) * C, C), at] = x.astype(bf16)
            out[pl.ds((3 * a + 2) * C, C), at] = after.astype(bf16)
            return 0
        lax.fori_loop(0, R + 2, body, 0)

    spread(VX, XL, 1)

    for c in wsend:
        c.wait_recv()
    for b in range(3):
        whole = WG[:, b].astype(f32).reshape(C, g.KP)
        W1[b] = whole[:, : g.KW].astype(bf16)
        if b == 0:
            end = whole[:, g.KP - LANES :]
            own = jnp.logical_and(lane >= edge, lane < edge + 3)
            bcol = jnp.sum(jnp.where(own, end, 0.0), axis=1, keepdims=True)

    pl.when(s < N - 1)(down.wait_recv)
    pl.when(s > 0)(upw.wait_recv)
    spread(VX, XL, 0)
    spread(VX, XL, 2)

    def conv(w, x):
        acc = None
        for b in range(3):
            part = jnp.dot(w[b], x[:, pl.ds(b * LANES, R * LANES)], preferred_element_type=f32)
            acc = part if acc is None else acc + part
        return acc

    PRE[...] = conv(W1, XL)

    for c in usend:
        c.wait_recv()

    dsum = jnp.zeros((C, LANES), f32)
    for j in range(R):
        p = PRE[:, pl.ds(j * LANES, LANES)] + bcol
        e = jnp.exp(-jnp.abs(p))
        soft = jnp.maximum(p, 0.0) + jnp.log(1.0 + e)
        gate = jnp.where(p >= 0.0, 1.0, e) / (1.0 + e)
        act = leakage * p + (1.0 - leakage) * soft
        ACT[:, j] = act.reshape(Pn, SHARE, LANES).astype(bf16)
        u = UX[:, j].astype(f32).reshape(C, LANES)
        d = (u * (leakage + (1.0 - leakage) * gate)).astype(bf16)
        DX[1, 1 + j] = d
        DB[:, pl.ds(j * LANES, LANES)] = d
        dsum = dsum + d.astype(f32)

    dcopies = []
    for e, (ds, dr) in enumerate(around):
        if dr == 0:
            src, dst = DX.at[1, pl.ds(1, R)], DX.at[1 - ds, pl.ds(1, R)]
        elif dr < 0:
            src, dst = DX.at[1, 1], DX.at[1 - ds, R + 1]
        else:
            src, dst = DX.at[1, R], DX.at[1 - ds, 0]
        c = copy(src, dst, d_s.at[e], d_r.at[e], s + ds, r + dr)
        pl.when(inside(ds, dr))(c.start)
        pending.append((inside(ds, dr), c))
        dcopies.append((inside(-ds, -dr), c))

    asend = []
    for k in range(1, Pn):
        to = chan_peer(k)
        c = copy(ACT.at[to], ACR.at[r], a_s.at[k], a_r.at[k], s, to)
        start(c)
        asend.append(c)
    ACR[r] = ACT[r]

    dcol = jnp.sum(dsum, axis=1, keepdims=True)
    for b in range(3):
        GT[b, :, pl.ds(0, g.KW)] = lax.dot_general(
            DB[...], XL[:, pl.ds(b * LANES, R * LANES)],
            (((1,), (1,)), ((), ())), preferred_element_type=f32,
        )
        cur = GT[b, :, last]
        cur = jnp.where(lane < edge, cur, 0.0)
        if b == 0:
            cur = jnp.where(lane == edge, dcol, cur)
        GT[b, :, last] = cur
        for to in range(Pn):
            GS[to, b] = GT[b, pl.ds(SHARE * to, SHARE), :].astype(GS.dtype)
    gsend = []
    for k in range(1, Pn):
        to = chan_peer(k)
        c = copy(GS.at[to], GR.at[r], g_s.at[k], g_r.at[k], s, to)
        start(c)
        gsend.append(c)
    GR[r] = GS[r]

    for b in range(3):
        whole = W1[2 - b].astype(f32).T
        blocks = []
        for a in range(3):
            for c_ in range(3):
                at = ((2 - a) * 3 + (2 - c_)) * C
                blocks.append(whole[at : at + C])
        W2[b] = jnp.concatenate(blocks, axis=1).astype(bf16)

    for ok, c in dcopies:
        pl.when(ok)(c.wait_recv)
    for a in range(3):
        spread(DX, DL, a)
    PRE[...] = conv(W2, DL)
    for j in range(R):
        v = PRE[:, pl.ds(j * LANES, LANES)]
        IGS[:, j] = v.reshape(Pn, SHARE, LANES).astype(bf16)
    isend = []
    for k in range(1, Pn):
        to = chan_peer(k)
        c = copy(IGS.at[to], IGR.at[r], i_s.at[k], i_r.at[k], s, to)
        start(c)
        isend.append(c)
    IGR[r] = IGS[r]

    for c in gsend:
        c.wait_recv()
    for b in range(3):
        acc = GR[0, b].astype(f32)
        for q in range(1, Pn):
            acc = acc + GR[q, b].astype(f32)
        for j in range(g.NJ):
            t = b * g.NJ + j
            SB[t // g.T, t % g.T] = acc[:, j * LANES : (j + 1) * LANES]
    for t in range(3 * g.NJ, M * g.T):
        SB[t // g.T, t % g.T] = jnp.zeros(tile, f32)
    q1send = []
    for k in range(1, M):
        m, to_s = group_peer(k)
        c = copy(SB.at[m], Q1.at[member], q1_s.at[k], q1_r.at[k], to_s, r)
        start(c)
        q1send.append(c)
    Q1[member] = SB[member]

    for c in asend:
        c.wait_recv()
    act_o[...] = ACR[...]

    for c in q1send:
        c.wait_recv()
    acc = Q1[0]
    for m in range(1, M):
        acc = acc + Q1[m]
    Q2[block] = acc
    q2send = []
    for k in range(1, B):
        c = copy(Q2.at[block], Q2.at[block], q2_s.at[k], q2_r.at[k], block_peer(k), r)
        start(c)
        q2send.append(c)
    for c in isend:
        c.wait_recv()
    ig_o[...] = IGR[...]
    for c in q2send:
        c.wait_recv()
    acc = Q2[0]
    for m in range(1, B):
        acc = acc + Q2[m]
    FIN[member] = acc * g.factor
    q3send = []
    for k in range(1, M):
        c = copy(FIN.at[member], FIN.at[member], q3_s.at[k], q3_r.at[k], group_peer(k)[1], r)
        start(c)
        q3send.append(c)
    for c in q3send:
        c.wait_recv()
    for a in range(3):
        for b in range(3):
            for c_ in range(3):
                at = (a * 3 + c_) * C
                t = b * g.NJ + at // LANES
                off = at % LANES
                wg_o[(a * 3 + b) * 3 + c_] = FIN[t // g.T, t % g.T][:, off : off + C]
    t = g.NJ - 1
    bg_o[...] = FIN[t // g.T, t % g.T]

    for ok, c in pending:
        if ok is None:
            c.wait_send()
        else:
            pl.when(ok)(c.wait_send)


def shards(g, volume, weight, bias, upstream):
    N, Pn, R, C, M, B = g.N, g.P, g.R, g.C, g.M, g.B
    vol = jnp.transpose(volume[:, 0], (1, 0, 2))
    up = jnp.transpose(upstream[:, 0], (1, 0, 2))
    wl = jnp.transpose(weight, (3, 0, 2, 4, 1)).reshape(3, SHARE, g.KW)
    wl = jnp.pad(wl, ((0, 0), (0, 0), (0, g.KP - g.KW)))
    bt = jnp.broadcast_to(bias[:, None], (SHARE, LANES))
    sds = jax.ShapeDtypeStruct
    vm = pl.BlockSpec(memory_space=pltpu.VMEM)
    rows = (R + 2) * LANES
    dma = pltpu.SemaphoreType.DMA
    V = pltpu.VMEM
    chan = [dma((Pn,)), dma((Pn,))]
    scratch = [
        V((g.H + 2, SHARE, LANES), bf16),
        V((3, R + 2, Pn, SHARE, LANES), bf16),
        V((Pn, R, SHARE, LANES), bf16),
        V((3, SHARE, g.KP), bf16),
        V((Pn, 3, SHARE, g.KP), bf16),
        V((9 * C, rows), bf16),
        V((3, R + 2, C, LANES), bf16),
        V((9 * C, rows), bf16),
        V((3, C, g.KW), bf16),
        V((3, C, g.KW), bf16),
        V((C, R * LANES), f32),
        V((C, R * LANES), bf16),
        V((Pn, R, SHARE, LANES), bf16),
        V((Pn, R, SHARE, LANES), bf16),
        V((Pn, R, SHARE, LANES), bf16),
        V((Pn, R, SHARE, LANES), bf16),
        V((3, C, g.KP), f32),
        V((Pn, 3, SHARE, g.KP), bf16),
        V((Pn, 3, SHARE, g.KP), bf16),
        V((M, g.T, SHARE, LANES), f32),
        V((M, g.T, SHARE, LANES), f32),
        V((B, g.T, SHARE, LANES), f32),
        V((M, g.T, SHARE, LANES), f32),
        *chan, *chan, *chan,
        dma((2,)), dma((2,)),
        dma((8,)), dma((8,)),
        *chan, *chan, *chan,
        dma((M,)), dma((M,)),
        dma((B,)), dma((B,)),
        dma((M,)), dma((M,)),
    ]
    act, ig, wg, bg = pl.pallas_call(
        functools.partial(kernel, g),
        out_shape=(
            sds((Pn, R, SHARE, LANES), bf16),
            sds((Pn, R, SHARE, LANES), bf16),
            sds((27, SHARE, C), f32),
            sds((SHARE, LANES), f32),
        ),
        in_specs=[vm] * 4,
        out_specs=(vm,) * 4,
        scratch_shapes=scratch,
        compiler_params=pltpu.CompilerParams(
            collective_id=0, has_side_effects=True, vmem_limit_bytes=40 << 20
        ),
    )(vol, up, wl, bt)

    def back(x):
        return jnp.transpose(x.reshape(g.H, SHARE, LANES), (1, 0, 2))[:, None]

    wgrad = jnp.transpose(wg.reshape(3, 3, 3, SHARE, C), (3, 4, 0, 1, 2))
    return back(act), back(ig), wgrad, bg[:, g.KW % LANES]


def solution(mesh, rows=48, halves=2, blocks=4):
    planes, ranks = mesh.shape["space"], mesh.shape["chan"]
    factor = 1.0 / math.sqrt(planes * rows * LANES)
    g = Plan(planes, ranks, rows, halves, blocks, factor)
    field = P("chan", "space", None, None)
    filters = P("chan", None, None, None, None)
    return jax.shard_map(
        functools.partial(shards, g),
        mesh=mesh,
        in_specs=(field, filters, P("chan"), field),
        out_specs=(field, field, filters, P("chan")),
        check_vma=False,
    )
```

```python
import functools
import math

import jax
import jax.numpy as jnp
from jax import lax
from jax.experimental import pallas as pl
from jax.experimental.pallas import tpu as pltpu
from jax.sharding import PartitionSpec as P

MESH = pl.DeviceIdType.MESH
f32 = jnp.float32
bf16 = jnp.bfloat16
leakage = 0.1
LANES = 128
SHARE = 8


class Plan:
    def __init__(self, planes, ranks, rows, halves, blocks, factor):
        self.N = planes
        self.P = ranks
        self.R = rows // ranks
        self.H = rows
        self.C = SHARE * ranks
        self.X = halves
        self.B = blocks
        self.U = planes // (halves * blocks)
        self.M = self.U * self.X
        self.KW = 9 * self.C
        self.NJ = self.KW // LANES + 1
        self.KP = self.NJ * LANES
        self.T = -(-3 * self.NJ // self.M)
        self.factor = factor


def kernel(
    g, vol, up, wl, bias,
    act_o, ig_o, wg_o, bg_o,
    RAW, RAWW, TALL, SEND, RCV, HV, XL, DX, DL, W1, W2, PRE, DB, AIS, AIR,
    GT, GS, GR, SB, Q1, Q2, FIN, OUTS, OUTW, OUTB,
    l_s, o_s, v_s, v_r, p_s, p_r, d_s, d_r, i_s, i_r,
    g_s, g_r, q1_s, q1_r, q2_s, q2_r, q3_s, q3_r,
):
    N, Pn, R, C, M, B, U = g.N, g.P, g.R, g.C, g.M, g.B, g.U
    s = lax.axis_index("space")
    r = lax.axis_index("chan")
    span = B * U
    x_lo, within = s // span, s % span
    block, unit = within // U, within % U
    member = x_lo * U + unit
    pending = []

    def chan_peer(k):
        return lax.rem(r + k, Pn)

    def group_peer(k):
        m = lax.rem(member + k, M)
        return m, (m // U) * span + block * U + m % U

    def block_peer(k):
        b = lax.rem(block + k, B)
        return x_lo * span + b * U + unit

    def copy(src, dst, ssem, rsem, to_s, to_r):
        return pltpu.make_async_remote_copy(
            src_ref=src, dst_ref=dst, send_sem=ssem, recv_sem=rsem,
            device_id=(to_s, to_r), device_id_type=MESH,
        )

    def start(c):
        c.start()
        pending.append((None, c))

    around = [(ds, dr) for ds in (-1, 0, 1) for dr in (-1, 0, 1) if (ds, dr) != (0, 0)]

    def inside(ds, dr):
        ok = None
        for here, step, end in ((s, ds, N), (r, dr, Pn)):
            if step:
                near = here > 0 if step < 0 else here < end - 1
                ok = near if ok is None else jnp.logical_and(ok, near)
        return ok

    barrier = pltpu.get_barrier_semaphore()

    def greet(to_s, to_r):
        pl.semaphore_signal(barrier, inc=1, device_id=(to_s, to_r), device_id_type=MESH)

    for k in range(1, Pn):
        greet(s, chan_peer(k))
    for k in range(1, M):
        greet(group_peer(k)[1], r)
    for k in range(1, B):
        greet(block_peer(k), r)
    for ds, dr in around:
        pl.when(inside(ds, dr))(functools.partial(greet, s + ds, r + dr))
    wide_s = 1 + jnp.where(s > 0, 1, 0) + jnp.where(s < N - 1, 1, 0)
    wide_r = 1 + jnp.where(r > 0, 1, 0) + jnp.where(r < Pn - 1, 1, 0)

    V, Wt = R + 2, 2 * R + 2
    loads = [
        pltpu.make_async_copy(vol, RAW.at[0], l_s.at[0]),
        pltpu.make_async_copy(up, RAW.at[1], l_s.at[1]),
        pltpu.make_async_copy(wl, RAWW, l_s.at[2]),
    ]
    for c in loads:
        c.start()
    tile = (SHARE, LANES)
    edge = g.KW % LANES
    for c in loads:
        c.wait()
    sub = lax.broadcasted_iota(jnp.int32, (SHARE, g.KP - g.KW), 0)
    col = lax.broadcasted_iota(jnp.int32, (SHARE, g.KP - g.KW), 1)
    b0 = jnp.zeros((SHARE, g.KP - g.KW), f32)
    for q in range(SHARE):
        b0 = jnp.where(sub == q, bias[q], b0)
    hi = b0.astype(bf16).astype(f32)
    mid = (b0 - hi).astype(bf16).astype(f32)
    low = (b0 - hi - mid).astype(bf16).astype(f32)
    tail = jnp.where(col == 0, hi, jnp.where(col == 1, mid, jnp.where(col == 2, low, 0.0)))
    for b in range(3):
        taps = [RAWW[(a * 3 + b) * 3 + c_].astype(f32) for a in range(3) for c_ in range(3)]
        whole = jnp.concatenate(taps + [tail], axis=1)
        for j in range(g.NJ):
            part = whole[:, j * LANES : (j + 1) * LANES].astype(bf16)
            for to in range(Pn):
                SEND[to, Wt + b * g.NJ + j] = part
    for n in range(2):
        TALL[n] = RAW[n].astype(f32).reshape(SHARE * g.H, LANES)
    zero_tile = jnp.zeros(tile, bf16)
    SEND[0, 0] = zero_tile
    SEND[Pn - 1, R + 1] = zero_tile
    for h in range(g.H):
        row = TALL[0, pl.ds(h, SHARE, stride=g.H), :].astype(bf16)
        for to in range(Pn):
            if 0 <= h + 1 - R * to < V:
                SEND[to, h + 1 - R * to] = row
        SEND[h // R, V + h % R] = TALL[1, pl.ds(h, SHARE, stride=g.H), :].astype(bf16)

    pl.semaphore_wait(barrier, (Pn - 1) + (M - 1) + (B - 1) + wide_s * wide_r - 1)

    vsend = []
    for k in range(1, Pn):
        to = chan_peer(k)
        c = copy(SEND.at[to], RCV.at[r], v_s.at[k], v_r.at[k], s, to)
        start(c)
        vsend.append(c)
    RCV[r] = SEND[r]

    def clear(ref, a):
        def body(i, _):
            ref[a, i] = jnp.zeros(ref.shape[2:], bf16)
            return 0
        lax.fori_loop(0, R + 2, body, 0)

    def clear_rows(ref, a):
        def body(i, _):
            ref[a, i] = jnp.zeros(ref.shape[2:], bf16)
            return 0
        lax.fori_loop(0, Pn, body, 0)

    @pl.when(s == 0)
    def _():
        clear_rows(HV, 0)
        clear(DX, 0)

    @pl.when(s == N - 1)
    def _():
        clear_rows(HV, 1)
        clear(DX, 2)

    @pl.when(r == 0)
    def _():
        for a in range(3):
            DX[a, 0] = jnp.zeros((C, LANES), bf16)

    @pl.when(r == Pn - 1)
    def _():
        for a in range(3):
            DX[a, R + 1] = jnp.zeros((C, LANES), bf16)

    for c in vsend:
        c.wait_recv()

    mine = RCV.at[:, pl.ds(0, V)]
    down = copy(mine, HV.at[1], p_s.at[0], p_r.at[0], s - 1, r)
    upw = copy(mine, HV.at[0], p_s.at[1], p_r.at[1], s + 1, r)
    pl.when(s > 0)(down.start)
    pl.when(s < N - 1)(upw.start)
    pending.append((s > 0, down))
    pending.append((s < N - 1, upw))

    last = pl.ds((g.NJ - 1) * LANES, LANES)
    lane = lax.broadcasted_iota(jnp.int32, (C, LANES), 1)

    def spread(row, out, a):
        def body(i, _):
            x = row(i).astype(f32).reshape(C, LANES)
            at = pl.ds(pl.multiple_of(i * LANES, LANES), LANES)
            before = jnp.where(lane == 0, 0.0, pltpu.roll(x, 1, 1))
            after = jnp.where(lane == LANES - 1, 0.0, pltpu.roll(x, LANES - 1, 1))
            out[pl.ds((3 * a) * C, C), at] = before.astype(bf16)
            out[pl.ds((3 * a + 1) * C, C), at] = x.astype(bf16)
            out[pl.ds((3 * a + 2) * C, C), at] = after.astype(bf16)
            return 0
        lax.fori_loop(0, R + 2, body, 0)

    spread(lambda i: RCV[:, i], XL, 1)

    for b in range(3):
        whole = jnp.concatenate(
            [RCV[:, Wt + b * g.NJ + j].astype(f32).reshape(C, LANES) for j in range(g.NJ)], axis=1
        )
        W1[b] = whole[:, : g.KW].astype(bf16)
        if b == 0:
            end = whole[:, g.KP - LANES :]
            own = jnp.logical_and(lane >= edge, lane < edge + 3)
            bcol = jnp.sum(jnp.where(own, end, 0.0), axis=1, keepdims=True)

    pl.when(s < N - 1)(down.wait_recv)
    pl.when(s > 0)(upw.wait_recv)
    spread(lambda i: HV[0, :, i], XL, 0)
    spread(lambda i: HV[1, :, i], XL, 2)

    def conv(w, x):
        acc = None
        for b in range(3):
            part = jnp.dot(w[b], x[:, pl.ds(b * LANES, R * LANES)], preferred_element_type=f32)
            acc = part if acc is None else acc + part
        return acc

    PRE[...] = conv(W1, XL)

    dsum = jnp.zeros((C, LANES), f32)
    for j in range(R):
        p = PRE[:, pl.ds(j * LANES, LANES)] + bcol
        e = jnp.exp(-jnp.abs(p))
        soft = jnp.maximum(p, 0.0) + jnp.log(1.0 + e)
        gate = jnp.where(p >= 0.0, 1.0, e) / (1.0 + e)
        act = leakage * p + (1.0 - leakage) * soft
        AIS[:, 0, j] = act.reshape(Pn, SHARE, LANES).astype(bf16)
        u = RCV[:, V + j].astype(f32).reshape(C, LANES)
        d = (u * (leakage + (1.0 - leakage) * gate)).astype(bf16)
        DX[1, 1 + j] = d
        DB[:, pl.ds(j * LANES, LANES)] = d
        dsum = dsum + d.astype(f32)

    dcol = jnp.sum(dsum, axis=1, keepdims=True)
    for b in range(3):
        GT[b, :, pl.ds(0, g.KW)] = lax.dot_general(
            DB[...], XL[:, pl.ds(b * LANES, R * LANES)],
            (((1,), (1,)), ((), ())), preferred_element_type=f32,
        )
        cur = GT[b, :, last]
        cur = jnp.where(lane < edge, cur, 0.0)
        if b == 0:
            cur = jnp.where(lane == edge, dcol, cur)
        GT[b, :, last] = cur
        for to in range(Pn):
            GS[to, b] = GT[b, pl.ds(SHARE * to, SHARE), :].astype(GS.dtype)
    gsend = []
    for k in range(1, Pn):
        to = chan_peer(k)
        c = copy(GS.at[to], GR.at[r], g_s.at[k], g_r.at[k], s, to)
        start(c)
        gsend.append(c)
    GR[r] = GS[r]

    dcopies = []
    for e, (ds, dr) in enumerate(around):
        if dr == 0:
            src, dst = DX.at[1, pl.ds(1, R)], DX.at[1 - ds, pl.ds(1, R)]
        elif dr < 0:
            src, dst = DX.at[1, 1], DX.at[1 - ds, R + 1]
        else:
            src, dst = DX.at[1, R], DX.at[1 - ds, 0]
        c = copy(src, dst, d_s.at[e], d_r.at[e], s + ds, r + dr)
        pl.when(inside(ds, dr))(c.start)
        pending.append((inside(ds, dr), c))
        dcopies.append((inside(-ds, -dr), c))

    for b in range(3):
        whole = W1[2 - b].astype(f32).T
        blocks = []
        for a in range(3):
            for c_ in range(3):
                at = ((2 - a) * 3 + (2 - c_)) * C
                blocks.append(whole[at : at + C])
        W2[b] = jnp.concatenate(blocks, axis=1).astype(bf16)

    for c in gsend:
        c.wait_recv()
    for b in range(3):
        acc = GR[0, b].astype(f32)
        for q in range(1, Pn):
            acc = acc + GR[q, b].astype(f32)
        for j in range(g.NJ):
            t = b * g.NJ + j
            SB[t // g.T, t % g.T] = acc[:, j * LANES : (j + 1) * LANES]
    for t in range(3 * g.NJ, M * g.T):
        SB[t // g.T, t % g.T] = jnp.zeros(tile, f32)
    q1send = []
    for k in range(1, M):
        m, to_s = group_peer(k)
        c = copy(SB.at[m], Q1.at[member], q1_s.at[k], q1_r.at[k], to_s, r)
        start(c)
        q1send.append(c)
    Q1[member] = SB[member]

    for ok, c in dcopies:
        pl.when(ok)(c.wait_recv)
    for a in range(3):
        spread(lambda i, a=a: DX[a, i], DL, a)
    PRE[...] = conv(W2, DL)
    for j in range(R):
        v = PRE[:, pl.ds(j * LANES, LANES)]
        AIS[:, 1, j] = v.reshape(Pn, SHARE, LANES).astype(bf16)
    isend = []
    for k in range(1, Pn):
        to = chan_peer(k)
        c = copy(AIS.at[to], AIR.at[r], i_s.at[k], i_r.at[k], s, to)
        start(c)
        isend.append(c)
    AIR[r] = AIS[r]

    for c in q1send:
        c.wait_recv()
    acc = Q1[0]
    for m in range(1, M):
        acc = acc + Q1[m]
    Q2[block] = acc
    q2send = []
    for k in range(1, B):
        c = copy(Q2.at[block], Q2.at[block], q2_s.at[k], q2_r.at[k], block_peer(k), r)
        start(c)
        q2send.append(c)
    for c in isend:
        c.wait_recv()
    leave = []
    for n, out in enumerate((act_o, ig_o)):
        TALL[n] = AIR[:, n].astype(f32).reshape(g.H * SHARE, LANES)
        for q in range(SHARE):
            OUTS[n, q] = TALL[n, pl.ds(q, g.H, stride=SHARE), :].astype(bf16)
        leave.append(pltpu.make_async_copy(OUTS.at[n], out, o_s.at[n]))
        leave[n].start()
    for c in q2send:
        c.wait_recv()
    acc = Q2[0]
    for m in range(1, B):
        acc = acc + Q2[m]
    FIN[member] = acc * g.factor
    q3send = []
    for k in range(1, M):
        c = copy(FIN.at[member], FIN.at[member], q3_s.at[k], q3_r.at[k], group_peer(k)[1], r)
        start(c)
        q3send.append(c)
    for c in q3send:
        c.wait_recv()
    for a in range(3):
        for b in range(3):
            for c_ in range(3):
                at = (a * 3 + c_) * C
                t = b * g.NJ + at // LANES
                off = at % LANES
                OUTW[(a * 3 + b) * 3 + c_] = FIN[t // g.T, t % g.T][:, off : off + C]
    t = g.NJ - 1
    sums = FIN[t // g.T, t % g.T][:, edge : edge + 1]
    spot = lax.broadcasted_iota(jnp.int32, tile, 0) == lax.broadcasted_iota(jnp.int32, tile, 1)
    OUTB[...] = jnp.sum(jnp.where(spot, sums, 0.0), axis=0, keepdims=True)[:, :SHARE]
    for n, (a, b) in enumerate(((OUTW, wg_o), (OUTB, bg_o))):
        leave.append(pltpu.make_async_copy(a, b, o_s.at[2 + n]))
        leave[-1].start()

    for ok, c in pending:
        if ok is None:
            c.wait_send()
        else:
            pl.when(ok)(c.wait_send)
    for c in leave:
        c.wait()


def deliver(act, ig, wg, bg, act_o, ig_o, wg_o, bg_o, sems):
    pairs = ((act, act_o), (ig, ig_o), (wg, wg_o), (bg, bg_o))
    moves = [pltpu.make_async_copy(a, b, sems.at[i]) for i, (a, b) in enumerate(pairs)]
    for c in moves:
        c.start()
    for c in moves:
        c.wait()


def shards(g, volume, weight, bias, upstream):
    Pn, R, C, M, B = g.P, g.R, g.C, g.M, g.B
    vol, up = volume[:, 0], upstream[:, 0]
    wl = jnp.transpose(weight, (2, 3, 4, 0, 1)).reshape(27, SHARE, C)
    sds = jax.ShapeDtypeStruct
    hbm = pl.BlockSpec(memory_space=pltpu.HBM)
    rows = (R + 2) * LANES
    dma = pltpu.SemaphoreType.DMA
    V = pltpu.VMEM
    chan = [dma((Pn,)), dma((Pn,))]
    scratch = [
        V((2, SHARE, g.H, LANES), bf16),
        V((27, SHARE, C), bf16),
        V((2, SHARE * g.H, LANES), f32),
        V((Pn, 2 * R + 2 + 3 * g.NJ, SHARE, LANES), bf16),
        V((Pn, 2 * R + 2 + 3 * g.NJ, SHARE, LANES), bf16),
        V((2, Pn, R + 2, SHARE, LANES), bf16),
        V((9 * C, rows), bf16),
        V((3, R + 2, C, LANES), bf16),
        V((9 * C, rows), bf16),
        V((3, C, g.KW), bf16),
        V((3, C, g.KW), bf16),
        V((C, R * LANES), f32),
        V((C, R * LANES), bf16),
        V((Pn, 2, R, SHARE, LANES), bf16),
        V((Pn, 2, R, SHARE, LANES), bf16),
        V((3, C, g.KP), f32),
        V((Pn, 3, SHARE, g.KP), bf16),
        V((Pn, 3, SHARE, g.KP), bf16),
        V((M, g.T, SHARE, LANES), f32),
        V((M, g.T, SHARE, LANES), f32),
        V((B, g.T, SHARE, LANES), f32),
        V((M, g.T, SHARE, LANES), f32),
        V((2, SHARE, g.H, LANES), bf16),
        V((27, SHARE, C), f32),
        V((1, SHARE), f32),
        dma((3,)),
        dma((4,)),
        *chan,
        dma((2,)), dma((2,)),
        dma((8,)), dma((8,)),
        *chan, *chan,
        dma((M,)), dma((M,)),
        dma((B,)), dma((B,)),
        dma((M,)), dma((M,)),
    ]
    act, ig, wg, bg = pl.pallas_call(
        functools.partial(kernel, g),
        out_shape=(
            sds((SHARE, g.H, LANES), bf16),
            sds((SHARE, g.H, LANES), bf16),
            sds((27, SHARE, C), f32),
            sds((1, SHARE), f32),
        ),
        in_specs=[hbm, hbm, hbm, pl.BlockSpec(memory_space=pltpu.SMEM)],
        out_specs=(hbm,) * 4,
        scratch_shapes=scratch,
        compiler_params=pltpu.CompilerParams(
            collective_id=0, has_side_effects=True, vmem_limit_bytes=62 << 20
        ),
    )(vol, up, wl, bias)
    act, ig, wg, bg = pl.pallas_call(
        deliver,
        out_shape=(
            sds((SHARE, g.H, LANES), bf16),
            sds((SHARE, g.H, LANES), bf16),
            sds((27, SHARE, C), f32),
            sds((1, SHARE), f32),
        ),
        in_specs=[hbm] * 4,
        out_specs=(hbm,) * 4,
        scratch_shapes=[dma((4,))],
    )(act, ig, wg, bg)
    wgrad = jnp.transpose(wg.reshape(3, 3, 3, SHARE, C), (3, 4, 0, 1, 2))
    return act[:, None], ig[:, None], wgrad, bg[0]


def solution(mesh, rows=48, halves=2, blocks=8):
    planes, ranks = mesh.shape["space"], mesh.shape["chan"]
    factor = 1.0 / math.sqrt(planes * rows * LANES)
    g = Plan(planes, ranks, rows, halves, blocks, factor)
    field = P("chan", "space", None, None)
    filters = P("chan", None, None, None, None)
    return jax.shard_map(
        functools.partial(shards, g),
        mesh=mesh,
        in_specs=(field, filters, P("chan"), field),
        out_specs=(field, field, filters, P("chan")),
        check_vma=False,
    )
```

```python
import functools
import math

import jax
import jax.numpy as jnp
from jax import lax
from jax.experimental import pallas as pl
from jax.experimental.pallas import tpu as pltpu
from jax.sharding import PartitionSpec as P

MESH = pl.DeviceIdType.MESH
f32 = jnp.float32
bf16 = jnp.bfloat16
leakage = 0.1
LANES = 128
SHARE = 8


class Plan:
    def __init__(self, planes, ranks, rows, halves, blocks, factor):
        self.N = planes
        self.P = ranks
        self.R = rows // ranks
        self.H = rows
        self.C = SHARE * ranks
        self.X = halves
        self.B = blocks
        self.U = planes // (halves * blocks)
        self.M = self.U * self.X
        self.KW = 9 * self.C
        self.NJ = self.KW // LANES + 1
        self.KP = self.NJ * LANES
        self.T = -(-3 * self.NJ // self.M)
        self.factor = factor


def kernel(
    g, vol, up, wl, bias,
    act_o, ig_o, wg_o, bg_o,
    RAW, RAWW, TALL, SENDV, SENDW, RCVV, RCVW, HV, XL, DX, DL, W1, W2, PRE, DB, AIS, AIR,
    GT, GS, GR, SB, Q1, Q2, FIN, OUTS, OUTW, OUTB,
    l_s, o_s, v_s, v_r, w_s, w_r, far, p_s, p_r, d_s, d_r, i_s, i_r,
    g_s, g_r, q1_s, q1_r, q2_s, q2_r, q3_s, q3_r,
):
    N, Pn, R, C, M, B, U = g.N, g.P, g.R, g.C, g.M, g.B, g.U
    s = lax.axis_index("space")
    r = lax.axis_index("chan")
    span = B * U
    x_lo, within = s // span, s % span
    block, unit = within // U, within % U
    member = x_lo * U + unit
    pending = []

    def chan_peer(k):
        return lax.rem(r + k, Pn)

    def group_peer(k):
        m = lax.rem(member + k, M)
        return m, (m // U) * span + block * U + m % U

    def block_peer(k):
        b = lax.rem(block + k, B)
        return x_lo * span + b * U + unit

    def copy(src, dst, ssem, rsem, to_s, to_r):
        return pltpu.make_async_remote_copy(
            src_ref=src, dst_ref=dst, send_sem=ssem, recv_sem=rsem,
            device_id=(to_s, to_r), device_id_type=MESH,
        )

    def start(c):
        c.start()
        pending.append((None, c))

    around = [(ds, dr) for ds in (-1, 0, 1) for dr in (-1, 0, 1) if (ds, dr) != (0, 0)]

    def inside(ds, dr):
        ok = None
        for here, step, end in ((s, ds, N), (r, dr, Pn)):
            if step:
                near = here > 0 if step < 0 else here < end - 1
                ok = near if ok is None else jnp.logical_and(ok, near)
        return ok

    barrier = pltpu.get_barrier_semaphore()

    def greet(to_s, to_r):
        pl.semaphore_signal(barrier, inc=1, device_id=(to_s, to_r), device_id_type=MESH)

    for k in range(1, Pn):
        greet(s, chan_peer(k))
    for k in range(1, M):
        greet(group_peer(k)[1], r)
    near = sorted({1, B - 1} - {0})
    for k in near:
        greet(block_peer(k), r)
    for ds, dr in around:
        pl.when(inside(ds, dr))(functools.partial(greet, s + ds, r + dr))
    wide_s = 1 + jnp.where(s > 0, 1, 0) + jnp.where(s < N - 1, 1, 0)
    wide_r = 1 + jnp.where(r > 0, 1, 0) + jnp.where(r < Pn - 1, 1, 0)

    V, Wt = R + 2, R
    loads = [
        pltpu.make_async_copy(vol, RAW.at[0], l_s.at[0]),
        pltpu.make_async_copy(up, RAW.at[1], l_s.at[1]),
        pltpu.make_async_copy(wl, RAWW, l_s.at[2]),
    ]
    for c in loads:
        c.start()
    tile = (SHARE, LANES)
    edge = g.KW % LANES
    for c in loads:
        c.wait()
    sub = lax.broadcasted_iota(jnp.int32, (SHARE, g.KP - g.KW), 0)
    col = lax.broadcasted_iota(jnp.int32, (SHARE, g.KP - g.KW), 1)
    b0 = jnp.zeros((SHARE, g.KP - g.KW), f32)
    for q in range(SHARE):
        b0 = jnp.where(sub == q, bias[q], b0)
    hi = b0.astype(bf16).astype(f32)
    mid = (b0 - hi).astype(bf16).astype(f32)
    low = (b0 - hi - mid).astype(bf16).astype(f32)
    tail = jnp.where(col == 0, hi, jnp.where(col == 1, mid, jnp.where(col == 2, low, 0.0)))
    for b in range(3):
        taps = [RAWW[(a * 3 + b) * 3 + c_].astype(f32) for a in range(3) for c_ in range(3)]
        whole = jnp.concatenate(taps + [tail], axis=1)
        for j in range(g.NJ):
            part = whole[:, j * LANES : (j + 1) * LANES].astype(bf16)
            for to in range(Pn):
                SENDW[to, Wt + b * g.NJ + j] = part
    for n in range(2):
        TALL[n] = RAW[n].astype(f32).reshape(SHARE * g.H, LANES)
    zero_tile = jnp.zeros(tile, bf16)
    SENDV[0, 0] = zero_tile
    SENDV[Pn - 1, R + 1] = zero_tile
    for h in range(g.H):
        row = TALL[0, pl.ds(h, SHARE, stride=g.H), :].astype(bf16)
        for to in range(Pn):
            if 0 <= h + 1 - R * to < V:
                SENDV[to, h + 1 - R * to] = row
        SENDW[h // R, h % R] = TALL[1, pl.ds(h, SHARE, stride=g.H), :].astype(bf16)

    pl.semaphore_wait(barrier, (Pn - 1) + (M - 1) + len(near) + wide_s * wide_r - 1)

    reach = [1 << i for i in range(8) if 1 << i < B // 2]

    def relay(i):
        if i < len(reach):
            for k in sorted({reach[i], B - reach[i]}):
                pl.semaphore_signal(
                    far.at[i], inc=1, device_id=(block_peer(k), r), device_id_type=MESH
                )

    def heard(i):
        if i < len(reach):
            pl.semaphore_wait(far.at[i], len({reach[i], B - reach[i]}))

    relay(0)

    vsend, wsend = [], []
    for k in range(1, Pn):
        to = chan_peer(k)
        c = copy(SENDV.at[to], RCVV.at[r], v_s.at[k], v_r.at[k], s, to)
        start(c)
        vsend.append(c)
    for k in range(1, Pn):
        to = chan_peer(k)
        c = copy(SENDW.at[to], RCVW.at[r], w_s.at[k], w_r.at[k], s, to)
        start(c)
        wsend.append(c)
    RCVV[r] = SENDV[r]
    RCVW[r] = SENDW[r]

    def clear(ref, a):
        def body(i, _):
            ref[a, i] = jnp.zeros(ref.shape[2:], bf16)
            return 0
        lax.fori_loop(0, R + 2, body, 0)

    def clear_rows(ref, a):
        def body(i, _):
            ref[a, i] = jnp.zeros(ref.shape[2:], bf16)
            return 0
        lax.fori_loop(0, Pn, body, 0)

    @pl.when(s == 0)
    def _():
        clear_rows(HV, 0)
        clear(DX, 0)

    @pl.when(s == N - 1)
    def _():
        clear_rows(HV, 1)
        clear(DX, 2)

    @pl.when(r == 0)
    def _():
        for a in range(3):
            DX[a, 0] = jnp.zeros((C, LANES), bf16)

    @pl.when(r == Pn - 1)
    def _():
        for a in range(3):
            DX[a, R + 1] = jnp.zeros((C, LANES), bf16)

    for c in vsend:
        c.wait_recv()

    down = copy(RCVV, HV.at[1], p_s.at[0], p_r.at[0], s - 1, r)
    upw = copy(RCVV, HV.at[0], p_s.at[1], p_r.at[1], s + 1, r)
    pl.when(s > 0)(down.start)
    pl.when(s < N - 1)(upw.start)
    pending.append((s > 0, down))
    pending.append((s < N - 1, upw))

    heard(0)
    relay(1)
    last = pl.ds((g.NJ - 1) * LANES, LANES)
    lane = lax.broadcasted_iota(jnp.int32, (C, LANES), 1)

    def spread(row, out, a):
        def body(i, _):
            x = row(i).astype(f32).reshape(C, LANES)
            at = pl.ds(pl.multiple_of(i * LANES, LANES), LANES)
            before = jnp.where(lane == 0, 0.0, pltpu.roll(x, 1, 1))
            after = jnp.where(lane == LANES - 1, 0.0, pltpu.roll(x, LANES - 1, 1))
            out[pl.ds((3 * a) * C, C), at] = before.astype(bf16)
            out[pl.ds((3 * a + 1) * C, C), at] = x.astype(bf16)
            out[pl.ds((3 * a + 2) * C, C), at] = after.astype(bf16)
            return 0
        lax.fori_loop(0, R + 2, body, 0)

    spread(lambda i: RCVV[:, i], XL, 1)

    for c in wsend:
        c.wait_recv()
    for b in range(3):
        whole = jnp.concatenate(
            [RCVW[:, Wt + b * g.NJ + j].astype(f32).reshape(C, LANES) for j in range(g.NJ)], axis=1
        )
        W1[b] = whole[:, : g.KW].astype(bf16)
        if b == 0:
            end = whole[:, g.KP - LANES :]
            own = jnp.logical_and(lane >= edge, lane < edge + 3)
            bcol = jnp.sum(jnp.where(own, end, 0.0), axis=1, keepdims=True)

    pl.when(s < N - 1)(down.wait_recv)
    pl.when(s > 0)(upw.wait_recv)
    spread(lambda i: HV[0, :, i], XL, 0)
    spread(lambda i: HV[1, :, i], XL, 2)

    def conv(w, x):
        acc = None
        for b in range(3):
            part = jnp.dot(w[b], x[:, pl.ds(b * LANES, R * LANES)], preferred_element_type=f32)
            acc = part if acc is None else acc + part
        return acc

    PRE[...] = conv(W1, XL)

    dsum = jnp.zeros((C, LANES), f32)
    for j in range(R):
        p = PRE[:, pl.ds(j * LANES, LANES)] + bcol
        e = jnp.exp(-jnp.abs(p))
        soft = jnp.maximum(p, 0.0) + jnp.log(1.0 + e)
        gate = jnp.where(p >= 0.0, 1.0, e) / (1.0 + e)
        act = leakage * p + (1.0 - leakage) * soft
        AIS[:, 0, j] = act.reshape(Pn, SHARE, LANES).astype(bf16)
        u = RCVW[:, j].astype(f32).reshape(C, LANES)
        d = (u * (leakage + (1.0 - leakage) * gate)).astype(bf16)
        DX[1, 1 + j] = d
        DB[:, pl.ds(j * LANES, LANES)] = d
        dsum = dsum + d.astype(f32)

    dcol = jnp.sum(dsum, axis=1, keepdims=True)
    for b in range(3):
        GT[b, :, pl.ds(0, g.KW)] = lax.dot_general(
            DB[...], XL[:, pl.ds(b * LANES, R * LANES)],
            (((1,), (1,)), ((), ())), preferred_element_type=f32,
        )
        cur = GT[b, :, last]
        cur = jnp.where(lane < edge, cur, 0.0)
        if b == 0:
            cur = jnp.where(lane == edge, dcol, cur)
        GT[b, :, last] = cur
        for to in range(Pn):
            GS[to, b] = GT[b, pl.ds(SHARE * to, SHARE), :].astype(GS.dtype)
    gsend = []
    for k in range(1, Pn):
        to = chan_peer(k)
        c = copy(GS.at[to], GR.at[r], g_s.at[k], g_r.at[k], s, to)
        start(c)
        gsend.append(c)
    GR[r] = GS[r]

    dcopies = []
    for e, (ds, dr) in enumerate(around):
        if dr == 0:
            src, dst = DX.at[1, pl.ds(1, R)], DX.at[1 - ds, pl.ds(1, R)]
        elif dr < 0:
            src, dst = DX.at[1, 1], DX.at[1 - ds, R + 1]
        else:
            src, dst = DX.at[1, R], DX.at[1 - ds, 0]
        c = copy(src, dst, d_s.at[e], d_r.at[e], s + ds, r + dr)
        pl.when(inside(ds, dr))(c.start)
        pending.append((inside(ds, dr), c))
        dcopies.append((inside(-ds, -dr), c))

    for b in range(3):
        whole = W1[2 - b].astype(f32).T
        blocks = []
        for a in range(3):
            for c_ in range(3):
                at = ((2 - a) * 3 + (2 - c_)) * C
                blocks.append(whole[at : at + C])
        W2[b] = jnp.concatenate(blocks, axis=1).astype(bf16)

    for c in gsend:
        c.wait_recv()
    for b in range(3):
        acc = GR[0, b].astype(f32)
        for q in range(1, Pn):
            acc = acc + GR[q, b].astype(f32)
        for j in range(g.NJ):
            t = b * g.NJ + j
            SB[t // g.T, t % g.T] = acc[:, j * LANES : (j + 1) * LANES]
    for t in range(3 * g.NJ, M * g.T):
        SB[t // g.T, t % g.T] = jnp.zeros(tile, f32)
    q1send = []
    for k in range(1, M):
        m, to_s = group_peer(k)
        c = copy(SB.at[m], Q1.at[member], q1_s.at[k], q1_r.at[k], to_s, r)
        start(c)
        q1send.append(c)
    Q1[member] = SB[member]

    for ok, c in dcopies:
        pl.when(ok)(c.wait_recv)
    for a in range(3):
        spread(lambda i, a=a: DX[a, i], DL, a)
    PRE[...] = conv(W2, DL)
    for j in range(R):
        v = PRE[:, pl.ds(j * LANES, LANES)]
        AIS[:, 1, j] = v.reshape(Pn, SHARE, LANES).astype(bf16)
    isend = []
    for k in range(1, Pn):
        to = chan_peer(k)
        c = copy(AIS.at[to], AIR.at[r], i_s.at[k], i_r.at[k], s, to)
        start(c)
        isend.append(c)
    AIR[r] = AIS[r]

    for c in q1send:
        c.wait_recv()
    acc = Q1[0]
    for m in range(1, M):
        acc = acc + Q1[m]
    Q2[block] = acc
    heard(1)
    q2send = []
    for k in range(1, B):
        c = copy(Q2.at[block], Q2.at[block], q2_s.at[k], q2_r.at[k], block_peer(k), r)
        start(c)
        q2send.append(c)
    for c in isend:
        c.wait_recv()
    leave = []
    for n, out in enumerate((act_o, ig_o)):
        TALL[n] = AIR[:, n].astype(f32).reshape(g.H * SHARE, LANES)
        for q in range(SHARE):
            OUTS[n, q] = TALL[n, pl.ds(q, g.H, stride=SHARE), :].astype(bf16)
        leave.append(pltpu.make_async_copy(OUTS.at[n], out, o_s.at[n]))
        leave[n].start()
    for c in q2send:
        c.wait_recv()
    acc = Q2[0]
    for m in range(1, B):
        acc = acc + Q2[m]
    FIN[member] = acc * g.factor
    q3send = []
    for k in range(1, M):
        c = copy(FIN.at[member], FIN.at[member], q3_s.at[k], q3_r.at[k], group_peer(k)[1], r)
        start(c)
        q3send.append(c)
    for c in q3send:
        c.wait_recv()
    for a in range(3):
        for b in range(3):
            for c_ in range(3):
                at = (a * 3 + c_) * C
                t = b * g.NJ + at // LANES
                off = at % LANES
                OUTW[(a * 3 + b) * 3 + c_] = FIN[t // g.T, t % g.T][:, off : off + C]
    t = g.NJ - 1
    sums = FIN[t // g.T, t % g.T][:, edge : edge + 1]
    spot = lax.broadcasted_iota(jnp.int32, tile, 0) == lax.broadcasted_iota(jnp.int32, tile, 1)
    OUTB[...] = jnp.sum(jnp.where(spot, sums, 0.0), axis=0, keepdims=True)[:, :SHARE]
    for n, (a, b) in enumerate(((OUTW, wg_o), (OUTB, bg_o))):
        leave.append(pltpu.make_async_copy(a, b, o_s.at[2 + n]))
        leave[-1].start()

    for ok, c in pending:
        if ok is None:
            c.wait_send()
        else:
            pl.when(ok)(c.wait_send)
    for c in leave:
        c.wait()


def deliver(act, ig, wg, bg, act_o, ig_o, wg_o, bg_o, act_v, ig_v, wg_v, bg_v, i_s, o_s):
    held = (act_v, ig_v, wg_v, bg_v)
    ins = [pltpu.make_async_copy(a, v, i_s.at[n]) for n, (a, v) in enumerate(zip((act, ig, wg, bg), held))]
    outs = (act_o, ig_o, wg_o, bg_o)
    outs = [pltpu.make_async_copy(v, b, o_s.at[n]) for n, (v, b) in enumerate(zip(held, outs))]
    for c in ins:
        c.start()
    for c, d in zip(ins, outs):
        c.wait()
        d.start()
    for d in outs:
        d.wait()


def shards(g, volume, weight, bias, upstream):
    Pn, R, C, M, B = g.P, g.R, g.C, g.M, g.B
    vol, up = volume[:, 0], upstream[:, 0]
    wl = jnp.transpose(weight, (2, 3, 4, 0, 1)).reshape(27, SHARE, C)
    sds = jax.ShapeDtypeStruct
    hbm = pl.BlockSpec(memory_space=pltpu.HBM)
    rows = (R + 2) * LANES
    dma = pltpu.SemaphoreType.DMA
    V = pltpu.VMEM
    chan = [dma((Pn,)), dma((Pn,))]
    scratch = [
        V((2, SHARE, g.H, LANES), bf16),
        V((27, SHARE, C), bf16),
        V((2, SHARE * g.H, LANES), f32),
        V((Pn, R + 2, SHARE, LANES), bf16),
        V((Pn, R + 3 * g.NJ, SHARE, LANES), bf16),
        V((Pn, R + 2, SHARE, LANES), bf16),
        V((Pn, R + 3 * g.NJ, SHARE, LANES), bf16),
        V((2, Pn, R + 2, SHARE, LANES), bf16),
        V((9 * C, rows), bf16),
        V((3, R + 2, C, LANES), bf16),
        V((9 * C, rows), bf16),
        V((3, C, g.KW), bf16),
        V((3, C, g.KW), bf16),
        V((C, R * LANES), f32),
        V((C, R * LANES), bf16),
        V((Pn, 2, R, SHARE, LANES), bf16),
        V((Pn, 2, R, SHARE, LANES), bf16),
        V((3, C, g.KP), f32),
        V((Pn, 3, SHARE, g.KP), bf16),
        V((Pn, 3, SHARE, g.KP), bf16),
        V((M, g.T, SHARE, LANES), f32),
        V((M, g.T, SHARE, LANES), f32),
        V((B, g.T, SHARE, LANES), f32),
        V((M, g.T, SHARE, LANES), f32),
        V((2, SHARE, g.H, LANES), bf16),
        V((27, SHARE, C), f32),
        V((1, SHARE), f32),
        dma((3,)),
        dma((4,)),
        *chan, *chan,
        pltpu.SemaphoreType.REGULAR((2,)),
        dma((2,)), dma((2,)),
        dma((8,)), dma((8,)),
        *chan, *chan,
        dma((M,)), dma((M,)),
        dma((B,)), dma((B,)),
        dma((M,)), dma((M,)),
    ]
    act, ig, wg, bg = pl.pallas_call(
        functools.partial(kernel, g),
        out_shape=(
            sds((SHARE, g.H, LANES), bf16),
            sds((SHARE, g.H, LANES), bf16),
            sds((27, SHARE, C), f32),
            sds((1, SHARE), f32),
        ),
        in_specs=[hbm, hbm, hbm, pl.BlockSpec(memory_space=pltpu.SMEM)],
        out_specs=(hbm,) * 4,
        scratch_shapes=scratch,
        compiler_params=pltpu.CompilerParams(
            collective_id=0, has_side_effects=True, vmem_limit_bytes=62 << 20
        ),
    )(vol, up, wl, bias)
    act, ig, wg, bg = pl.pallas_call(
        deliver,
        out_shape=(
            sds((SHARE, g.H, LANES), bf16),
            sds((SHARE, g.H, LANES), bf16),
            sds((27, SHARE, C), f32),
            sds((1, SHARE), f32),
        ),
        in_specs=[hbm] * 4,
        out_specs=(hbm,) * 4,
        scratch_shapes=[
            V((SHARE, g.H, LANES), bf16),
            V((SHARE, g.H, LANES), bf16),
            V((27, SHARE, C), f32),
            V((1, SHARE), f32),
            dma((4,)),
            dma((4,)),
        ],
    )(act, ig, wg, bg)
    wgrad = jnp.transpose(wg.reshape(3, 3, 3, SHARE, C), (3, 4, 0, 1, 2))
    return act[:, None], ig[:, None], wgrad, bg[0]


def solution(mesh, rows=48, halves=2, blocks=8):
    planes, ranks = mesh.shape["space"], mesh.shape["chan"]
    factor = 1.0 / math.sqrt(planes * rows * LANES)
    g = Plan(planes, ranks, rows, halves, blocks, factor)
    field = P("chan", "space", None, None)
    filters = P("chan", None, None, None, None)
    return jax.shard_map(
        functools.partial(shards, g),
        mesh=mesh,
        in_specs=(field, filters, P("chan"), field),
        out_specs=(field, field, filters, P("chan")),
        check_vma=False,
    )
```

```python
import functools
import math

import jax
import jax.numpy as jnp
from jax import lax
from jax.experimental import pallas as pl
from jax.experimental.pallas import tpu as pltpu
from jax.sharding import PartitionSpec as P

MESH = pl.DeviceIdType.MESH
f32 = jnp.float32
bf16 = jnp.bfloat16
leakage = 0.1
LANES = 128
SHARE = 8


class Plan:
    def __init__(self, planes, ranks, rows, halves, blocks, factor):
        self.N = planes
        self.P = ranks
        self.R = rows // ranks
        self.H = rows
        self.C = SHARE * ranks
        self.X = halves
        self.B = blocks
        self.U = planes // (halves * blocks)
        self.M = self.U * self.X
        self.KW = 9 * self.C
        self.NJ = self.KW // LANES + 1
        self.KP = self.NJ * LANES
        self.T = -(-3 * self.NJ // self.M)
        self.factor = factor


def kernel(
    g, vol, up, wl, bias,
    act_o, ig_o, wg_o, bg_o,
    RAW, RAWW, RAWB, TALL, SENDV, SENDW, RCVV, RCVW, HV, XL, DX, DL, W1, WA, W2, PRE, DB, AIS, AIR,
    GT, GS, GR, SB, Q1, Q2, FIN, OUTS, OUTW, OUTB,
    l_s, o_s, v_s, v_r, w_s, w_r, far, p_s, p_r, d_s, d_r, i_s, i_r,
    g_s, g_r, q1_s, q1_r, q2_s, q2_r, q3_s, q3_r,
):
    N, Pn, R, C, M, B, U = g.N, g.P, g.R, g.C, g.M, g.B, g.U
    s = lax.axis_index("space")
    r = lax.axis_index("chan")
    span = B * U
    x_lo, within = s // span, s % span
    block, unit = within // U, within % U
    member = x_lo * U + unit
    pending = []

    def chan_peer(k):
        return lax.rem(r + k, Pn)

    def group_peer(k):
        m = lax.rem(member + k, M)
        return m, (m // U) * span + block * U + m % U

    def block_peer(k):
        b = lax.rem(block + k, B)
        return x_lo * span + b * U + unit

    def copy(src, dst, ssem, rsem, to_s, to_r):
        return pltpu.make_async_remote_copy(
            src_ref=src, dst_ref=dst, send_sem=ssem, recv_sem=rsem,
            device_id=(to_s, to_r), device_id_type=MESH,
        )

    def start(c):
        c.start()
        pending.append((None, c))

    around = [(ds, dr) for ds in (-1, 0, 1) for dr in (-1, 0, 1) if (ds, dr) != (0, 0)]

    def inside(ds, dr):
        ok = None
        for here, step, end in ((s, ds, N), (r, dr, Pn)):
            if step:
                near = here > 0 if step < 0 else here < end - 1
                ok = near if ok is None else jnp.logical_and(ok, near)
        return ok

    barrier = pltpu.get_barrier_semaphore()

    def greet(to_s, to_r):
        pl.semaphore_signal(barrier, inc=1, device_id=(to_s, to_r), device_id_type=MESH)

    for k in range(1, Pn):
        greet(s, chan_peer(k))
    for k in range(1, M):
        greet(group_peer(k)[1], r)
    near = sorted({1, B - 1} - {0})
    for k in near:
        greet(block_peer(k), r)
    for ds, dr in around:
        pl.when(inside(ds, dr))(functools.partial(greet, s + ds, r + dr))
    wide_s = 1 + jnp.where(s > 0, 1, 0) + jnp.where(s < N - 1, 1, 0)
    wide_r = 1 + jnp.where(r > 0, 1, 0) + jnp.where(r < Pn - 1, 1, 0)

    V, Wt = R + 2, R
    loads = [
        pltpu.make_async_copy(vol, RAW.at[0], l_s.at[0]),
        pltpu.make_async_copy(up, RAW.at[1], l_s.at[1]),
        pltpu.make_async_copy(wl, RAWW, l_s.at[2]),
        pltpu.make_async_copy(bias, RAWB, l_s.at[3]),
    ]
    for c in loads:
        c.start()
    tile = (SHARE, LANES)
    edge = g.KW % LANES
    for c in loads:
        c.wait()
    sub = lax.broadcasted_iota(jnp.int32, (SHARE, g.KP - g.KW), 0)
    col = lax.broadcasted_iota(jnp.int32, (SHARE, g.KP - g.KW), 1)
    b0 = jnp.zeros((SHARE, g.KP - g.KW), f32)
    for q in range(SHARE):
        b0 = jnp.where(sub == q, RAWB[0, q], b0)
    hi = b0.astype(bf16).astype(f32)
    mid = (b0 - hi).astype(bf16).astype(f32)
    low = (b0 - hi - mid).astype(bf16).astype(f32)
    tail = jnp.where(col == 0, hi, jnp.where(col == 1, mid, jnp.where(col == 2, low, 0.0)))
    for b in range(3):
        taps = [RAWW[(a * 3 + b) * 3 + c_].astype(f32) for a in range(3) for c_ in range(3)]
        whole = jnp.concatenate(taps + [tail], axis=1)
        for j in range(g.NJ):
            part = whole[:, j * LANES : (j + 1) * LANES].astype(bf16)
            for to in range(Pn):
                SENDW[to, Wt + b * g.NJ + j] = part
    for n in range(2):
        TALL[n] = RAW[n].astype(f32).reshape(SHARE * g.H, LANES)
    zero_tile = jnp.zeros(tile, bf16)
    SENDV[0, 0] = zero_tile
    SENDV[Pn - 1, R + 1] = zero_tile
    for h in range(g.H):
        row = TALL[0, pl.ds(h, SHARE, stride=g.H), :].astype(bf16)
        for to in range(Pn):
            if 0 <= h + 1 - R * to < V:
                SENDV[to, h + 1 - R * to] = row
        SENDW[h // R, h % R] = TALL[1, pl.ds(h, SHARE, stride=g.H), :].astype(bf16)

    pl.semaphore_wait(barrier, (Pn - 1) + (M - 1) + len(near) + wide_s * wide_r - 1)

    reach = [1 << i for i in range(8) if 1 << i < B // 2]

    def relay(i):
        if i < len(reach):
            for k in sorted({reach[i], B - reach[i]}):
                pl.semaphore_signal(
                    far.at[i], inc=1, device_id=(block_peer(k), r), device_id_type=MESH
                )

    def heard(i):
        if i < len(reach):
            pl.semaphore_wait(far.at[i], len({reach[i], B - reach[i]}))

    relay(0)

    RCVV[r] = SENDV[r]

    def nearness(k):
        return k % 2, min(k, Pn - k)

    vsend, wsend = [], []
    for k in sorted(range(1, Pn), key=nearness, reverse=True):
        to = chan_peer(k)
        c = copy(SENDV.at[to], RCVV.at[r], v_s.at[k], v_r.at[k], s, to)
        start(c)
        vsend.append((k, c))
    for k in range(1, Pn):
        to = chan_peer(k)
        c = copy(SENDW.at[to], RCVW.at[r], w_s.at[k], w_r.at[k], s, to)
        start(c)
        wsend.append(c)
    RCVW[r] = SENDW[r]

    def clear(ref, a):
        def body(i, _):
            ref[a, i] = jnp.zeros(ref.shape[2:], bf16)
            return 0
        lax.fori_loop(0, R + 2, body, 0)

    def clear_rows(ref, a):
        def body(i, _):
            ref[a, i] = jnp.zeros(ref.shape[2:], bf16)
            return 0
        lax.fori_loop(0, Pn, body, 0)

    @pl.when(s == 0)
    def _():
        clear_rows(HV, 0)
        clear(DX, 0)

    @pl.when(s == N - 1)
    def _():
        clear_rows(HV, 1)
        clear(DX, 2)

    @pl.when(r == 0)
    def _():
        for a in range(3):
            DX[a, 0] = jnp.zeros((C, LANES), bf16)

    @pl.when(r == Pn - 1)
    def _():
        for a in range(3):
            DX[a, R + 1] = jnp.zeros((C, LANES), bf16)

    halo = [[], []]

    def forward(k):
        q = lax.rem(r + Pn - k, Pn)
        for n, (ok, to) in enumerate(((s > 0, s - 1), (s < N - 1, s + 1))):
            c = copy(RCVV.at[q], HV.at[1 - n, q], p_s.at[n, k], p_r.at[n, k], to, r)
            pl.when(ok)(c.start)
            pending.append((ok, c))
            halo[n].append(c)

    forward(0)
    for k, c in sorted(vsend, key=lambda kc: nearness(kc[0])):
        c.wait_recv()
        forward(k)

    heard(0)
    relay(1)
    last = pl.ds((g.NJ - 1) * LANES, LANES)
    lane = lax.broadcasted_iota(jnp.int32, (C, LANES), 1)

    def spread(row, out, a):
        def body(i, _):
            x = row(i).astype(f32).reshape(C, LANES)
            at = pl.ds(pl.multiple_of(i * LANES, LANES), LANES)
            before = jnp.where(lane == 0, 0.0, pltpu.roll(x, 1, 1))
            after = jnp.where(lane == LANES - 1, 0.0, pltpu.roll(x, LANES - 1, 1))
            out[pl.ds((3 * a) * C, C), at] = before.astype(bf16)
            out[pl.ds((3 * a + 1) * C, C), at] = x.astype(bf16)
            out[pl.ds((3 * a + 2) * C, C), at] = after.astype(bf16)
            return 0
        lax.fori_loop(0, R + 2, body, 0)

    spread(lambda i: RCVV[:, i], XL, 1)

    for c in wsend:
        c.wait_recv()
    for b in range(3):
        whole = jnp.concatenate(
            [RCVW[:, Wt + b * g.NJ + j].astype(f32).reshape(C, LANES) for j in range(g.NJ)], axis=1
        )
        W1[b] = whole[:, : g.KW].astype(bf16)
        for a in range(3):
            WA[a, b] = whole[:, a * 3 * C : (a + 1) * 3 * C].astype(bf16)
        if b == 0:
            end = whole[:, g.KP - LANES :]
            own = jnp.logical_and(lane >= edge, lane < edge + 3)
            bcol = jnp.sum(jnp.where(own, end, 0.0), axis=1, keepdims=True)

    def conv(w, x):
        acc = None
        for b in range(3):
            part = jnp.dot(w[b], x[:, pl.ds(b * LANES, R * LANES)], preferred_element_type=f32)
            acc = part if acc is None else acc + part
        return acc

    def third(a):
        acc = None
        for b in range(3):
            x = XL[pl.ds(a * 3 * C, 3 * C), pl.ds(b * LANES, R * LANES)]
            part = jnp.dot(WA[a, b], x, preferred_element_type=f32)
            acc = part if acc is None else acc + part
        return acc

    PRE[...] = third(1)
    for n, ok in enumerate((s < N - 1, s > 0)):
        @pl.when(ok)
        def _(n=n):
            for c in halo[n]:
                c.wait_recv()

    spread(lambda i: HV[0, :, i], XL, 0)
    spread(lambda i: HV[1, :, i], XL, 2)

    PRE[...] = PRE[...] + third(0) + third(2)

    dsum = jnp.zeros((C, LANES), f32)
    for j in range(R):
        p = PRE[:, pl.ds(j * LANES, LANES)] + bcol
        e = jnp.exp(-jnp.abs(p))
        soft = jnp.maximum(p, 0.0) + jnp.log(1.0 + e)
        gate = jnp.where(p >= 0.0, 1.0, e) / (1.0 + e)
        act = leakage * p + (1.0 - leakage) * soft
        AIS[:, 0, j] = act.reshape(Pn, SHARE, LANES).astype(bf16)
        u = RCVW[:, j].astype(f32).reshape(C, LANES)
        d = (u * (leakage + (1.0 - leakage) * gate)).astype(bf16)
        DX[1, 1 + j] = d
        DB[:, pl.ds(j * LANES, LANES)] = d
        dsum = dsum + d.astype(f32)

    dcol = jnp.sum(dsum, axis=1, keepdims=True)
    for b in range(3):
        GT[b, :, pl.ds(0, g.KW)] = lax.dot_general(
            DB[...], XL[:, pl.ds(b * LANES, R * LANES)],
            (((1,), (1,)), ((), ())), preferred_element_type=f32,
        )
        cur = GT[b, :, last]
        cur = jnp.where(lane < edge, cur, 0.0)
        if b == 0:
            cur = jnp.where(lane == edge, dcol, cur)
        GT[b, :, last] = cur
        for to in range(Pn):
            GS[to, b] = GT[b, pl.ds(SHARE * to, SHARE), :].astype(GS.dtype)
    gsend = []
    for k in range(1, Pn):
        to = chan_peer(k)
        c = copy(GS.at[to], GR.at[r], g_s.at[k], g_r.at[k], s, to)
        start(c)
        gsend.append(c)
    GR[r] = GS[r]

    dcopies = []
    for e, (ds, dr) in enumerate(around):
        if dr == 0:
            src, dst = DX.at[1, pl.ds(1, R)], DX.at[1 - ds, pl.ds(1, R)]
        elif dr < 0:
            src, dst = DX.at[1, 1], DX.at[1 - ds, R + 1]
        else:
            src, dst = DX.at[1, R], DX.at[1 - ds, 0]
        c = copy(src, dst, d_s.at[e], d_r.at[e], s + ds, r + dr)
        pl.when(inside(ds, dr))(c.start)
        pending.append((inside(ds, dr), c))
        dcopies.append((inside(-ds, -dr), c))

    for b in range(3):
        whole = W1[2 - b].astype(f32).T
        blocks = []
        for a in range(3):
            for c_ in range(3):
                at = ((2 - a) * 3 + (2 - c_)) * C
                blocks.append(whole[at : at + C])
        W2[b] = jnp.concatenate(blocks, axis=1).astype(bf16)

    for c in gsend:
        c.wait_recv()
    for b in range(3):
        acc = GR[0, b].astype(f32)
        for q in range(1, Pn):
            acc = acc + GR[q, b].astype(f32)
        for j in range(g.NJ):
            t = b * g.NJ + j
            SB[t // g.T, t % g.T] = acc[:, j * LANES : (j + 1) * LANES]
    for t in range(3 * g.NJ, M * g.T):
        SB[t // g.T, t % g.T] = jnp.zeros(tile, f32)
    q1send = []
    for k in range(1, M):
        m, to_s = group_peer(k)
        c = copy(SB.at[m], Q1.at[member], q1_s.at[k], q1_r.at[k], to_s, r)
        start(c)
        q1send.append(c)
    Q1[member] = SB[member]

    for ok, c in dcopies:
        pl.when(ok)(c.wait_recv)
    for a in range(3):
        spread(lambda i, a=a: DX[a, i], DL, a)
    PRE[...] = conv(W2, DL)
    for j in range(R):
        v = PRE[:, pl.ds(j * LANES, LANES)]
        AIS[:, 1, j] = v.reshape(Pn, SHARE, LANES).astype(bf16)
    isend = []
    for k in range(1, Pn):
        to = chan_peer(k)
        c = copy(AIS.at[to], AIR.at[r], i_s.at[k], i_r.at[k], s, to)
        start(c)
        isend.append(c)
    AIR[r] = AIS[r]

    for c in q1send:
        c.wait_recv()
    acc = Q1[0]
    for m in range(1, M):
        acc = acc + Q1[m]
    Q2[block] = acc
    heard(1)
    q2send = []
    for k in range(1, B):
        c = copy(Q2.at[block], Q2.at[block], q2_s.at[k], q2_r.at[k], block_peer(k), r)
        start(c)
        q2send.append(c)
    for c in isend:
        c.wait_recv()
    leave = []
    for n, out in enumerate((act_o, ig_o)):
        TALL[n] = AIR[:, n].astype(f32).reshape(g.H * SHARE, LANES)
        for q in range(SHARE):
            OUTS[n, q] = TALL[n, pl.ds(q, g.H, stride=SHARE), :].astype(bf16)
        leave.append(pltpu.make_async_copy(OUTS.at[n], out, o_s.at[n]))
        leave[n].start()
    for c in q2send:
        c.wait_recv()
    acc = Q2[0]
    for m in range(1, B):
        acc = acc + Q2[m]
    FIN[member] = acc * g.factor
    q3send = []
    for k in range(1, M):
        c = copy(FIN.at[member], FIN.at[member], q3_s.at[k], q3_r.at[k], group_peer(k)[1], r)
        start(c)
        q3send.append(c)
    for c in q3send:
        c.wait_recv()
    for a in range(3):
        for b in range(3):
            for c_ in range(3):
                at = (a * 3 + c_) * C
                t = b * g.NJ + at // LANES
                off = at % LANES
                OUTW[(a * 3 + b) * 3 + c_] = FIN[t // g.T, t % g.T][:, off : off + C]
    t = g.NJ - 1
    sums = FIN[t // g.T, t % g.T][:, edge : edge + 1]
    spot = lax.broadcasted_iota(jnp.int32, tile, 0) == lax.broadcasted_iota(jnp.int32, tile, 1)
    OUTB[...] = jnp.sum(jnp.where(spot, sums, 0.0), axis=0, keepdims=True)[:, :SHARE]
    for n, (a, b) in enumerate(((OUTW, wg_o), (OUTB, bg_o))):
        leave.append(pltpu.make_async_copy(a, b, o_s.at[2 + n]))
        leave[-1].start()

    for ok, c in pending:
        if ok is None:
            c.wait_send()
        else:
            pl.when(ok)(c.wait_send)
    for c in leave:
        c.wait()


def deliver(act, ig, wg, bg, act_o, ig_o, wg_o, bg_o, act_v, ig_v, wg_v, bg_v, i_s, o_s):
    held = (act_v, ig_v, wg_v, bg_v)
    ins = [pltpu.make_async_copy(a, v, i_s.at[n]) for n, (a, v) in enumerate(zip((act, ig, wg, bg), held))]
    outs = (act_o, ig_o, wg_o, bg_o)
    outs = [pltpu.make_async_copy(v, b, o_s.at[n]) for n, (v, b) in enumerate(zip(held, outs))]
    for c in ins:
        c.start()
    for c, d in zip(ins, outs):
        c.wait()
        d.start()
    for d in outs:
        d.wait()


def shards(g, volume, weight, bias, upstream):
    Pn, R, C, M, B = g.P, g.R, g.C, g.M, g.B
    vol, up = volume[:, 0], upstream[:, 0]
    wl = jnp.transpose(weight, (2, 3, 4, 0, 1)).reshape(27, SHARE, C)
    sds = jax.ShapeDtypeStruct
    hbm = pl.BlockSpec(memory_space=pltpu.HBM)
    rows = (R + 2) * LANES
    dma = pltpu.SemaphoreType.DMA
    V = pltpu.VMEM
    chan = [dma((Pn,)), dma((Pn,))]
    scratch = [
        V((2, SHARE, g.H, LANES), bf16),
        V((27, SHARE, C), bf16),
        pltpu.SMEM((1, SHARE), f32),
        V((2, SHARE * g.H, LANES), f32),
        V((Pn, R + 2, SHARE, LANES), bf16),
        V((Pn, R + 3 * g.NJ, SHARE, LANES), bf16),
        V((Pn, R + 2, SHARE, LANES), bf16),
        V((Pn, R + 3 * g.NJ, SHARE, LANES), bf16),
        V((2, Pn, R + 2, SHARE, LANES), bf16),
        V((9 * C, rows), bf16),
        V((3, R + 2, C, LANES), bf16),
        V((9 * C, rows), bf16),
        V((3, C, g.KW), bf16),
        V((3, 3, C, 3 * C), bf16),
        V((3, C, g.KW), bf16),
        V((C, R * LANES), f32),
        V((C, R * LANES), bf16),
        V((Pn, 2, R, SHARE, LANES), bf16),
        V((Pn, 2, R, SHARE, LANES), bf16),
        V((3, C, g.KP), f32),
        V((Pn, 3, SHARE, g.KP), bf16),
        V((Pn, 3, SHARE, g.KP), bf16),
        V((M, g.T, SHARE, LANES), f32),
        V((M, g.T, SHARE, LANES), f32),
        V((B, g.T, SHARE, LANES), f32),
        V((M, g.T, SHARE, LANES), f32),
        V((2, SHARE, g.H, LANES), bf16),
        V((27, SHARE, C), f32),
        V((1, SHARE), f32),
        dma((4,)),
        dma((4,)),
        *chan, *chan,
        pltpu.SemaphoreType.REGULAR((2,)),
        dma((2, Pn)), dma((2, Pn)),
        dma((8,)), dma((8,)),
        *chan, *chan,
        dma((M,)), dma((M,)),
        dma((B,)), dma((B,)),
        dma((M,)), dma((M,)),
    ]
    act, ig, wg, bg = pl.pallas_call(
        functools.partial(kernel, g),
        out_shape=(
            sds((SHARE, g.H, LANES), bf16),
            sds((SHARE, g.H, LANES), bf16),
            sds((27, SHARE, C), f32),
            sds((1, SHARE), f32),
        ),
        in_specs=[hbm] * 4,
        out_specs=(hbm,) * 4,
        scratch_shapes=scratch,
        compiler_params=pltpu.CompilerParams(
            collective_id=0, has_side_effects=True, vmem_limit_bytes=62 << 20
        ),
    )(vol, up, wl, bias[None])
    act, ig, wg, bg = pl.pallas_call(
        deliver,
        out_shape=(
            sds((SHARE, g.H, LANES), bf16),
            sds((SHARE, g.H, LANES), bf16),
            sds((27, SHARE, C), f32),
            sds((1, SHARE), f32),
        ),
        in_specs=[hbm] * 4,
        out_specs=(hbm,) * 4,
        scratch_shapes=[
            V((SHARE, g.H, LANES), bf16),
            V((SHARE, g.H, LANES), bf16),
            V((27, SHARE, C), f32),
            V((1, SHARE), f32),
            dma((4,)),
            dma((4,)),
        ],
    )(act, ig, wg, bg)
    wgrad = jnp.transpose(wg.reshape(3, 3, 3, SHARE, C), (3, 4, 0, 1, 2))
    return act[:, None], ig[:, None], wgrad, bg[0]


def solution(mesh, rows=48, halves=2, blocks=8):
    planes, ranks = mesh.shape["space"], mesh.shape["chan"]
    factor = 1.0 / math.sqrt(planes * rows * LANES)
    g = Plan(planes, ranks, rows, halves, blocks, factor)
    field = P("chan", "space", None, None)
    filters = P("chan", None, None, None, None)
    return jax.shard_map(
        functools.partial(shards, g),
        mesh=mesh,
        in_specs=(field, filters, P("chan"), field),
        out_specs=(field, field, filters, P("chan")),
        check_vma=False,
    )
```

```python
import functools
import math

import jax
import jax.numpy as jnp
from jax import lax
from jax.experimental import pallas as pl
from jax.experimental.pallas import tpu as pltpu
from jax.sharding import PartitionSpec as P

MESH = pl.DeviceIdType.MESH
f32 = jnp.float32
bf16 = jnp.bfloat16
leakage = 0.1
LANES = 128
SHARE = 8


class Plan:
    def __init__(self, planes, ranks, rows, halves, blocks, factor):
        self.N = planes
        self.P = ranks
        self.R = rows // ranks
        self.H = rows
        self.C = SHARE * ranks
        self.X = halves
        self.B = blocks
        self.U = planes // (halves * blocks)
        self.M = self.U * self.X
        self.KW = 9 * self.C
        self.NJ = self.KW // LANES + 1
        self.KP = self.NJ * LANES
        self.T = -(-3 * self.NJ // self.M)
        self.factor = factor


def kernel(
    g, vol, up, wl, bias,
    act_o, ig_o, wg_o, bg_o,
    RAW, RAWW, RAWB, TALL, SENDV, SENDW, RCVV, RCVW, HV, XL, DX, DL, W1, WA, W2, PRE, DB, AIS, AIR,
    GT, GS, GR, SB, Q1, Q2, FIN,
    l_s, v_s, v_r, w_s, w_r, far, p_s, p_r, d_s, d_r, i_s, i_r,
    g_s, g_r, q1_s, q1_r, q2_s, q2_r, q3_s, q3_r,
):
    N, Pn, R, C, M, B, U = g.N, g.P, g.R, g.C, g.M, g.B, g.U
    s = lax.axis_index("space")
    r = lax.axis_index("chan")
    span = B * U
    x_lo, within = s // span, s % span
    block, unit = within // U, within % U
    member = x_lo * U + unit
    pending = []

    def chan_peer(k):
        return lax.rem(r + k, Pn)

    def group_peer(k):
        m = lax.rem(member + k, M)
        return m, (m // U) * span + block * U + m % U

    def block_peer(k):
        b = lax.rem(block + k, B)
        return x_lo * span + b * U + unit

    def copy(src, dst, ssem, rsem, to_s, to_r):
        return pltpu.make_async_remote_copy(
            src_ref=src, dst_ref=dst, send_sem=ssem, recv_sem=rsem,
            device_id=(to_s, to_r), device_id_type=MESH,
        )

    def start(c):
        c.start()
        pending.append((None, c))

    around = [(ds, dr) for ds in (-1, 0, 1) for dr in (-1, 0, 1) if (ds, dr) != (0, 0)]

    def inside(ds, dr):
        ok = None
        for here, step, end in ((s, ds, N), (r, dr, Pn)):
            if step:
                near = here > 0 if step < 0 else here < end - 1
                ok = near if ok is None else jnp.logical_and(ok, near)
        return ok

    barrier = pltpu.get_barrier_semaphore()

    def greet(to_s, to_r):
        pl.semaphore_signal(barrier, inc=1, device_id=(to_s, to_r), device_id_type=MESH)

    for k in range(1, Pn):
        greet(s, chan_peer(k))
    for k in range(1, M):
        greet(group_peer(k)[1], r)
    near = sorted({1, B - 1} - {0})
    for k in near:
        greet(block_peer(k), r)
    for ds, dr in around:
        pl.when(inside(ds, dr))(functools.partial(greet, s + ds, r + dr))
    wide_s = 1 + jnp.where(s > 0, 1, 0) + jnp.where(s < N - 1, 1, 0)
    wide_r = 1 + jnp.where(r > 0, 1, 0) + jnp.where(r < Pn - 1, 1, 0)

    V, Wt = R + 2, R
    loads = [
        pltpu.make_async_copy(vol, RAW.at[0], l_s.at[0]),
        pltpu.make_async_copy(up, RAW.at[1], l_s.at[1]),
        pltpu.make_async_copy(wl, RAWW, l_s.at[2]),
        pltpu.make_async_copy(bias, RAWB, l_s.at[3]),
    ]
    for c in loads:
        c.start()
    tile = (SHARE, LANES)
    edge = g.KW % LANES
    for c in loads:
        c.wait()
    sub = lax.broadcasted_iota(jnp.int32, (SHARE, g.KP - g.KW), 0)
    col = lax.broadcasted_iota(jnp.int32, (SHARE, g.KP - g.KW), 1)
    b0 = jnp.zeros((SHARE, g.KP - g.KW), f32)
    for q in range(SHARE):
        b0 = jnp.where(sub == q, RAWB[0, q], b0)
    hi = b0.astype(bf16).astype(f32)
    mid = (b0 - hi).astype(bf16).astype(f32)
    low = (b0 - hi - mid).astype(bf16).astype(f32)
    tail = jnp.where(col == 0, hi, jnp.where(col == 1, mid, jnp.where(col == 2, low, 0.0)))
    for b in range(3):
        taps = [RAWW[(a * 3 + b) * 3 + c_].astype(f32) for a in range(3) for c_ in range(3)]
        whole = jnp.concatenate(taps + [tail], axis=1)
        for j in range(g.NJ):
            part = whole[:, j * LANES : (j + 1) * LANES].astype(bf16)
            for to in range(Pn):
                SENDW[to, Wt + b * g.NJ + j] = part
    for n in range(2):
        TALL[n] = RAW[n].astype(f32).reshape(SHARE * g.H, LANES)
    zero_tile = jnp.zeros(tile, bf16)
    SENDV[0, 0] = zero_tile
    SENDV[Pn - 1, R + 1] = zero_tile
    for h in range(g.H):
        row = TALL[0, pl.ds(h, SHARE, stride=g.H), :].astype(bf16)
        for to in range(Pn):
            if 0 <= h + 1 - R * to < V:
                SENDV[to, h + 1 - R * to] = row
        SENDW[h // R, h % R] = TALL[1, pl.ds(h, SHARE, stride=g.H), :].astype(bf16)

    pl.semaphore_wait(barrier, (Pn - 1) + (M - 1) + len(near) + wide_s * wide_r - 1)

    reach = [1 << i for i in range(8) if 1 << i < B // 2]

    def relay(i):
        if i < len(reach):
            for k in sorted({reach[i], B - reach[i]}):
                pl.semaphore_signal(
                    far.at[i], inc=1, device_id=(block_peer(k), r), device_id_type=MESH
                )

    def heard(i):
        if i < len(reach):
            pl.semaphore_wait(far.at[i], len({reach[i], B - reach[i]}))

    relay(0)

    RCVV[r] = SENDV[r]

    def nearness(k):
        return k % 2, min(k, Pn - k)

    vsend, wsend = [], []
    for k in sorted(range(1, Pn), key=nearness, reverse=True):
        to = chan_peer(k)
        c = copy(SENDV.at[to], RCVV.at[r], v_s.at[k], v_r.at[k], s, to)
        start(c)
        vsend.append((k, c))
    for k in range(1, Pn):
        to = chan_peer(k)
        c = copy(SENDW.at[to], RCVW.at[r], w_s.at[k], w_r.at[k], s, to)
        start(c)
        wsend.append(c)
    RCVW[r] = SENDW[r]

    def clear(ref, a):
        def body(i, _):
            ref[a, i] = jnp.zeros(ref.shape[2:], bf16)
            return 0
        lax.fori_loop(0, R + 2, body, 0)

    def clear_rows(ref, a):
        def body(i, _):
            ref[a, i] = jnp.zeros(ref.shape[2:], bf16)
            return 0
        lax.fori_loop(0, Pn, body, 0)

    @pl.when(s == 0)
    def _():
        clear_rows(HV, 0)
        clear(DX, 0)

    @pl.when(s == N - 1)
    def _():
        clear_rows(HV, 1)
        clear(DX, 2)

    @pl.when(r == 0)
    def _():
        for a in range(3):
            DX[a, 0] = jnp.zeros((C, LANES), bf16)

    @pl.when(r == Pn - 1)
    def _():
        for a in range(3):
            DX[a, R + 1] = jnp.zeros((C, LANES), bf16)

    halo = [[], []]

    def forward(k):
        q = lax.rem(r + Pn - k, Pn)
        for n, (ok, to) in enumerate(((s > 0, s - 1), (s < N - 1, s + 1))):
            c = copy(RCVV.at[q], HV.at[1 - n, q], p_s.at[n, k], p_r.at[n, k], to, r)
            pl.when(ok)(c.start)
            pending.append((ok, c))
            halo[n].append(c)

    forward(0)
    for k, c in sorted(vsend, key=lambda kc: nearness(kc[0])):
        c.wait_recv()
        forward(k)

    heard(0)
    relay(1)
    last = pl.ds((g.NJ - 1) * LANES, LANES)
    lane = lax.broadcasted_iota(jnp.int32, (C, LANES), 1)

    def spread(row, out, a):
        def body(i, _):
            x = row(i).astype(f32).reshape(C, LANES)
            at = pl.ds(pl.multiple_of(i * LANES, LANES), LANES)
            before = jnp.where(lane == 0, 0.0, pltpu.roll(x, 1, 1))
            after = jnp.where(lane == LANES - 1, 0.0, pltpu.roll(x, LANES - 1, 1))
            out[pl.ds((3 * a) * C, C), at] = before.astype(bf16)
            out[pl.ds((3 * a + 1) * C, C), at] = x.astype(bf16)
            out[pl.ds((3 * a + 2) * C, C), at] = after.astype(bf16)
            return 0
        lax.fori_loop(0, R + 2, body, 0)

    spread(lambda i: RCVV[:, i], XL, 1)

    for c in wsend:
        c.wait_recv()
    for b in range(3):
        whole = jnp.concatenate(
            [RCVW[:, Wt + b * g.NJ + j].astype(f32).reshape(C, LANES) for j in range(g.NJ)], axis=1
        )
        W1[b] = whole[:, : g.KW].astype(bf16)
        for a in range(3):
            WA[a, b] = whole[:, a * 3 * C : (a + 1) * 3 * C].astype(bf16)
        if b == 0:
            end = whole[:, g.KP - LANES :]
            own = jnp.logical_and(lane >= edge, lane < edge + 3)
            bcol = jnp.sum(jnp.where(own, end, 0.0), axis=1, keepdims=True)

    def conv(w, x):
        acc = None
        for b in range(3):
            part = jnp.dot(w[b], x[:, pl.ds(b * LANES, R * LANES)], preferred_element_type=f32)
            acc = part if acc is None else acc + part
        return acc

    def third(a):
        acc = None
        for b in range(3):
            x = XL[pl.ds(a * 3 * C, 3 * C), pl.ds(b * LANES, R * LANES)]
            part = jnp.dot(WA[a, b], x, preferred_element_type=f32)
            acc = part if acc is None else acc + part
        return acc

    PRE[...] = third(1)
    for n, ok in enumerate((s < N - 1, s > 0)):
        @pl.when(ok)
        def _(n=n):
            for c in halo[n]:
                c.wait_recv()

    spread(lambda i: HV[0, :, i], XL, 0)
    spread(lambda i: HV[1, :, i], XL, 2)

    PRE[...] = PRE[...] + third(0) + third(2)

    dsum = jnp.zeros((C, LANES), f32)
    for j in range(R):
        p = PRE[:, pl.ds(j * LANES, LANES)] + bcol
        e = jnp.exp(-jnp.abs(p))
        soft = jnp.maximum(p, 0.0) + jnp.log(1.0 + e)
        gate = jnp.where(p >= 0.0, 1.0, e) / (1.0 + e)
        act = leakage * p + (1.0 - leakage) * soft
        AIS[:, 0, j] = act.reshape(Pn, SHARE, LANES).astype(bf16)
        u = RCVW[:, j].astype(f32).reshape(C, LANES)
        d = (u * (leakage + (1.0 - leakage) * gate)).astype(bf16)
        DX[1, 1 + j] = d
        DB[:, pl.ds(j * LANES, LANES)] = d
        dsum = dsum + d.astype(f32)

    dcol = jnp.sum(dsum, axis=1, keepdims=True)
    gsend = []
    for b in range(3):
        GT[b, :, pl.ds(0, g.KW)] = lax.dot_general(
            DB[...], XL[:, pl.ds(b * LANES, R * LANES)],
            (((1,), (1,)), ((), ())), preferred_element_type=f32,
        )
        cur = GT[b, :, last]
        cur = jnp.where(lane < edge, cur, 0.0)
        if b == 0:
            cur = jnp.where(lane == edge, dcol, cur)
        GT[b, :, last] = cur
        for to in range(Pn):
            GS[b, to] = GT[b, pl.ds(SHARE * to, SHARE), :].astype(GS.dtype)
        sent = []
        for k in sorted(range(1, Pn), key=nearness, reverse=True):
            to = chan_peer(k)
            c = copy(GS.at[b, to], GR.at[b, r], g_s.at[b, k], g_r.at[b, k], s, to)
            start(c)
            sent.append(c)
        gsend.append(sent)
        GR[b, r] = GS[b, r]

    dcopies = []
    for e, (ds, dr) in enumerate(around):
        if dr == 0:
            src, dst = DX.at[1, pl.ds(1, R)], DX.at[1 - ds, pl.ds(1, R)]
        elif dr < 0:
            src, dst = DX.at[1, 1], DX.at[1 - ds, R + 1]
        else:
            src, dst = DX.at[1, R], DX.at[1 - ds, 0]
        c = copy(src, dst, d_s.at[e], d_r.at[e], s + ds, r + dr)
        pl.when(inside(ds, dr))(c.start)
        pending.append((inside(ds, dr), c))
        dcopies.append((inside(-ds, -dr), c))

    for b in range(3):
        whole = W1[2 - b].astype(f32).T
        blocks = []
        for a in range(3):
            for c_ in range(3):
                at = ((2 - a) * 3 + (2 - c_)) * C
                blocks.append(whole[at : at + C])
        W2[b] = jnp.concatenate(blocks, axis=1).astype(bf16)

    for b in range(3):
        for c in gsend[b]:
            c.wait_recv()
        acc = GR[b, 0].astype(f32)
        for q in range(1, Pn):
            acc = acc + GR[b, q].astype(f32)
        for j in range(g.NJ):
            t = b * g.NJ + j
            SB[t // g.T, t % g.T] = acc[:, j * LANES : (j + 1) * LANES]
    for t in range(3 * g.NJ, M * g.T):
        SB[t // g.T, t % g.T] = jnp.zeros(tile, f32)
    q1send = []
    for k in range(1, M):
        m, to_s = group_peer(k)
        c = copy(SB.at[m], Q1.at[member], q1_s.at[k], q1_r.at[k], to_s, r)
        start(c)
        q1send.append(c)
    Q1[member] = SB[member]

    for ok, c in dcopies:
        pl.when(ok)(c.wait_recv)
    for a in range(3):
        spread(lambda i, a=a: DX[a, i], DL, a)
    PRE[...] = conv(W2, DL)
    for j in range(R):
        v = PRE[:, pl.ds(j * LANES, LANES)]
        AIS[:, 1, j] = v.reshape(Pn, SHARE, LANES).astype(bf16)
    isend = []
    for k in range(1, Pn):
        to = chan_peer(k)
        c = copy(AIS.at[to], AIR.at[r], i_s.at[k], i_r.at[k], s, to)
        start(c)
        isend.append(c)
    AIR[r] = AIS[r]

    for c in q1send:
        c.wait_recv()
    acc = Q1[0]
    for m in range(1, M):
        acc = acc + Q1[m]
    Q2[block] = acc
    heard(1)
    q2send = []
    for k in range(1, B):
        c = copy(Q2.at[block], Q2.at[block], q2_s.at[k], q2_r.at[k], block_peer(k), r)
        start(c)
        q2send.append(c)
    for c in isend:
        c.wait_recv()
    for n, out in enumerate((act_o, ig_o)):
        TALL[n] = AIR[:, n].astype(f32).reshape(g.H * SHARE, LANES)
        for q in range(SHARE):
            out[q] = TALL[n, pl.ds(q, g.H, stride=SHARE), :].astype(bf16)
    for c in q2send:
        c.wait_recv()
    acc = Q2[0]
    for m in range(1, B):
        acc = acc + Q2[m]
    FIN[member] = acc * g.factor
    q3send = []
    for k in range(1, M):
        c = copy(FIN.at[member], FIN.at[member], q3_s.at[k], q3_r.at[k], group_peer(k)[1], r)
        start(c)
        q3send.append(c)
    for c in q3send:
        c.wait_recv()
    for a in range(3):
        for b in range(3):
            for c_ in range(3):
                at = (a * 3 + c_) * C
                t = b * g.NJ + at // LANES
                off = at % LANES
                wg_o[(a * 3 + b) * 3 + c_] = FIN[t // g.T, t % g.T][:, off : off + C]
    t = g.NJ - 1
    sums = FIN[t // g.T, t % g.T][:, edge : edge + 1]
    spot = lax.broadcasted_iota(jnp.int32, tile, 0) == lax.broadcasted_iota(jnp.int32, tile, 1)
    bg_o[...] = jnp.sum(jnp.where(spot, sums, 0.0), axis=0, keepdims=True)[:, :SHARE]

    for ok, c in pending:
        if ok is None:
            c.wait_send()
        else:
            pl.when(ok)(c.wait_send)


def deliver(act, ig, wg, bg, act_o, ig_o, wg_o, bg_o, sems):
    pairs = ((act, act_o), (ig, ig_o), (wg, wg_o), (bg, bg_o))
    moves = [pltpu.make_async_copy(a, b, sems.at[n]) for n, (a, b) in enumerate(pairs)]
    for c in moves:
        c.start()
    for c in moves:
        c.wait()


def shards(g, volume, weight, bias, upstream):
    Pn, R, C, M, B = g.P, g.R, g.C, g.M, g.B
    vol, up = volume[:, 0], upstream[:, 0]
    wl = jnp.transpose(weight, (2, 3, 4, 0, 1)).reshape(27, SHARE, C)
    sds = jax.ShapeDtypeStruct
    hbm = pl.BlockSpec(memory_space=pltpu.HBM)
    rows = (R + 2) * LANES
    dma = pltpu.SemaphoreType.DMA
    V = pltpu.VMEM
    chan = [dma((Pn,)), dma((Pn,))]
    scratch = [
        V((2, SHARE, g.H, LANES), bf16),
        V((27, SHARE, C), bf16),
        pltpu.SMEM((1, SHARE), f32),
        V((2, SHARE * g.H, LANES), f32),
        V((Pn, R + 2, SHARE, LANES), bf16),
        V((Pn, R + 3 * g.NJ, SHARE, LANES), bf16),
        V((Pn, R + 2, SHARE, LANES), bf16),
        V((Pn, R + 3 * g.NJ, SHARE, LANES), bf16),
        V((2, Pn, R + 2, SHARE, LANES), bf16),
        V((9 * C, rows), bf16),
        V((3, R + 2, C, LANES), bf16),
        V((9 * C, rows), bf16),
        V((3, C, g.KW), bf16),
        V((3, 3, C, 3 * C), bf16),
        V((3, C, g.KW), bf16),
        V((C, R * LANES), f32),
        V((C, R * LANES), bf16),
        V((Pn, 2, R, SHARE, LANES), bf16),
        V((Pn, 2, R, SHARE, LANES), bf16),
        V((3, C, g.KP), f32),
        V((3, Pn, SHARE, g.KP), bf16),
        V((3, Pn, SHARE, g.KP), bf16),
        V((M, g.T, SHARE, LANES), f32),
        V((M, g.T, SHARE, LANES), f32),
        V((B, g.T, SHARE, LANES), f32),
        V((M, g.T, SHARE, LANES), f32),
        dma((4,)),
        *chan, *chan,
        pltpu.SemaphoreType.REGULAR((2,)),
        dma((2, Pn)), dma((2, Pn)),
        dma((8,)), dma((8,)),
        *chan,
        dma((3, Pn)), dma((3, Pn)),
        dma((M,)), dma((M,)),
        dma((B,)), dma((B,)),
        dma((M,)), dma((M,)),
    ]
    act, ig, wg, bg = pl.pallas_call(
        functools.partial(kernel, g),
        out_shape=(
            sds((SHARE, g.H, LANES), bf16),
            sds((SHARE, g.H, LANES), bf16),
            sds((27, SHARE, C), f32),
            sds((1, SHARE), f32),
        ),
        in_specs=[hbm] * 4,
        out_specs=(pl.BlockSpec(memory_space=pltpu.VMEM),) * 4,
        scratch_shapes=scratch,
        compiler_params=pltpu.CompilerParams(
            collective_id=0, has_side_effects=True, vmem_limit_bytes=40 << 20
        ),
    )(*(pltpu.with_memory_space_constraint(x, pltpu.HBM) for x in (vol, up, wl, bias[None])))
    act, ig, wg, bg = pl.pallas_call(
        deliver,
        out_shape=(
            sds((SHARE, g.H, LANES), bf16),
            sds((SHARE, g.H, LANES), bf16),
            sds((27, SHARE, C), f32),
            sds((1, SHARE), f32),
        ),
        in_specs=[pl.BlockSpec(memory_space=pl.ANY)] * 4,
        out_specs=(hbm,) * 4,
        scratch_shapes=[dma((4,))],
        compiler_params=pltpu.CompilerParams(vmem_limit_bytes=1 << 20),
    )(act, ig, wg, bg)
    wgrad = jnp.transpose(wg.reshape(3, 3, 3, SHARE, C), (3, 4, 0, 1, 2))
    return act[:, None], ig[:, None], wgrad, bg[0]


def solution(mesh, rows=48, halves=2, blocks=8):
    planes, ranks = mesh.shape["space"], mesh.shape["chan"]
    factor = 1.0 / math.sqrt(planes * rows * LANES)
    g = Plan(planes, ranks, rows, halves, blocks, factor)
    field = P("chan", "space", None, None)
    filters = P("chan", None, None, None, None)
    return jax.shard_map(
        functools.partial(shards, g),
        mesh=mesh,
        in_specs=(field, filters, P("chan"), field),
        out_specs=(field, field, filters, P("chan")),
        check_vma=False,
    )
```

```python
import functools
import math

import jax
import jax.numpy as jnp
from jax import lax
from jax.experimental import pallas as pl
from jax.experimental.pallas import tpu as pltpu
from jax.sharding import PartitionSpec as P

MESH = pl.DeviceIdType.MESH
f32 = jnp.float32
bf16 = jnp.bfloat16
leakage = 0.1
LANES = 128
SHARE = 8


class Plan:
    def __init__(self, planes, ranks, rows, halves, blocks, factor):
        self.N = planes
        self.P = ranks
        self.R = rows // ranks
        self.H = rows
        self.C = SHARE * ranks
        self.X = halves
        self.B = blocks
        self.U = planes // (halves * blocks)
        self.M = self.U * self.X
        self.KW = 9 * self.C
        self.NJ = self.KW // LANES + 1
        self.KP = self.NJ * LANES
        self.T = -(-3 * self.NJ // self.M)
        self.factor = factor


def kernel(
    g, vol, up, wl, bias,
    act_o, ig_o, wg_o, bg_o,
    RAW, RAWW, RAWB, TALL, SENDV, SENDW, RCVV, RCVW, HV, XL, DX, DL, W1, WA, W2, PRE, DB, AIS, AIR,
    GT, GS, GR, SB, Q1, Q2, FIN,
    l_s, v_s, v_r, w_s, w_r, far, p_s, p_r, d_s, d_r, i_s, i_r,
    g_s, g_r, q1_s, q1_r, q2_s, q2_r, q3_s, q3_r,
):
    N, Pn, R, C, M, B, U = g.N, g.P, g.R, g.C, g.M, g.B, g.U
    s = lax.axis_index("space")
    r = lax.axis_index("chan")
    span = B * U
    x_lo, within = s // span, s % span
    block, unit = within // U, within % U
    member = x_lo * U + unit
    pending = []

    def chan_peer(k):
        return lax.rem(r + k, Pn)

    def group_peer(k):
        m = lax.rem(member + k, M)
        return m, (m // U) * span + block * U + m % U

    def block_peer(k):
        b = lax.rem(block + k, B)
        return x_lo * span + b * U + unit

    def copy(src, dst, ssem, rsem, to_s, to_r):
        return pltpu.make_async_remote_copy(
            src_ref=src, dst_ref=dst, send_sem=ssem, recv_sem=rsem,
            device_id=(to_s, to_r), device_id_type=MESH,
        )

    def start(c):
        c.start()
        pending.append((None, c))

    around = [(ds, dr) for ds in (-1, 0, 1) for dr in (-1, 0, 1) if (ds, dr) != (0, 0)]

    def inside(ds, dr):
        ok = None
        for here, step, end in ((s, ds, N), (r, dr, Pn)):
            if step:
                near = here > 0 if step < 0 else here < end - 1
                ok = near if ok is None else jnp.logical_and(ok, near)
        return ok

    barrier = pltpu.get_barrier_semaphore()

    def greet(to_s, to_r):
        pl.semaphore_signal(barrier, inc=1, device_id=(to_s, to_r), device_id_type=MESH)

    for k in range(1, Pn):
        greet(s, chan_peer(k))
    for k in range(1, M):
        greet(group_peer(k)[1], r)
    near = sorted({1, B - 1} - {0})
    for k in near:
        greet(block_peer(k), r)
    for ds, dr in around:
        pl.when(inside(ds, dr))(functools.partial(greet, s + ds, r + dr))
    wide_s = 1 + jnp.where(s > 0, 1, 0) + jnp.where(s < N - 1, 1, 0)
    wide_r = 1 + jnp.where(r > 0, 1, 0) + jnp.where(r < Pn - 1, 1, 0)

    V, Wt = R + 2, R
    loads = [
        pltpu.make_async_copy(vol, RAW.at[0], l_s.at[0]),
        pltpu.make_async_copy(up, RAW.at[1], l_s.at[1]),
        pltpu.make_async_copy(wl, RAWW, l_s.at[2]),
        pltpu.make_async_copy(bias, RAWB, l_s.at[3]),
    ]
    for c in loads:
        c.start()
    tile = (SHARE, LANES)
    edge = g.KW % LANES
    for c in loads:
        c.wait()
    sub = lax.broadcasted_iota(jnp.int32, (SHARE, g.KP - g.KW), 0)
    col = lax.broadcasted_iota(jnp.int32, (SHARE, g.KP - g.KW), 1)
    b0 = jnp.zeros((SHARE, g.KP - g.KW), f32)
    for q in range(SHARE):
        b0 = jnp.where(sub == q, RAWB[0, q], b0)
    hi = b0.astype(bf16).astype(f32)
    mid = (b0 - hi).astype(bf16).astype(f32)
    low = (b0 - hi - mid).astype(bf16).astype(f32)
    tail = jnp.where(col == 0, hi, jnp.where(col == 1, mid, jnp.where(col == 2, low, 0.0)))
    for b in range(3):
        taps = [RAWW[(a * 3 + b) * 3 + c_].astype(f32) for a in range(3) for c_ in range(3)]
        whole = jnp.concatenate(taps + [tail], axis=1)
        for j in range(g.NJ):
            part = whole[:, j * LANES : (j + 1) * LANES].astype(bf16)
            for to in range(Pn):
                SENDW[to, Wt + b * g.NJ + j] = part
    for n in range(2):
        TALL[n] = RAW[n].astype(f32).reshape(SHARE * g.H, LANES)
    zero_tile = jnp.zeros(tile, bf16)
    SENDV[0, 0] = zero_tile
    SENDV[Pn - 1, R + 1] = zero_tile
    for h in range(g.H):
        row = TALL[0, pl.ds(h, SHARE, stride=g.H), :].astype(bf16)
        for to in range(Pn):
            if 0 <= h + 1 - R * to < V:
                SENDV[to, h + 1 - R * to] = row
        SENDW[h // R, h % R] = TALL[1, pl.ds(h, SHARE, stride=g.H), :].astype(bf16)

    pl.semaphore_wait(barrier, (Pn - 1) + (M - 1) + len(near) + wide_s * wide_r - 1)

    reach = [1 << i for i in range(8) if 1 << i < B // 2]

    def relay(i):
        if i < len(reach):
            for k in sorted({reach[i], B - reach[i]}):
                pl.semaphore_signal(
                    far.at[i], inc=1, device_id=(block_peer(k), r), device_id_type=MESH
                )

    def heard(i):
        if i < len(reach):
            pl.semaphore_wait(far.at[i], len({reach[i], B - reach[i]}))

    relay(0)

    RCVV[r] = SENDV[r]

    def nearness(k):
        return k % 2, min(k, Pn - k)

    vsend, wsend = [], []
    for k in sorted(range(1, Pn), key=nearness, reverse=True):
        to = chan_peer(k)
        c = copy(SENDV.at[to], RCVV.at[r], v_s.at[k], v_r.at[k], s, to)
        start(c)
        vsend.append((k, c))
    for k in range(1, Pn):
        to = chan_peer(k)
        c = copy(SENDW.at[to], RCVW.at[r], w_s.at[k], w_r.at[k], s, to)
        start(c)
        wsend.append(c)
    RCVW[r] = SENDW[r]

    def clear(ref, a):
        def body(i, _):
            ref[a, i] = jnp.zeros(ref.shape[2:], bf16)
            return 0
        lax.fori_loop(0, R + 2, body, 0)

    def clear_rows(ref, a):
        def body(i, _):
            ref[a, i] = jnp.zeros(ref.shape[2:], bf16)
            return 0
        lax.fori_loop(0, Pn, body, 0)

    @pl.when(s == 0)
    def _():
        clear_rows(HV, 0)
        clear(DX, 0)

    @pl.when(s == N - 1)
    def _():
        clear_rows(HV, 1)
        clear(DX, 2)

    @pl.when(r == 0)
    def _():
        for a in range(3):
            DX[a, 0] = jnp.zeros((C, LANES), bf16)

    @pl.when(r == Pn - 1)
    def _():
        for a in range(3):
            DX[a, R + 1] = jnp.zeros((C, LANES), bf16)

    halo = [[], []]

    def forward(k):
        q = lax.rem(r + Pn - k, Pn)
        for n, (ok, to) in enumerate(((s > 0, s - 1), (s < N - 1, s + 1))):
            c = copy(RCVV.at[q], HV.at[1 - n, q], p_s.at[n, k], p_r.at[n, k], to, r)
            pl.when(ok)(c.start)
            pending.append((ok, c))
            halo[n].append(c)

    forward(0)
    for k, c in sorted(vsend, key=lambda kc: nearness(kc[0])):
        c.wait_recv()
        forward(k)

    heard(0)
    relay(1)
    last = pl.ds((g.NJ - 1) * LANES, LANES)
    lane = lax.broadcasted_iota(jnp.int32, (C, LANES), 1)

    def spread(row, out, a):
        def body(i, _):
            x = row(i).astype(f32).reshape(C, LANES)
            at = pl.ds(pl.multiple_of(i * LANES, LANES), LANES)
            before = jnp.where(lane == 0, 0.0, pltpu.roll(x, 1, 1))
            after = jnp.where(lane == LANES - 1, 0.0, pltpu.roll(x, LANES - 1, 1))
            out[pl.ds((3 * a) * C, C), at] = before.astype(bf16)
            out[pl.ds((3 * a + 1) * C, C), at] = x.astype(bf16)
            out[pl.ds((3 * a + 2) * C, C), at] = after.astype(bf16)
            return 0
        lax.fori_loop(0, R + 2, body, 0)

    spread(lambda i: RCVV[:, i], XL, 1)

    for c in wsend:
        c.wait_recv()
    for b in range(3):
        whole = jnp.concatenate(
            [RCVW[:, Wt + b * g.NJ + j].astype(f32).reshape(C, LANES) for j in range(g.NJ)], axis=1
        )
        W1[b] = whole[:, : g.KW].astype(bf16)
        for a in range(3):
            WA[a, b] = whole[:, a * 3 * C : (a + 1) * 3 * C].astype(bf16)
        if b == 0:
            end = whole[:, g.KP - LANES :]
            own = jnp.logical_and(lane >= edge, lane < edge + 3)
            bcol = jnp.sum(jnp.where(own, end, 0.0), axis=1, keepdims=True)

    def conv(w, x):
        acc = None
        for b in range(3):
            part = jnp.dot(w[b], x[:, pl.ds(b * LANES, R * LANES)], preferred_element_type=f32)
            acc = part if acc is None else acc + part
        return acc

    def third(a):
        acc = None
        for b in range(3):
            x = XL[pl.ds(a * 3 * C, 3 * C), pl.ds(b * LANES, R * LANES)]
            part = jnp.dot(WA[a, b], x, preferred_element_type=f32)
            acc = part if acc is None else acc + part
        return acc

    PRE[...] = third(1)
    for n, ok in enumerate((s < N - 1, s > 0)):
        @pl.when(ok)
        def _(n=n):
            for c in halo[n]:
                c.wait_recv()

    spread(lambda i: HV[0, :, i], XL, 0)
    spread(lambda i: HV[1, :, i], XL, 2)

    PRE[...] = PRE[...] + third(0) + third(2)

    dsum = jnp.zeros((C, LANES), f32)
    for j in range(R):
        p = PRE[:, pl.ds(j * LANES, LANES)] + bcol
        e = jnp.exp(-jnp.abs(p))
        soft = jnp.maximum(p, 0.0) + jnp.log(1.0 + e)
        gate = jnp.where(p >= 0.0, 1.0, e) / (1.0 + e)
        act = leakage * p + (1.0 - leakage) * soft
        AIS[:, 0, j] = act.reshape(Pn, SHARE, LANES).astype(bf16)
        u = RCVW[:, j].astype(f32).reshape(C, LANES)
        d = (u * (leakage + (1.0 - leakage) * gate)).astype(bf16)
        DX[1, 1 + j] = d
        DB[:, pl.ds(j * LANES, LANES)] = d
        dsum = dsum + d.astype(f32)

    dcol = jnp.sum(dsum, axis=1, keepdims=True)
    gsend = []
    for b in range(3):
        GT[b, :, pl.ds(0, g.KW)] = lax.dot_general(
            DB[...], XL[:, pl.ds(b * LANES, R * LANES)],
            (((1,), (1,)), ((), ())), preferred_element_type=f32,
        )
        cur = GT[b, :, last]
        cur = jnp.where(lane < edge, cur, 0.0)
        if b == 0:
            cur = jnp.where(lane == edge, dcol, cur)
        GT[b, :, last] = cur
        for to in range(Pn):
            GS[b, to] = GT[b, pl.ds(SHARE * to, SHARE), :].astype(GS.dtype)
        sent = []
        for k in sorted(range(1, Pn), key=nearness, reverse=True):
            to = chan_peer(k)
            c = copy(GS.at[b, to], GR.at[b, r], g_s.at[b, k], g_r.at[b, k], s, to)
            start(c)
            sent.append(c)
        gsend.append(sent)
        GR[b, r] = GS[b, r]

    dcopies = []
    for e, (ds, dr) in enumerate(around):
        if dr == 0:
            src, dst = DX.at[1, pl.ds(1, R)], DX.at[1 - ds, pl.ds(1, R)]
        elif dr < 0:
            src, dst = DX.at[1, 1], DX.at[1 - ds, R + 1]
        else:
            src, dst = DX.at[1, R], DX.at[1 - ds, 0]
        c = copy(src, dst, d_s.at[e], d_r.at[e], s + ds, r + dr)
        pl.when(inside(ds, dr))(c.start)
        pending.append((inside(ds, dr), c))
        dcopies.append((inside(-ds, -dr), c))

    for b in range(3):
        whole = W1[2 - b].astype(f32).T
        blocks = []
        for a in range(3):
            for c_ in range(3):
                at = ((2 - a) * 3 + (2 - c_)) * C
                blocks.append(whole[at : at + C])
        W2[b] = jnp.concatenate(blocks, axis=1).astype(bf16)

    for b in range(3):
        for c in gsend[b]:
            c.wait_recv()
        acc = GR[b, 0].astype(f32)
        for q in range(1, Pn):
            acc = acc + GR[b, q].astype(f32)
        for j in range(g.NJ):
            t = b * g.NJ + j
            SB[t // g.T, t % g.T] = acc[:, j * LANES : (j + 1) * LANES]
    for t in range(3 * g.NJ, M * g.T):
        SB[t // g.T, t % g.T] = jnp.zeros(tile, f32)
    q1send = []
    for k in range(1, M):
        m, to_s = group_peer(k)
        c = copy(SB.at[m], Q1.at[member], q1_s.at[k], q1_r.at[k], to_s, r)
        start(c)
        q1send.append(c)
    Q1[member] = SB[member]

    for ok, c in dcopies:
        pl.when(ok)(c.wait_recv)
    for a in range(3):
        spread(lambda i, a=a: DX[a, i], DL, a)
    for c in q1send:
        c.wait_recv()
    acc = Q1[0]
    for m in range(1, M):
        acc = acc + Q1[m]
    Q2[block] = acc
    heard(1)
    q2send = []
    for k in sorted(range(1, B), key=lambda k: -min(k, B - k)):
        c = copy(Q2.at[block], Q2.at[block], q2_s.at[k], q2_r.at[k], block_peer(k), r)
        start(c)
        q2send.append(c)
    PRE[...] = conv(W2, DL)
    for j in range(R):
        v = PRE[:, pl.ds(j * LANES, LANES)]
        AIS[:, 1, j] = v.reshape(Pn, SHARE, LANES).astype(bf16)
    isend = []
    for k in range(1, Pn):
        to = chan_peer(k)
        c = copy(AIS.at[to], AIR.at[r], i_s.at[k], i_r.at[k], s, to)
        start(c)
        isend.append(c)
    AIR[r] = AIS[r]

    for c in q2send:
        c.wait_recv()
    acc = Q2[0]
    for m in range(1, B):
        acc = acc + Q2[m]
    FIN[member] = acc * g.factor
    q3send = []
    for k in range(1, M):
        c = copy(FIN.at[member], FIN.at[member], q3_s.at[k], q3_r.at[k], group_peer(k)[1], r)
        start(c)
        q3send.append(c)
    for c in isend:
        c.wait_recv()
    for n, out in enumerate((act_o, ig_o)):
        TALL[n] = AIR[:, n].astype(f32).reshape(g.H * SHARE, LANES)
        for q in range(SHARE):
            out[q] = TALL[n, pl.ds(q, g.H, stride=SHARE), :].astype(bf16)
    for c in q3send:
        c.wait_recv()
    for a in range(3):
        for b in range(3):
            for c_ in range(3):
                at = (a * 3 + c_) * C
                t = b * g.NJ + at // LANES
                off = at % LANES
                wg_o[(a * 3 + b) * 3 + c_] = FIN[t // g.T, t % g.T][:, off : off + C]
    t = g.NJ - 1
    sums = FIN[t // g.T, t % g.T][:, edge : edge + 1]
    spot = lax.broadcasted_iota(jnp.int32, tile, 0) == lax.broadcasted_iota(jnp.int32, tile, 1)
    bg_o[...] = jnp.sum(jnp.where(spot, sums, 0.0), axis=0, keepdims=True)[:, :SHARE]

    for ok, c in pending:
        if ok is None:
            c.wait_send()
        else:
            pl.when(ok)(c.wait_send)


def deliver(act, ig, wg, bg, act_o, ig_o, wg_o, bg_o, sems):
    pairs = ((act, act_o), (ig, ig_o), (wg, wg_o), (bg, bg_o))
    moves = [pltpu.make_async_copy(a, b, sems.at[n]) for n, (a, b) in enumerate(pairs)]
    for c in moves:
        c.start()
    for c in moves:
        c.wait()


def shards(g, volume, weight, bias, upstream):
    Pn, R, C, M, B = g.P, g.R, g.C, g.M, g.B
    vol, up = volume[:, 0], upstream[:, 0]
    wl = jnp.transpose(weight, (2, 3, 4, 0, 1)).reshape(27, SHARE, C)
    sds = jax.ShapeDtypeStruct
    hbm = pl.BlockSpec(memory_space=pltpu.HBM)
    rows = (R + 2) * LANES
    dma = pltpu.SemaphoreType.DMA
    V = pltpu.VMEM
    chan = [dma((Pn,)), dma((Pn,))]
    scratch = [
        V((2, SHARE, g.H, LANES), bf16),
        V((27, SHARE, C), bf16),
        pltpu.SMEM((1, SHARE), f32),
        V((2, SHARE * g.H, LANES), f32),
        V((Pn, R + 2, SHARE, LANES), bf16),
        V((Pn, R + 3 * g.NJ, SHARE, LANES), bf16),
        V((Pn, R + 2, SHARE, LANES), bf16),
        V((Pn, R + 3 * g.NJ, SHARE, LANES), bf16),
        V((2, Pn, R + 2, SHARE, LANES), bf16),
        V((9 * C, rows), bf16),
        V((3, R + 2, C, LANES), bf16),
        V((9 * C, rows), bf16),
        V((3, C, g.KW), bf16),
        V((3, 3, C, 3 * C), bf16),
        V((3, C, g.KW), bf16),
        V((C, R * LANES), f32),
        V((C, R * LANES), bf16),
        V((Pn, 2, R, SHARE, LANES), bf16),
        V((Pn, 2, R, SHARE, LANES), bf16),
        V((3, C, g.KP), f32),
        V((3, Pn, SHARE, g.KP), bf16),
        V((3, Pn, SHARE, g.KP), bf16),
        V((M, g.T, SHARE, LANES), f32),
        V((M, g.T, SHARE, LANES), f32),
        V((B, g.T, SHARE, LANES), f32),
        V((M, g.T, SHARE, LANES), f32),
        dma((4,)),
        *chan, *chan,
        pltpu.SemaphoreType.REGULAR((2,)),
        dma((2, Pn)), dma((2, Pn)),
        dma((8,)), dma((8,)),
        *chan,
        dma((3, Pn)), dma((3, Pn)),
        dma((M,)), dma((M,)),
        dma((B,)), dma((B,)),
        dma((M,)), dma((M,)),
    ]
    act, ig, wg, bg = pl.pallas_call(
        functools.partial(kernel, g),
        out_shape=(
            sds((SHARE, g.H, LANES), bf16),
            sds((SHARE, g.H, LANES), bf16),
            sds((27, SHARE, C), f32),
            sds((1, SHARE), f32),
        ),
        in_specs=[hbm] * 4,
        out_specs=(pl.BlockSpec(memory_space=pltpu.VMEM),) * 4,
        scratch_shapes=scratch,
        compiler_params=pltpu.CompilerParams(
            collective_id=0, has_side_effects=True, vmem_limit_bytes=40 << 20
        ),
    )(*(pltpu.with_memory_space_constraint(x, pltpu.HBM) for x in (vol, up, wl, bias[None])))
    act, ig, wg, bg = pl.pallas_call(
        deliver,
        out_shape=(
            sds((SHARE, g.H, LANES), bf16),
            sds((SHARE, g.H, LANES), bf16),
            sds((27, SHARE, C), f32),
            sds((1, SHARE), f32),
        ),
        in_specs=[pl.BlockSpec(memory_space=pl.ANY)] * 4,
        out_specs=(hbm,) * 4,
        scratch_shapes=[dma((4,))],
        compiler_params=pltpu.CompilerParams(vmem_limit_bytes=1 << 20),
    )(act, ig, wg, bg)
    wgrad = jnp.transpose(wg.reshape(3, 3, 3, SHARE, C), (3, 4, 0, 1, 2))
    return act[:, None], ig[:, None], wgrad, bg[0]


def solution(mesh, rows=48, halves=2, blocks=8):
    planes, ranks = mesh.shape["space"], mesh.shape["chan"]
    factor = 1.0 / math.sqrt(planes * rows * LANES)
    g = Plan(planes, ranks, rows, halves, blocks, factor)
    field = P("chan", "space", None, None)
    filters = P("chan", None, None, None, None)
    return jax.shard_map(
        functools.partial(shards, g),
        mesh=mesh,
        in_specs=(field, filters, P("chan"), field),
        out_specs=(field, field, filters, P("chan")),
        check_vma=False,
    )
```

```python
import functools
import math

import jax
import jax.numpy as jnp
from jax import lax
from jax.experimental import pallas as pl
from jax.experimental.pallas import tpu as pltpu
from jax.sharding import PartitionSpec as P

MESH = pl.DeviceIdType.MESH
f32 = jnp.float32
bf16 = jnp.bfloat16
leakage = 0.1
LANES = 128
SHARE = 8


class Plan:
    def __init__(self, planes, ranks, rows, halves, blocks, factor):
        self.N = planes
        self.P = ranks
        self.R = rows // ranks
        self.H = rows
        self.C = SHARE * ranks
        self.X = halves
        self.B = blocks
        self.U = planes // (halves * blocks)
        self.M = self.U * self.X
        self.KW = 9 * self.C
        self.NJ = self.KW // LANES + 1
        self.KP = self.NJ * LANES
        self.T = -(-3 * self.NJ // self.M)
        self.factor = factor


def kernel(
    g, vol, up, wl, bias,
    act_o, ig_o, wg_o, bg_o,
    RAW, RAWW, RAWB, TALL, SENDV, SENDU, SENDW, RCVV, RCVU, RCVW, HV, XL, DX, DL, W1, WA, W2, PRE, DB, AIS, AIR,
    GT, GS, GR, SB, Q1, Q2, FIN,
    l_s, v_s, v_r, w_s, w_r, u_s, u_r, far, p_s, p_r, d_s, d_r, i_s, i_r,
    g_s, g_r, q1_s, q1_r, q2_s, q2_r, q3_s, q3_r,
):
    N, Pn, R, C, M, B, U = g.N, g.P, g.R, g.C, g.M, g.B, g.U
    s = lax.axis_index("space")
    r = lax.axis_index("chan")
    span = B * U
    x_lo, within = s // span, s % span
    block, unit = within // U, within % U
    member = x_lo * U + unit
    pending = []

    def chan_peer(k):
        return lax.rem(r + k, Pn)

    def group_peer(k):
        m = lax.rem(member + k, M)
        return m, (m // U) * span + block * U + m % U

    def block_peer(k):
        b = lax.rem(block + k, B)
        return x_lo * span + b * U + unit

    def copy(src, dst, ssem, rsem, to_s, to_r):
        return pltpu.make_async_remote_copy(
            src_ref=src, dst_ref=dst, send_sem=ssem, recv_sem=rsem,
            device_id=(to_s, to_r), device_id_type=MESH,
        )

    def start(c):
        c.start()
        pending.append((None, c))

    around = [(ds, dr) for ds in (-1, 0, 1) for dr in (-1, 0, 1) if (ds, dr) != (0, 0)]

    def inside(ds, dr):
        ok = None
        for here, step, end in ((s, ds, N), (r, dr, Pn)):
            if step:
                near = here > 0 if step < 0 else here < end - 1
                ok = near if ok is None else jnp.logical_and(ok, near)
        return ok

    barrier = pltpu.get_barrier_semaphore()

    def greet(to_s, to_r):
        pl.semaphore_signal(barrier, inc=1, device_id=(to_s, to_r), device_id_type=MESH)

    for k in range(1, Pn):
        greet(s, chan_peer(k))
    for k in range(1, M):
        greet(group_peer(k)[1], r)
    near = sorted({1, B - 1} - {0})
    for k in near:
        greet(block_peer(k), r)
    for ds, dr in around:
        pl.when(inside(ds, dr))(functools.partial(greet, s + ds, r + dr))
    wide_s = 1 + jnp.where(s > 0, 1, 0) + jnp.where(s < N - 1, 1, 0)
    wide_r = 1 + jnp.where(r > 0, 1, 0) + jnp.where(r < Pn - 1, 1, 0)

    V = R + 2
    loads = [
        pltpu.make_async_copy(vol, RAW.at[0], l_s.at[0]),
        pltpu.make_async_copy(up, RAW.at[1], l_s.at[1]),
        pltpu.make_async_copy(wl, RAWW, l_s.at[2]),
        pltpu.make_async_copy(bias, RAWB, l_s.at[3]),
    ]
    for c in loads:
        c.start()
    tile = (SHARE, LANES)
    edge = g.KW % LANES
    for c in loads:
        c.wait()
    sub = lax.broadcasted_iota(jnp.int32, (SHARE, g.KP - g.KW), 0)
    col = lax.broadcasted_iota(jnp.int32, (SHARE, g.KP - g.KW), 1)
    b0 = jnp.zeros((SHARE, g.KP - g.KW), f32)
    for q in range(SHARE):
        b0 = jnp.where(sub == q, RAWB[0, q], b0)
    hi = b0.astype(bf16).astype(f32)
    mid = (b0 - hi).astype(bf16).astype(f32)
    low = (b0 - hi - mid).astype(bf16).astype(f32)
    tail = jnp.where(col == 0, hi, jnp.where(col == 1, mid, jnp.where(col == 2, low, 0.0)))
    for b in range(3):
        taps = [RAWW[(a * 3 + b) * 3 + c_].astype(f32) for a in range(3) for c_ in range(3)]
        whole = jnp.concatenate(taps + [tail], axis=1)
        for j in range(g.NJ):
            part = whole[:, j * LANES : (j + 1) * LANES].astype(bf16)
            for to in range(Pn):
                SENDW[to, b * g.NJ + j] = part
    for n in range(2):
        TALL[n] = RAW[n].astype(f32).reshape(SHARE * g.H, LANES)
    zero_tile = jnp.zeros(tile, bf16)
    SENDV[0, 0] = zero_tile
    SENDV[Pn - 1, R + 1] = zero_tile
    for h in range(g.H):
        row = TALL[0, pl.ds(h, SHARE, stride=g.H), :].astype(bf16)
        for to in range(Pn):
            if 0 <= h + 1 - R * to < V:
                SENDV[to, h + 1 - R * to] = row
        SENDU[h // R, h % R] = TALL[1, pl.ds(h, SHARE, stride=g.H), :].astype(bf16)

    pl.semaphore_wait(barrier, (Pn - 1) + (M - 1) + len(near) + wide_s * wide_r - 1)

    reach = [1 << i for i in range(8) if 1 << i < B // 2]

    def relay(i):
        if i < len(reach):
            for k in sorted({reach[i], B - reach[i]}):
                pl.semaphore_signal(
                    far.at[i], inc=1, device_id=(block_peer(k), r), device_id_type=MESH
                )

    def heard(i):
        if i < len(reach):
            pl.semaphore_wait(far.at[i], len({reach[i], B - reach[i]}))

    relay(0)

    RCVV[r] = SENDV[r]

    def nearness(k):
        return k % 2, min(k, Pn - k)

    vsend, wsend = [], []
    for k in sorted(range(1, Pn), key=nearness, reverse=True):
        to = chan_peer(k)
        c = copy(SENDV.at[to], RCVV.at[r], v_s.at[k], v_r.at[k], s, to)
        start(c)
        vsend.append((k, c))
    for k in range(1, Pn):
        to = chan_peer(k)
        c = copy(SENDW.at[to], RCVW.at[r], w_s.at[k], w_r.at[k], s, to)
        start(c)
        wsend.append(c)
    RCVW[r] = SENDW[r]
    RCVU[r] = SENDU[r]

    def clear(ref, a):
        def body(i, _):
            ref[a, i] = jnp.zeros(ref.shape[2:], bf16)
            return 0
        lax.fori_loop(0, R + 2, body, 0)

    def clear_rows(ref, a):
        def body(i, _):
            ref[a, i] = jnp.zeros(ref.shape[2:], bf16)
            return 0
        lax.fori_loop(0, Pn, body, 0)

    @pl.when(s == 0)
    def _():
        clear_rows(HV, 0)
        clear(DX, 0)

    @pl.when(s == N - 1)
    def _():
        clear_rows(HV, 1)
        clear(DX, 2)

    @pl.when(r == 0)
    def _():
        for a in range(3):
            DX[a, 0] = jnp.zeros((C, LANES), bf16)

    @pl.when(r == Pn - 1)
    def _():
        for a in range(3):
            DX[a, R + 1] = jnp.zeros((C, LANES), bf16)

    halo = [[], []]

    def forward(k):
        q = lax.rem(r + Pn - k, Pn)
        for n, (ok, to) in enumerate(((s > 0, s - 1), (s < N - 1, s + 1))):
            c = copy(RCVV.at[q], HV.at[1 - n, q], p_s.at[n, k], p_r.at[n, k], to, r)
            pl.when(ok)(c.start)
            pending.append((ok, c))
            halo[n].append(c)

    forward(0)
    for k, c in sorted(vsend, key=lambda kc: nearness(kc[0])):
        c.wait_recv()
        forward(k)

    usend = []
    for k in sorted(range(1, Pn), key=nearness, reverse=True):
        to = chan_peer(k)
        c = copy(SENDU.at[to], RCVU.at[r], u_s.at[k], u_r.at[k], s, to)
        start(c)
        usend.append(c)

    heard(0)
    relay(1)
    last = pl.ds((g.NJ - 1) * LANES, LANES)
    lane = lax.broadcasted_iota(jnp.int32, (C, LANES), 1)

    def spread(row, out, a):
        def body(i, _):
            x = row(i).astype(f32).reshape(C, LANES)
            at = pl.ds(pl.multiple_of(i * LANES, LANES), LANES)
            before = jnp.where(lane == 0, 0.0, pltpu.roll(x, 1, 1))
            after = jnp.where(lane == LANES - 1, 0.0, pltpu.roll(x, LANES - 1, 1))
            out[pl.ds((3 * a) * C, C), at] = before.astype(bf16)
            out[pl.ds((3 * a + 1) * C, C), at] = x.astype(bf16)
            out[pl.ds((3 * a + 2) * C, C), at] = after.astype(bf16)
            return 0
        lax.fori_loop(0, R + 2, body, 0)

    spread(lambda i: RCVV[:, i], XL, 1)

    for c in wsend:
        c.wait_recv()
    for b in range(3):
        whole = jnp.concatenate(
            [RCVW[:, b * g.NJ + j].astype(f32).reshape(C, LANES) for j in range(g.NJ)], axis=1
        )
        W1[b] = whole[:, : g.KW].astype(bf16)
        for a in range(3):
            WA[a, b] = whole[:, a * 3 * C : (a + 1) * 3 * C].astype(bf16)
        if b == 0:
            end = whole[:, g.KP - LANES :]
            own = jnp.logical_and(lane >= edge, lane < edge + 3)
            bcol = jnp.sum(jnp.where(own, end, 0.0), axis=1, keepdims=True)

    def conv(w, x):
        acc = None
        for b in range(3):
            part = jnp.dot(w[b], x[:, pl.ds(b * LANES, R * LANES)], preferred_element_type=f32)
            acc = part if acc is None else acc + part
        return acc

    def third(a):
        acc = None
        for b in range(3):
            x = XL[pl.ds(a * 3 * C, 3 * C), pl.ds(b * LANES, R * LANES)]
            part = jnp.dot(WA[a, b], x, preferred_element_type=f32)
            acc = part if acc is None else acc + part
        return acc

    PRE[...] = third(1)
    for n, ok in enumerate((s < N - 1, s > 0)):
        @pl.when(ok)
        def _(n=n):
            for c in halo[n]:
                c.wait_recv()

    spread(lambda i: HV[0, :, i], XL, 0)
    spread(lambda i: HV[1, :, i], XL, 2)

    PRE[...] = PRE[...] + third(0) + third(2)

    for c in usend:
        c.wait_recv()
    dsum = jnp.zeros((C, LANES), f32)
    for j in range(R):
        p = PRE[:, pl.ds(j * LANES, LANES)] + bcol
        e = jnp.exp(-jnp.abs(p))
        soft = jnp.maximum(p, 0.0) + jnp.log(1.0 + e)
        gate = jnp.where(p >= 0.0, 1.0, e) / (1.0 + e)
        act = leakage * p + (1.0 - leakage) * soft
        AIS[:, 0, j] = act.reshape(Pn, SHARE, LANES).astype(bf16)
        u = RCVU[:, j].astype(f32).reshape(C, LANES)
        d = (u * (leakage + (1.0 - leakage) * gate)).astype(bf16)
        DX[1, 1 + j] = d
        DB[:, pl.ds(j * LANES, LANES)] = d
        dsum = dsum + d.astype(f32)

    dcol = jnp.sum(dsum, axis=1, keepdims=True)
    gsend = []
    for b in range(3):
        GT[b, :, pl.ds(0, g.KW)] = lax.dot_general(
            DB[...], XL[:, pl.ds(b * LANES, R * LANES)],
            (((1,), (1,)), ((), ())), preferred_element_type=f32,
        )
        cur = GT[b, :, last]
        cur = jnp.where(lane < edge, cur, 0.0)
        if b == 0:
            cur = jnp.where(lane == edge, dcol, cur)
        GT[b, :, last] = cur
        for to in range(Pn):
            GS[b, to] = GT[b, pl.ds(SHARE * to, SHARE), :].astype(GS.dtype)
        sent = []
        for k in sorted(range(1, Pn), key=nearness, reverse=True):
            to = chan_peer(k)
            c = copy(GS.at[b, to], GR.at[b, r], g_s.at[b, k], g_r.at[b, k], s, to)
            start(c)
            sent.append(c)
        gsend.append(sent)
        GR[b, r] = GS[b, r]

    dcopies = []
    for e, (ds, dr) in enumerate(around):
        if dr == 0:
            src, dst = DX.at[1, pl.ds(1, R)], DX.at[1 - ds, pl.ds(1, R)]
        elif dr < 0:
            src, dst = DX.at[1, 1], DX.at[1 - ds, R + 1]
        else:
            src, dst = DX.at[1, R], DX.at[1 - ds, 0]
        c = copy(src, dst, d_s.at[e], d_r.at[e], s + ds, r + dr)
        pl.when(inside(ds, dr))(c.start)
        pending.append((inside(ds, dr), c))
        dcopies.append((inside(-ds, -dr), c))

    for b in range(3):
        whole = W1[2 - b].astype(f32).T
        blocks = []
        for a in range(3):
            for c_ in range(3):
                at = ((2 - a) * 3 + (2 - c_)) * C
                blocks.append(whole[at : at + C])
        W2[b] = jnp.concatenate(blocks, axis=1).astype(bf16)

    for b in range(3):
        for c in gsend[b]:
            c.wait_recv()
        acc = GR[b, 0].astype(f32)
        for q in range(1, Pn):
            acc = acc + GR[b, q].astype(f32)
        for j in range(g.NJ):
            t = b * g.NJ + j
            SB[t // g.T, t % g.T] = acc[:, j * LANES : (j + 1) * LANES]
    for t in range(3 * g.NJ, M * g.T):
        SB[t // g.T, t % g.T] = jnp.zeros(tile, f32)
    q1send = []
    for k in range(1, M):
        m, to_s = group_peer(k)
        c = copy(SB.at[m], Q1.at[member], q1_s.at[k], q1_r.at[k], to_s, r)
        start(c)
        q1send.append(c)
    Q1[member] = SB[member]

    for ok, c in dcopies:
        pl.when(ok)(c.wait_recv)
    for a in range(3):
        spread(lambda i, a=a: DX[a, i], DL, a)
    for c in q1send:
        c.wait_recv()
    acc = Q1[0]
    for m in range(1, M):
        acc = acc + Q1[m]
    Q2[block] = acc.astype(bf16)
    heard(1)
    q2send = []
    for k in sorted(range(1, B), key=lambda k: -min(k, B - k)):
        c = copy(Q2.at[block], Q2.at[block], q2_s.at[k], q2_r.at[k], block_peer(k), r)
        start(c)
        q2send.append(c)
    PRE[...] = conv(W2, DL)
    for j in range(R):
        v = PRE[:, pl.ds(j * LANES, LANES)]
        AIS[:, 1, j] = v.reshape(Pn, SHARE, LANES).astype(bf16)
    isend = []
    for k in range(1, Pn):
        to = chan_peer(k)
        c = copy(AIS.at[to], AIR.at[r], i_s.at[k], i_r.at[k], s, to)
        start(c)
        isend.append(c)
    AIR[r] = AIS[r]

    for c in q2send:
        c.wait_recv()
    acc = Q2[0].astype(f32)
    for m in range(1, B):
        acc = acc + Q2[m].astype(f32)
    FIN[member] = acc * g.factor
    q3send = []
    for k in range(1, M):
        c = copy(FIN.at[member], FIN.at[member], q3_s.at[k], q3_r.at[k], group_peer(k)[1], r)
        start(c)
        q3send.append(c)
    for c in isend:
        c.wait_recv()
    for n, out in enumerate((act_o, ig_o)):
        TALL[n] = AIR[:, n].astype(f32).reshape(g.H * SHARE, LANES)
        for q in range(SHARE):
            out[q] = TALL[n, pl.ds(q, g.H, stride=SHARE), :].astype(bf16)
    for c in q3send:
        c.wait_recv()
    for a in range(3):
        for b in range(3):
            for c_ in range(3):
                at = (a * 3 + c_) * C
                t = b * g.NJ + at // LANES
                off = at % LANES
                wg_o[(a * 3 + b) * 3 + c_] = FIN[t // g.T, t % g.T][:, off : off + C]
    t = g.NJ - 1
    sums = FIN[t // g.T, t % g.T][:, edge : edge + 1]
    spot = lax.broadcasted_iota(jnp.int32, tile, 0) == lax.broadcasted_iota(jnp.int32, tile, 1)
    bg_o[...] = jnp.sum(jnp.where(spot, sums, 0.0), axis=0, keepdims=True)[:, :SHARE]

    for ok, c in pending:
        if ok is None:
            c.wait_send()
        else:
            pl.when(ok)(c.wait_send)


def deliver(act, ig, wg, bg, act_o, ig_o, wg_o, bg_o, sems):
    pairs = ((act, act_o), (ig, ig_o), (wg, wg_o), (bg, bg_o))
    moves = [pltpu.make_async_copy(a, b, sems.at[n]) for n, (a, b) in enumerate(pairs)]
    for c in moves:
        c.start()
    for c in moves:
        c.wait()


def shards(g, volume, weight, bias, upstream):
    Pn, R, C, M, B = g.P, g.R, g.C, g.M, g.B
    vol, up = volume[:, 0], upstream[:, 0]
    wl = jnp.transpose(weight, (2, 3, 4, 0, 1)).reshape(27, SHARE, C)
    sds = jax.ShapeDtypeStruct
    hbm = pl.BlockSpec(memory_space=pltpu.HBM)
    rows = (R + 2) * LANES
    dma = pltpu.SemaphoreType.DMA
    V = pltpu.VMEM
    chan = [dma((Pn,)), dma((Pn,))]
    scratch = [
        V((2, SHARE, g.H, LANES), bf16),
        V((27, SHARE, C), bf16),
        pltpu.SMEM((1, SHARE), f32),
        V((2, SHARE * g.H, LANES), f32),
        V((Pn, R + 2, SHARE, LANES), bf16),
        V((Pn, R, SHARE, LANES), bf16),
        V((Pn, 3 * g.NJ, SHARE, LANES), bf16),
        V((Pn, R + 2, SHARE, LANES), bf16),
        V((Pn, R, SHARE, LANES), bf16),
        V((Pn, 3 * g.NJ, SHARE, LANES), bf16),
        V((2, Pn, R + 2, SHARE, LANES), bf16),
        V((9 * C, rows), bf16),
        V((3, R + 2, C, LANES), bf16),
        V((9 * C, rows), bf16),
        V((3, C, g.KW), bf16),
        V((3, 3, C, 3 * C), bf16),
        V((3, C, g.KW), bf16),
        V((C, R * LANES), f32),
        V((C, R * LANES), bf16),
        V((Pn, 2, R, SHARE, LANES), bf16),
        V((Pn, 2, R, SHARE, LANES), bf16),
        V((3, C, g.KP), f32),
        V((3, Pn, SHARE, g.KP), bf16),
        V((3, Pn, SHARE, g.KP), bf16),
        V((M, g.T, SHARE, LANES), f32),
        V((M, g.T, SHARE, LANES), f32),
        V((B, g.T, SHARE, LANES), bf16),
        V((M, g.T, SHARE, LANES), f32),
        dma((4,)),
        *chan, *chan, *chan,
        pltpu.SemaphoreType.REGULAR((2,)),
        dma((2, Pn)), dma((2, Pn)),
        dma((8,)), dma((8,)),
        *chan,
        dma((3, Pn)), dma((3, Pn)),
        dma((M,)), dma((M,)),
        dma((B,)), dma((B,)),
        dma((M,)), dma((M,)),
    ]
    act, ig, wg, bg = pl.pallas_call(
        functools.partial(kernel, g),
        out_shape=(
            sds((SHARE, g.H, LANES), bf16),
            sds((SHARE, g.H, LANES), bf16),
            sds((27, SHARE, C), f32),
            sds((1, SHARE), f32),
        ),
        in_specs=[hbm] * 4,
        out_specs=(pl.BlockSpec(memory_space=pltpu.VMEM),) * 4,
        scratch_shapes=scratch,
        compiler_params=pltpu.CompilerParams(
            collective_id=0, has_side_effects=True, vmem_limit_bytes=40 << 20
        ),
    )(*(pltpu.with_memory_space_constraint(x, pltpu.HBM) for x in (vol, up, wl, bias[None])))
    act, ig, wg, bg = pl.pallas_call(
        deliver,
        out_shape=(
            sds((SHARE, g.H, LANES), bf16),
            sds((SHARE, g.H, LANES), bf16),
            sds((27, SHARE, C), f32),
            sds((1, SHARE), f32),
        ),
        in_specs=[pl.BlockSpec(memory_space=pl.ANY)] * 4,
        out_specs=(hbm,) * 4,
        scratch_shapes=[dma((4,))],
        compiler_params=pltpu.CompilerParams(vmem_limit_bytes=1 << 20),
    )(act, ig, wg, bg)
    wgrad = jnp.transpose(wg.reshape(3, 3, 3, SHARE, C), (3, 4, 0, 1, 2))
    return act[:, None], ig[:, None], wgrad, bg[0]


def solution(mesh, rows=48, halves=2, blocks=8):
    planes, ranks = mesh.shape["space"], mesh.shape["chan"]
    factor = 1.0 / math.sqrt(planes * rows * LANES)
    g = Plan(planes, ranks, rows, halves, blocks, factor)
    field = P("chan", "space", None, None)
    filters = P("chan", None, None, None, None)
    return jax.shard_map(
        functools.partial(shards, g),
        mesh=mesh,
        in_specs=(field, filters, P("chan"), field),
        out_specs=(field, field, filters, P("chan")),
        check_vma=False,
    )
```

```python
import functools
import math

import jax
import jax.numpy as jnp
from jax import lax
from jax.experimental import pallas as pl
from jax.experimental.pallas import tpu as pltpu
from jax.sharding import PartitionSpec as P

MESH = pl.DeviceIdType.MESH
f32 = jnp.float32
bf16 = jnp.bfloat16
leakage = 0.1
LANES = 128
SHARE = 8


class Plan:
    def __init__(self, planes, ranks, rows, halves, blocks, factor):
        self.N = planes
        self.P = ranks
        self.R = rows // ranks
        self.H = rows
        self.C = SHARE * ranks
        self.X = halves
        self.B = blocks
        self.U = planes // (halves * blocks)
        self.M = self.U * self.X
        self.KW = 9 * self.C
        self.NJ = self.KW // LANES + 1
        self.KP = self.NJ * LANES
        self.T = -(-3 * self.NJ // self.M)
        self.factor = factor


def kernel(
    g, vol, up, wl, bias,
    act_o, ig_o, wg_o, bg_o,
    RAW, RAWW, RAWB, TALL, SENDV, SENDU, SENDW, RCVV, RCVU, RCVW, HV, XL, DX, DL, W1, WA, W2, PRE, DB, AIS, AIR,
    GT, GS, GR, SB, Q1, Q2, FIN,
    l_s, v_s, v_r, w_s, w_r, u_s, u_r, far, p_s, p_r, d_s, d_r, i_s, i_r,
    g_s, g_r, q1_s, q1_r, q2_s, q2_r, q3_s, q3_r,
):
    N, Pn, R, C, M, B, U = g.N, g.P, g.R, g.C, g.M, g.B, g.U
    s = lax.axis_index("space")
    r = lax.axis_index("chan")
    span = B * U
    x_lo, within = s // span, s % span
    block, unit = within // U, within % U
    member = x_lo * U + unit
    pending = []

    def chan_peer(k):
        return lax.rem(r + k, Pn)

    def group_peer(k):
        m = lax.rem(member + k, M)
        return m, (m // U) * span + block * U + m % U

    def block_peer(k):
        b = lax.rem(block + k, B)
        return x_lo * span + b * U + unit

    def copy(src, dst, ssem, rsem, to_s, to_r):
        return pltpu.make_async_remote_copy(
            src_ref=src, dst_ref=dst, send_sem=ssem, recv_sem=rsem,
            device_id=(to_s, to_r), device_id_type=MESH,
        )

    def start(c):
        c.start()
        pending.append((None, c))

    def sent_all(copies):
        for ok, c in copies:
            if ok is None:
                c.wait_send()
            else:
                pl.when(ok)(c.wait_send)

    around = [(ds, dr) for ds in (-1, 0, 1) for dr in (-1, 0, 1) if (ds, dr) != (0, 0)]

    def inside(ds, dr):
        ok = None
        for here, step, end in ((s, ds, N), (r, dr, Pn)):
            if step:
                near = here > 0 if step < 0 else here < end - 1
                ok = near if ok is None else jnp.logical_and(ok, near)
        return ok

    barrier = pltpu.get_barrier_semaphore()

    def greet(to_s, to_r):
        pl.semaphore_signal(barrier, inc=1, device_id=(to_s, to_r), device_id_type=MESH)

    for k in range(1, Pn):
        greet(s, chan_peer(k))
    for k in range(1, M):
        greet(group_peer(k)[1], r)
    near = sorted({1, B - 1} - {0})
    for k in near:
        greet(block_peer(k), r)
    for ds, dr in around:
        pl.when(inside(ds, dr))(functools.partial(greet, s + ds, r + dr))
    wide_s = 1 + jnp.where(s > 0, 1, 0) + jnp.where(s < N - 1, 1, 0)
    wide_r = 1 + jnp.where(r > 0, 1, 0) + jnp.where(r < Pn - 1, 1, 0)

    V = R + 2
    loads = [
        pltpu.make_async_copy(vol, RAW.at[0], l_s.at[0]),
        pltpu.make_async_copy(up, RAW.at[1], l_s.at[1]),
        pltpu.make_async_copy(wl, RAWW, l_s.at[2]),
        pltpu.make_async_copy(bias, RAWB, l_s.at[3]),
    ]
    for c in loads:
        c.start()
    tile = (SHARE, LANES)
    edge = g.KW % LANES
    for c in loads:
        c.wait()
    sub = lax.broadcasted_iota(jnp.int32, (SHARE, g.KP - g.KW), 0)
    col = lax.broadcasted_iota(jnp.int32, (SHARE, g.KP - g.KW), 1)
    b0 = jnp.zeros((SHARE, g.KP - g.KW), f32)
    for q in range(SHARE):
        b0 = jnp.where(sub == q, RAWB[0, q], b0)
    hi = b0.astype(bf16).astype(f32)
    mid = (b0 - hi).astype(bf16).astype(f32)
    low = (b0 - hi - mid).astype(bf16).astype(f32)
    tail = jnp.where(col == 0, hi, jnp.where(col == 1, mid, jnp.where(col == 2, low, 0.0)))
    for b in range(3):
        taps = [RAWW[(a * 3 + b) * 3 + c_].astype(f32) for a in range(3) for c_ in range(3)]
        whole = jnp.concatenate(taps + [tail], axis=1)
        for j in range(g.NJ):
            part = whole[:, j * LANES : (j + 1) * LANES].astype(bf16)
            for to in range(Pn):
                SENDW[to, b * g.NJ + j] = part
    for n in range(2):
        TALL[n] = RAW[n].astype(f32).reshape(SHARE * g.H, LANES)
    zero_tile = jnp.zeros(tile, bf16)
    SENDV[0, 0] = zero_tile
    SENDV[Pn - 1, R + 1] = zero_tile
    for h in range(g.H):
        row = TALL[0, pl.ds(h, SHARE, stride=g.H), :].astype(bf16)
        for to in range(Pn):
            if 0 <= h + 1 - R * to < V:
                SENDV[to, h + 1 - R * to] = row
        SENDU[h // R, h % R] = TALL[1, pl.ds(h, SHARE, stride=g.H), :].astype(bf16)

    pl.semaphore_wait(barrier, (Pn - 1) + (M - 1) + len(near) + wide_s * wide_r - 1)

    reach = [1 << i for i in range(8) if 1 << i < B // 2]

    def relay(i):
        if i < len(reach):
            for k in sorted({reach[i], B - reach[i]}):
                pl.semaphore_signal(
                    far.at[i], inc=1, device_id=(block_peer(k), r), device_id_type=MESH
                )

    def heard(i):
        if i < len(reach):
            pl.semaphore_wait(far.at[i], len({reach[i], B - reach[i]}))

    relay(0)

    RCVV[r] = SENDV[r]

    def nearness(k):
        return k % 2, min(k, Pn - k)

    vsend, wsend = [], []
    for k in sorted(range(1, Pn), key=nearness, reverse=True):
        to = chan_peer(k)
        c = copy(SENDV.at[to], RCVV.at[r], v_s.at[k], v_r.at[k], s, to)
        start(c)
        vsend.append((k, c))
    for k in range(1, Pn):
        to = chan_peer(k)
        c = copy(SENDW.at[to], RCVW.at[r], w_s.at[k], w_r.at[k], s, to)
        start(c)
        wsend.append(c)
    RCVW[r] = SENDW[r]
    RCVU[r] = SENDU[r]

    def clear(ref, a):
        def body(i, _):
            ref[a, i] = jnp.zeros(ref.shape[2:], bf16)
            return 0
        lax.fori_loop(0, R + 2, body, 0)

    def clear_rows(ref, a):
        def body(i, _):
            ref[a, i] = jnp.zeros(ref.shape[2:], bf16)
            return 0
        lax.fori_loop(0, Pn, body, 0)

    @pl.when(s == 0)
    def _():
        clear_rows(HV, 0)
        clear(DX, 0)

    @pl.when(s == N - 1)
    def _():
        clear_rows(HV, 1)
        clear(DX, 2)

    @pl.when(r == 0)
    def _():
        for a in range(3):
            DX[a, 0] = jnp.zeros((C, LANES), bf16)

    @pl.when(r == Pn - 1)
    def _():
        for a in range(3):
            DX[a, R + 1] = jnp.zeros((C, LANES), bf16)

    halo = [[], []]

    def forward(k):
        q = lax.rem(r + Pn - k, Pn)
        for n, (ok, to) in enumerate(((s > 0, s - 1), (s < N - 1, s + 1))):
            c = copy(RCVV.at[q], HV.at[1 - n, q], p_s.at[n, k], p_r.at[n, k], to, r)
            pl.when(ok)(c.start)
            pending.append((ok, c))
            halo[n].append(c)

    forward(0)
    for k, c in sorted(vsend, key=lambda kc: nearness(kc[0])):
        c.wait_recv()
        forward(k)

    usend = []
    for k in sorted(range(1, Pn), key=nearness, reverse=True):
        to = chan_peer(k)
        c = copy(SENDU.at[to], RCVU.at[r], u_s.at[k], u_r.at[k], s, to)
        start(c)
        usend.append(c)

    heard(0)
    relay(1)
    last = pl.ds((g.NJ - 1) * LANES, LANES)
    lane = lax.broadcasted_iota(jnp.int32, (C, LANES), 1)

    def spread(row, out, a):
        def body(i, _):
            x = row(i).astype(f32).reshape(C, LANES)
            at = pl.ds(pl.multiple_of(i * LANES, LANES), LANES)
            before = jnp.where(lane == 0, 0.0, pltpu.roll(x, 1, 1))
            after = jnp.where(lane == LANES - 1, 0.0, pltpu.roll(x, LANES - 1, 1))
            out[pl.ds((3 * a) * C, C), at] = before.astype(bf16)
            out[pl.ds((3 * a + 1) * C, C), at] = x.astype(bf16)
            out[pl.ds((3 * a + 2) * C, C), at] = after.astype(bf16)
            return 0
        lax.fori_loop(0, R + 2, body, 0)

    spread(lambda i: RCVV[:, i], XL, 1)

    for c in wsend:
        c.wait_recv()
    for b in range(3):
        whole = jnp.concatenate(
            [RCVW[:, b * g.NJ + j].astype(f32).reshape(C, LANES) for j in range(g.NJ)], axis=1
        )
        W1[b] = whole[:, : g.KW].astype(bf16)
        for a in range(3):
            WA[a, b] = whole[:, a * 3 * C : (a + 1) * 3 * C].astype(bf16)
        if b == 0:
            end = whole[:, g.KP - LANES :]
            own = jnp.logical_and(lane >= edge, lane < edge + 3)
            bcol = jnp.sum(jnp.where(own, end, 0.0), axis=1, keepdims=True)

    def conv(w, x):
        acc = None
        for b in range(3):
            part = jnp.dot(w[b], x[:, pl.ds(b * LANES, R * LANES)], preferred_element_type=f32)
            acc = part if acc is None else acc + part
        return acc

    def third(a):
        acc = None
        for b in range(3):
            x = XL[pl.ds(a * 3 * C, 3 * C), pl.ds(b * LANES, R * LANES)]
            part = jnp.dot(WA[a, b], x, preferred_element_type=f32)
            acc = part if acc is None else acc + part
        return acc

    PRE[...] = third(1)
    for n, ok in enumerate((s < N - 1, s > 0)):
        @pl.when(ok)
        def _(n=n):
            for c in halo[n]:
                c.wait_recv()

    spread(lambda i: HV[0, :, i], XL, 0)
    spread(lambda i: HV[1, :, i], XL, 2)

    PRE[...] = PRE[...] + third(0) + third(2)

    for c in usend:
        c.wait_recv()
    dsum = jnp.zeros((C, LANES), f32)
    for j in range(R):
        p = PRE[:, pl.ds(j * LANES, LANES)] + bcol
        e = jnp.exp(-jnp.abs(p))
        soft = jnp.maximum(p, 0.0) + jnp.log(1.0 + e)
        gate = jnp.where(p >= 0.0, 1.0, e) / (1.0 + e)
        act = leakage * p + (1.0 - leakage) * soft
        AIS[:, 0, j] = act.reshape(Pn, SHARE, LANES).astype(bf16)
        u = RCVU[:, j].astype(f32).reshape(C, LANES)
        d = (u * (leakage + (1.0 - leakage) * gate)).astype(bf16)
        DX[1, 1 + j] = d
        DB[:, pl.ds(j * LANES, LANES)] = d
        dsum = dsum + d.astype(f32)

    dcol = jnp.sum(dsum, axis=1, keepdims=True)
    gsend = []
    for b in range(3):
        GT[b, :, pl.ds(0, g.KW)] = lax.dot_general(
            DB[...], XL[:, pl.ds(b * LANES, R * LANES)],
            (((1,), (1,)), ((), ())), preferred_element_type=f32,
        )
        cur = GT[b, :, last]
        cur = jnp.where(lane < edge, cur, 0.0)
        if b == 0:
            cur = jnp.where(lane == edge, dcol, cur)
        GT[b, :, last] = cur
        for to in range(Pn):
            GS[b, to] = GT[b, pl.ds(SHARE * to, SHARE), :].astype(GS.dtype)
        sent = []
        for k in sorted(range(1, Pn), key=nearness, reverse=True):
            to = chan_peer(k)
            c = copy(GS.at[b, to], GR.at[b, r], g_s.at[b, k], g_r.at[b, k], s, to)
            start(c)
            sent.append(c)
        gsend.append(sent)
        GR[b, r] = GS[b, r]

    dcopies = []
    for e, (ds, dr) in enumerate(around):
        if dr == 0:
            src, dst = DX.at[1, pl.ds(1, R)], DX.at[1 - ds, pl.ds(1, R)]
        elif dr < 0:
            src, dst = DX.at[1, 1], DX.at[1 - ds, R + 1]
        else:
            src, dst = DX.at[1, R], DX.at[1 - ds, 0]
        c = copy(src, dst, d_s.at[e], d_r.at[e], s + ds, r + dr)
        pl.when(inside(ds, dr))(c.start)
        pending.append((inside(ds, dr), c))
        dcopies.append((inside(-ds, -dr), c))

    for b in range(3):
        whole = W1[2 - b].astype(f32).T
        blocks = []
        for a in range(3):
            for c_ in range(3):
                at = ((2 - a) * 3 + (2 - c_)) * C
                blocks.append(whole[at : at + C])
        W2[b] = jnp.concatenate(blocks, axis=1).astype(bf16)

    for b in range(3):
        for c in gsend[b]:
            c.wait_recv()
        acc = GR[b, 0].astype(f32)
        for q in range(1, Pn):
            acc = acc + GR[b, q].astype(f32)
        for j in range(g.NJ):
            t = b * g.NJ + j
            SB[t // g.T, t % g.T] = acc[:, j * LANES : (j + 1) * LANES]
    for t in range(3 * g.NJ, M * g.T):
        SB[t // g.T, t % g.T] = jnp.zeros(tile, f32)
    q1send = []
    for k in range(1, M):
        m, to_s = group_peer(k)
        c = copy(SB.at[m], Q1.at[member], q1_s.at[k], q1_r.at[k], to_s, r)
        start(c)
        q1send.append(c)
    Q1[member] = SB[member]

    for ok, c in dcopies:
        pl.when(ok)(c.wait_recv)
    for a in range(3):
        spread(lambda i, a=a: DX[a, i], DL, a)
    for c in q1send:
        c.wait_recv()
    acc = Q1[0]
    for m in range(1, M):
        acc = acc + Q1[m]
    Q2[block] = acc.astype(bf16)
    heard(1)
    early = len(pending)
    q2send = []
    for k in sorted(range(1, B), key=lambda k: -min(k, B - k)):
        c = copy(Q2.at[block], Q2.at[block], q2_s.at[k], q2_r.at[k], block_peer(k), r)
        start(c)
        q2send.append(c)
    PRE[...] = conv(W2, DL)
    for j in range(R):
        v = PRE[:, pl.ds(j * LANES, LANES)]
        AIS[:, 1, j] = v.reshape(Pn, SHARE, LANES).astype(bf16)
    isend = []
    for k in range(1, Pn):
        to = chan_peer(k)
        c = copy(AIS.at[to], AIR.at[r], i_s.at[k], i_r.at[k], s, to)
        start(c)
        isend.append(c)
    AIR[r] = AIS[r]
    sent_all(pending[:early])
    del pending[:early]

    for c in q2send:
        c.wait_recv()
    acc = Q2[0].astype(f32)
    for m in range(1, B):
        acc = acc + Q2[m].astype(f32)
    FIN[member] = acc * g.factor
    q3send = []
    for k in range(1, M):
        c = copy(FIN.at[member], FIN.at[member], q3_s.at[k], q3_r.at[k], group_peer(k)[1], r)
        start(c)
        q3send.append(c)
    for c in isend:
        c.wait_recv()
    for n, out in enumerate((act_o, ig_o)):
        TALL[n] = AIR[:, n].astype(f32).reshape(g.H * SHARE, LANES)
        for q in range(SHARE):
            out[q] = TALL[n, pl.ds(q, g.H, stride=SHARE), :].astype(bf16)
    for c in q3send:
        c.wait_recv()
    for a in range(3):
        for b in range(3):
            for c_ in range(3):
                at = (a * 3 + c_) * C
                t = b * g.NJ + at // LANES
                off = at % LANES
                wg_o[(a * 3 + b) * 3 + c_] = FIN[t // g.T, t % g.T][:, off : off + C]
    t = g.NJ - 1
    sums = FIN[t // g.T, t % g.T][:, edge : edge + 1]
    spot = lax.broadcasted_iota(jnp.int32, tile, 0) == lax.broadcasted_iota(jnp.int32, tile, 1)
    bg_o[...] = jnp.sum(jnp.where(spot, sums, 0.0), axis=0, keepdims=True)[:, :SHARE]

    sent_all(pending)


def deliver(act, ig, wg, bg, act_o, ig_o, wg_o, bg_o, sems):
    pairs = ((act, act_o), (ig, ig_o), (wg, wg_o), (bg, bg_o))
    moves = [pltpu.make_async_copy(a, b, sems.at[n]) for n, (a, b) in enumerate(pairs)]
    for c in moves:
        c.start()
    for c in moves:
        c.wait()


def shards(g, volume, weight, bias, upstream):
    Pn, R, C, M, B = g.P, g.R, g.C, g.M, g.B
    vol, up = volume[:, 0], upstream[:, 0]
    wl = jnp.transpose(weight, (2, 3, 4, 0, 1)).reshape(27, SHARE, C)
    sds = jax.ShapeDtypeStruct
    hbm = pl.BlockSpec(memory_space=pltpu.HBM)
    rows = (R + 2) * LANES
    dma = pltpu.SemaphoreType.DMA
    V = pltpu.VMEM
    chan = [dma((Pn,)), dma((Pn,))]
    scratch = [
        V((2, SHARE, g.H, LANES), bf16),
        V((27, SHARE, C), bf16),
        pltpu.SMEM((1, SHARE), f32),
        V((2, SHARE * g.H, LANES), f32),
        V((Pn, R + 2, SHARE, LANES), bf16),
        V((Pn, R, SHARE, LANES), bf16),
        V((Pn, 3 * g.NJ, SHARE, LANES), bf16),
        V((Pn, R + 2, SHARE, LANES), bf16),
        V((Pn, R, SHARE, LANES), bf16),
        V((Pn, 3 * g.NJ, SHARE, LANES), bf16),
        V((2, Pn, R + 2, SHARE, LANES), bf16),
        V((9 * C, rows), bf16),
        V((3, R + 2, C, LANES), bf16),
        V((9 * C, rows), bf16),
        V((3, C, g.KW), bf16),
        V((3, 3, C, 3 * C), bf16),
        V((3, C, g.KW), bf16),
        V((C, R * LANES), f32),
        V((C, R * LANES), bf16),
        V((Pn, 2, R, SHARE, LANES), bf16),
        V((Pn, 2, R, SHARE, LANES), bf16),
        V((3, C, g.KP), f32),
        V((3, Pn, SHARE, g.KP), bf16),
        V((3, Pn, SHARE, g.KP), bf16),
        V((M, g.T, SHARE, LANES), f32),
        V((M, g.T, SHARE, LANES), f32),
        V((B, g.T, SHARE, LANES), bf16),
        V((M, g.T, SHARE, LANES), f32),
        dma((4,)),
        *chan, *chan, *chan,
        pltpu.SemaphoreType.REGULAR((2,)),
        dma((2, Pn)), dma((2, Pn)),
        dma((8,)), dma((8,)),
        *chan,
        dma((3, Pn)), dma((3, Pn)),
        dma((M,)), dma((M,)),
        dma((B,)), dma((B,)),
        dma((M,)), dma((M,)),
    ]
    act, ig, wg, bg = pl.pallas_call(
        functools.partial(kernel, g),
        out_shape=(
            sds((SHARE, g.H, LANES), bf16),
            sds((SHARE, g.H, LANES), bf16),
            sds((27, SHARE, C), f32),
            sds((1, SHARE), f32),
        ),
        in_specs=[hbm] * 4,
        out_specs=(pl.BlockSpec(memory_space=pltpu.VMEM),) * 4,
        scratch_shapes=scratch,
        compiler_params=pltpu.CompilerParams(
            collective_id=0, has_side_effects=True, vmem_limit_bytes=40 << 20
        ),
    )(*(pltpu.with_memory_space_constraint(x, pltpu.HBM) for x in (vol, up, wl, bias[None])))
    act, ig, wg, bg = pl.pallas_call(
        deliver,
        out_shape=(
            sds((SHARE, g.H, LANES), bf16),
            sds((SHARE, g.H, LANES), bf16),
            sds((27, SHARE, C), f32),
            sds((1, SHARE), f32),
        ),
        in_specs=[pl.BlockSpec(memory_space=pl.ANY)] * 4,
        out_specs=(hbm,) * 4,
        scratch_shapes=[dma((4,))],
        compiler_params=pltpu.CompilerParams(vmem_limit_bytes=1 << 20),
    )(act, ig, wg, bg)
    wgrad = jnp.transpose(wg.reshape(3, 3, 3, SHARE, C), (3, 4, 0, 1, 2))
    return act[:, None], ig[:, None], wgrad, bg[0]


def solution(mesh, rows=48, halves=2, blocks=8):
    planes, ranks = mesh.shape["space"], mesh.shape["chan"]
    factor = 1.0 / math.sqrt(planes * rows * LANES)
    g = Plan(planes, ranks, rows, halves, blocks, factor)
    field = P("chan", "space", None, None)
    filters = P("chan", None, None, None, None)
    return jax.shard_map(
        functools.partial(shards, g),
        mesh=mesh,
        in_specs=(field, filters, P("chan"), field),
        out_specs=(field, field, filters, P("chan")),
        check_vma=False,
    )
```

```python
import functools
import math

import jax
import jax.numpy as jnp
from jax import lax
from jax.experimental import pallas as pl
from jax.experimental.pallas import tpu as pltpu
from jax.sharding import PartitionSpec as P

MESH = pl.DeviceIdType.MESH
f32 = jnp.float32
bf16 = jnp.bfloat16
leakage = 0.1
LANES = 128
SHARE = 8


class Plan:
    def __init__(self, planes, ranks, rows, halves, blocks, factor):
        self.N = planes
        self.P = ranks
        self.R = rows // ranks
        self.H = rows
        self.C = SHARE * ranks
        self.X = halves
        self.B = blocks
        self.U = planes // (halves * blocks)
        self.M = self.U * self.X
        self.KW = 9 * self.C
        self.NJ = self.KW // LANES + 1
        self.KP = self.NJ * LANES
        self.T = -(-3 * self.NJ // self.M)
        self.factor = factor


def kernel(
    g, vol, up, wl, bias,
    act_o, ig_o, wg_o, bg_o,
    RAW, RAWW, RAWB, TALL, SENDV, SENDU, SENDW, RCVV, RCVU, RCVW, HV, XL, DX, DL, W1, WA, W2, PRE, DB, AIS, AIR,
    GT, GS, GR, SB, Q1, Q2, FIN,
    l_s, v_s, v_r, w_s, w_r, u_s, u_r, far, p_s, p_r, d_s, d_r, i_s, i_r,
    g_s, g_r, q1_s, q1_r, q2_s, q2_r, q3_s, q3_r,
):
    N, Pn, R, C, M, B, U = g.N, g.P, g.R, g.C, g.M, g.B, g.U
    s = lax.axis_index("space")
    r = lax.axis_index("chan")
    span = B * U
    x_lo, within = s // span, s % span
    block, unit = within // U, within % U
    member = x_lo * U + unit
    pending = []

    def chan_peer(k):
        return lax.rem(r + k, Pn)

    def group_peer(k):
        m = lax.rem(member + k, M)
        return m, (m // U) * span + block * U + m % U

    def block_peer(k):
        b = lax.rem(block + k, B)
        return x_lo * span + b * U + unit

    def copy(src, dst, ssem, rsem, to_s, to_r):
        return pltpu.make_async_remote_copy(
            src_ref=src, dst_ref=dst, send_sem=ssem, recv_sem=rsem,
            device_id=(to_s, to_r), device_id_type=MESH,
        )

    def start(c):
        c.start()
        pending.append((None, c))

    def sent_all(copies):
        for ok, c in copies:
            if ok is None:
                c.wait_send()
            else:
                pl.when(ok)(c.wait_send)

    around = [(ds, dr) for ds in (-1, 0, 1) for dr in (-1, 0, 1) if (ds, dr) != (0, 0)]

    def inside(ds, dr):
        ok = None
        for here, step, end in ((s, ds, N), (r, dr, Pn)):
            if step:
                near = here > 0 if step < 0 else here < end - 1
                ok = near if ok is None else jnp.logical_and(ok, near)
        return ok

    barrier = pltpu.get_barrier_semaphore()

    def greet(to_s, to_r):
        pl.semaphore_signal(barrier, inc=1, device_id=(to_s, to_r), device_id_type=MESH)

    for k in range(1, Pn):
        greet(s, chan_peer(k))
    for k in range(1, M):
        greet(group_peer(k)[1], r)
    near = sorted({1, B - 1} - {0})
    for k in near:
        greet(block_peer(k), r)
    for ds, dr in around:
        pl.when(inside(ds, dr))(functools.partial(greet, s + ds, r + dr))
    wide_s = 1 + jnp.where(s > 0, 1, 0) + jnp.where(s < N - 1, 1, 0)
    wide_r = 1 + jnp.where(r > 0, 1, 0) + jnp.where(r < Pn - 1, 1, 0)

    V = R + 2
    loads = [
        pltpu.make_async_copy(vol, RAW.at[0], l_s.at[0]),
        pltpu.make_async_copy(up, RAW.at[1], l_s.at[1]),
        pltpu.make_async_copy(wl, RAWW, l_s.at[2]),
        pltpu.make_async_copy(bias, RAWB, l_s.at[3]),
    ]
    for c in loads:
        c.start()
    tile = (SHARE, LANES)
    edge = g.KW % LANES
    for c in loads:
        c.wait()
    sub = lax.broadcasted_iota(jnp.int32, (SHARE, g.KP - g.KW), 0)
    col = lax.broadcasted_iota(jnp.int32, (SHARE, g.KP - g.KW), 1)
    b0 = jnp.zeros((SHARE, g.KP - g.KW), f32)
    for q in range(SHARE):
        b0 = jnp.where(sub == q, RAWB[0, q], b0)
    hi = b0.astype(bf16).astype(f32)
    mid = (b0 - hi).astype(bf16).astype(f32)
    low = (b0 - hi - mid).astype(bf16).astype(f32)
    tail = jnp.where(col == 0, hi, jnp.where(col == 1, mid, jnp.where(col == 2, low, 0.0)))
    for b in range(3):
        taps = [RAWW[(a * 3 + b) * 3 + c_].astype(f32) for a in range(3) for c_ in range(3)]
        whole = jnp.concatenate(taps + [tail], axis=1)
        for j in range(g.NJ):
            part = whole[:, j * LANES : (j + 1) * LANES].astype(bf16)
            for to in range(Pn):
                SENDW[to, b * g.NJ + j] = part
    for n in range(2):
        TALL[n] = RAW[n].astype(f32).reshape(SHARE * g.H, LANES)
    zero_tile = jnp.zeros(tile, bf16)
    SENDV[0, 0] = zero_tile
    SENDV[Pn - 1, R + 1] = zero_tile
    for h in range(g.H):
        row = TALL[0, pl.ds(h, SHARE, stride=g.H), :].astype(bf16)
        for to in range(Pn):
            if 0 <= h + 1 - R * to < V:
                SENDV[to, h + 1 - R * to] = row
        SENDU[h // R, h % R] = TALL[1, pl.ds(h, SHARE, stride=g.H), :].astype(bf16)

    pl.semaphore_wait(barrier, (Pn - 1) + (M - 1) + len(near) + wide_s * wide_r - 1)

    reach = [1 << i for i in range(8) if 1 << i < B // 2]

    def relay(i):
        if i < len(reach):
            for k in sorted({reach[i], B - reach[i]}):
                pl.semaphore_signal(
                    far.at[i], inc=1, device_id=(block_peer(k), r), device_id_type=MESH
                )

    def heard(i):
        if i < len(reach):
            pl.semaphore_wait(far.at[i], len({reach[i], B - reach[i]}))

    relay(0)

    RCVV[r] = SENDV[r]

    def nearness(k):
        return k % 2, min(k, Pn - k)

    vsend, wsend = [], []
    for k in sorted(range(1, Pn), key=nearness, reverse=True):
        to = chan_peer(k)
        c = copy(SENDV.at[to], RCVV.at[r], v_s.at[k], v_r.at[k], s, to)
        start(c)
        vsend.append((k, c))
    for k in range(1, Pn):
        to = chan_peer(k)
        c = copy(SENDW.at[to], RCVW.at[r], w_s.at[k], w_r.at[k], s, to)
        start(c)
        wsend.append(c)
    RCVW[r] = SENDW[r]
    RCVU[r] = SENDU[r]

    def clear(ref, a):
        def body(i, _):
            ref[a, i] = jnp.zeros(ref.shape[2:], bf16)
            return 0
        lax.fori_loop(0, R + 2, body, 0)

    def clear_rows(ref, a):
        def body(i, _):
            ref[a, i] = jnp.zeros(ref.shape[2:], bf16)
            return 0
        lax.fori_loop(0, Pn, body, 0)

    @pl.when(s == 0)
    def _():
        clear_rows(HV, 0)
        clear(DX, 0)

    @pl.when(s == N - 1)
    def _():
        clear_rows(HV, 1)
        clear(DX, 2)

    @pl.when(r == 0)
    def _():
        for a in range(3):
            DX[a, 0] = jnp.zeros((C, LANES), bf16)

    @pl.when(r == Pn - 1)
    def _():
        for a in range(3):
            DX[a, R + 1] = jnp.zeros((C, LANES), bf16)

    halo = [[], []]

    def forward(k):
        q = lax.rem(r + Pn - k, Pn)
        for n, (ok, to) in enumerate(((s > 0, s - 1), (s < N - 1, s + 1))):
            c = copy(RCVV.at[q], HV.at[1 - n, q], p_s.at[n, k], p_r.at[n, k], to, r)
            pl.when(ok)(c.start)
            pending.append((ok, c))
            halo[n].append(c)

    forward(0)
    for k, c in sorted(vsend, key=lambda kc: nearness(kc[0])):
        c.wait_recv()
        forward(k)

    usend = []
    for k in sorted(range(1, Pn), key=nearness, reverse=True):
        to = chan_peer(k)
        c = copy(SENDU.at[to], RCVU.at[r], u_s.at[k], u_r.at[k], s, to)
        start(c)
        usend.append(c)

    heard(0)
    relay(1)
    last = pl.ds((g.NJ - 1) * LANES, LANES)
    lane = lax.broadcasted_iota(jnp.int32, (C, LANES), 1)

    def spread(row, out, a):
        for i in range(R + 2):
            x = row(i).astype(f32).reshape(C, LANES)
            at = pl.ds(i * LANES, LANES)
            before = jnp.where(lane == 0, 0.0, pltpu.roll(x, 1, 1))
            after = jnp.where(lane == LANES - 1, 0.0, pltpu.roll(x, LANES - 1, 1))
            out[pl.ds((3 * a) * C, C), at] = before.astype(bf16)
            out[pl.ds((3 * a + 1) * C, C), at] = x.astype(bf16)
            out[pl.ds((3 * a + 2) * C, C), at] = after.astype(bf16)

    spread(lambda i: RCVV[:, i], XL, 1)

    for c in wsend:
        c.wait_recv()
    for b in range(3):
        whole = jnp.concatenate(
            [RCVW[:, b * g.NJ + j].astype(f32).reshape(C, LANES) for j in range(g.NJ)], axis=1
        )
        W1[b] = whole[:, : g.KW].astype(bf16)
        for a in range(3):
            WA[a, b] = whole[:, a * 3 * C : (a + 1) * 3 * C].astype(bf16)
        if b == 0:
            end = whole[:, g.KP - LANES :]
            own = jnp.logical_and(lane >= edge, lane < edge + 3)
            bcol = jnp.sum(jnp.where(own, end, 0.0), axis=1, keepdims=True)

    def conv(w, x):
        acc = None
        for b in range(3):
            part = jnp.dot(w[b], x[:, pl.ds(b * LANES, R * LANES)], preferred_element_type=f32)
            acc = part if acc is None else acc + part
        return acc

    def third(a):
        acc = None
        for b in range(3):
            x = XL[pl.ds(a * 3 * C, 3 * C), pl.ds(b * LANES, R * LANES)]
            part = jnp.dot(WA[a, b], x, preferred_element_type=f32)
            acc = part if acc is None else acc + part
        return acc

    PRE[...] = third(1)
    for n, ok in enumerate((s < N - 1, s > 0)):
        @pl.when(ok)
        def _(n=n):
            for c in halo[n]:
                c.wait_recv()

    spread(lambda i: HV[0, :, i], XL, 0)
    spread(lambda i: HV[1, :, i], XL, 2)

    PRE[...] = PRE[...] + third(0) + third(2)

    for c in usend:
        c.wait_recv()
    dsum = jnp.zeros((C, LANES), f32)
    for j in range(R):
        p = PRE[:, pl.ds(j * LANES, LANES)] + bcol
        e = jnp.exp(-jnp.abs(p))
        gate = jnp.where(p >= 0.0, 1.0, e) / (1.0 + e)
        u = RCVU[:, j].astype(f32).reshape(C, LANES)
        d = (u * (leakage + (1.0 - leakage) * gate)).astype(bf16)
        DX[1, 1 + j] = d
        DB[:, pl.ds(j * LANES, LANES)] = d
        dsum = dsum + d.astype(f32)

    dcol = jnp.sum(dsum, axis=1, keepdims=True)
    gsend = []
    for b in range(3):
        GT[b, :, pl.ds(0, g.KW)] = lax.dot_general(
            DB[...], XL[:, pl.ds(b * LANES, R * LANES)],
            (((1,), (1,)), ((), ())), preferred_element_type=f32,
        )
        cur = GT[b, :, last]
        cur = jnp.where(lane < edge, cur, 0.0)
        if b == 0:
            cur = jnp.where(lane == edge, dcol, cur)
        GT[b, :, last] = cur
        for to in range(Pn):
            GS[b, to] = GT[b, pl.ds(SHARE * to, SHARE), :].astype(GS.dtype)
        sent = []
        for k in sorted(range(1, Pn), key=nearness, reverse=True):
            to = chan_peer(k)
            c = copy(GS.at[b, to], GR.at[b, r], g_s.at[b, k], g_r.at[b, k], s, to)
            start(c)
            sent.append(c)
        gsend.append(sent)
        GR[b, r] = GS[b, r]

    dcopies = []
    for e, (ds, dr) in enumerate(around):
        if dr == 0:
            src, dst = DX.at[1, pl.ds(1, R)], DX.at[1 - ds, pl.ds(1, R)]
        elif dr < 0:
            src, dst = DX.at[1, 1], DX.at[1 - ds, R + 1]
        else:
            src, dst = DX.at[1, R], DX.at[1 - ds, 0]
        c = copy(src, dst, d_s.at[e], d_r.at[e], s + ds, r + dr)
        pl.when(inside(ds, dr))(c.start)
        pending.append((inside(ds, dr), c))
        dcopies.append((inside(-ds, -dr), c))

    for j in range(R):
        p = PRE[:, pl.ds(j * LANES, LANES)] + bcol
        soft = jnp.maximum(p, 0.0) + jnp.log(1.0 + jnp.exp(-jnp.abs(p)))
        act = leakage * p + (1.0 - leakage) * soft
        AIS[:, 0, j] = act.reshape(Pn, SHARE, LANES).astype(bf16)

    for b in range(3):
        whole = W1[2 - b].astype(f32).T
        blocks = []
        for a in range(3):
            for c_ in range(3):
                at = ((2 - a) * 3 + (2 - c_)) * C
                blocks.append(whole[at : at + C])
        W2[b] = jnp.concatenate(blocks, axis=1).astype(bf16)

    for b in range(3):
        for c in gsend[b]:
            c.wait_recv()
        acc = GR[b, 0].astype(f32)
        for q in range(1, Pn):
            acc = acc + GR[b, q].astype(f32)
        for j in range(g.NJ):
            t = b * g.NJ + j
            SB[t // g.T, t % g.T] = acc[:, j * LANES : (j + 1) * LANES]
    for t in range(3 * g.NJ, M * g.T):
        SB[t // g.T, t % g.T] = jnp.zeros(tile, f32)
    q1send = []
    for k in range(1, M):
        m, to_s = group_peer(k)
        c = copy(SB.at[m], Q1.at[member], q1_s.at[k], q1_r.at[k], to_s, r)
        start(c)
        q1send.append(c)
    Q1[member] = SB[member]

    for ok, c in dcopies:
        pl.when(ok)(c.wait_recv)
    for a in range(3):
        spread(lambda i, a=a: DX[a, i], DL, a)
    for c in q1send:
        c.wait_recv()
    acc = Q1[0]
    for m in range(1, M):
        acc = acc + Q1[m]
    Q2[block] = acc.astype(bf16)
    heard(1)
    early = len(pending)
    q2send = []
    for k in sorted(range(1, B), key=lambda k: -min(k, B - k)):
        c = copy(Q2.at[block], Q2.at[block], q2_s.at[k], q2_r.at[k], block_peer(k), r)
        start(c)
        q2send.append(c)
    PRE[...] = conv(W2, DL)
    for j in range(R):
        v = PRE[:, pl.ds(j * LANES, LANES)]
        AIS[:, 1, j] = v.reshape(Pn, SHARE, LANES).astype(bf16)
    isend = []
    for k in range(1, Pn):
        to = chan_peer(k)
        c = copy(AIS.at[to], AIR.at[r], i_s.at[k], i_r.at[k], s, to)
        start(c)
        isend.append(c)
    AIR[r] = AIS[r]
    sent_all(pending[:early])
    del pending[:early]

    for c in q2send:
        c.wait_recv()
    acc = Q2[0].astype(f32)
    for m in range(1, B):
        acc = acc + Q2[m].astype(f32)
    FIN[member] = acc * g.factor
    q3send = []
    for k in range(1, M):
        c = copy(FIN.at[member], FIN.at[member], q3_s.at[k], q3_r.at[k], group_peer(k)[1], r)
        start(c)
        q3send.append(c)
    for c in isend:
        c.wait_recv()
    for n, out in enumerate((act_o, ig_o)):
        TALL[n] = AIR[:, n].astype(f32).reshape(g.H * SHARE, LANES)
        for q in range(SHARE):
            out[q] = TALL[n, pl.ds(q, g.H, stride=SHARE), :].astype(bf16)
    for c in q3send:
        c.wait_recv()
    for a in range(3):
        for b in range(3):
            for c_ in range(3):
                at = (a * 3 + c_) * C
                t = b * g.NJ + at // LANES
                off = at % LANES
                wg_o[(a * 3 + b) * 3 + c_] = FIN[t // g.T, t % g.T][:, off : off + C]
    t = g.NJ - 1
    sums = FIN[t // g.T, t % g.T][:, edge : edge + 1]
    spot = lax.broadcasted_iota(jnp.int32, tile, 0) == lax.broadcasted_iota(jnp.int32, tile, 1)
    bg_o[...] = jnp.sum(jnp.where(spot, sums, 0.0), axis=0, keepdims=True)[:, :SHARE]

    sent_all(pending)


def deliver(act, ig, wg, bg, act_o, ig_o, wg_o, bg_o, sems):
    pairs = ((act, act_o), (ig, ig_o), (wg, wg_o), (bg, bg_o))
    moves = [pltpu.make_async_copy(a, b, sems.at[n]) for n, (a, b) in enumerate(pairs)]
    for c in moves:
        c.start()
    for c in moves:
        c.wait()


def shards(g, volume, weight, bias, upstream):
    Pn, R, C, M, B = g.P, g.R, g.C, g.M, g.B
    vol, up = volume[:, 0], upstream[:, 0]
    wl = jnp.transpose(weight, (2, 3, 4, 0, 1)).reshape(27, SHARE, C)
    sds = jax.ShapeDtypeStruct
    hbm = pl.BlockSpec(memory_space=pltpu.HBM)
    rows = (R + 2) * LANES
    dma = pltpu.SemaphoreType.DMA
    V = pltpu.VMEM
    chan = [dma((Pn,)), dma((Pn,))]
    scratch = [
        V((2, SHARE, g.H, LANES), bf16),
        V((27, SHARE, C), bf16),
        pltpu.SMEM((1, SHARE), f32),
        V((2, SHARE * g.H, LANES), f32),
        V((Pn, R + 2, SHARE, LANES), bf16),
        V((Pn, R, SHARE, LANES), bf16),
        V((Pn, 3 * g.NJ, SHARE, LANES), bf16),
        V((Pn, R + 2, SHARE, LANES), bf16),
        V((Pn, R, SHARE, LANES), bf16),
        V((Pn, 3 * g.NJ, SHARE, LANES), bf16),
        V((2, Pn, R + 2, SHARE, LANES), bf16),
        V((9 * C, rows), bf16),
        V((3, R + 2, C, LANES), bf16),
        V((9 * C, rows), bf16),
        V((3, C, g.KW), bf16),
        V((3, 3, C, 3 * C), bf16),
        V((3, C, g.KW), bf16),
        V((C, R * LANES), f32),
        V((C, R * LANES), bf16),
        V((Pn, 2, R, SHARE, LANES), bf16),
        V((Pn, 2, R, SHARE, LANES), bf16),
        V((3, C, g.KP), f32),
        V((3, Pn, SHARE, g.KP), bf16),
        V((3, Pn, SHARE, g.KP), bf16),
        V((M, g.T, SHARE, LANES), f32),
        V((M, g.T, SHARE, LANES), f32),
        V((B, g.T, SHARE, LANES), bf16),
        V((M, g.T, SHARE, LANES), f32),
        dma((4,)),
        *chan, *chan, *chan,
        pltpu.SemaphoreType.REGULAR((2,)),
        dma((2, Pn)), dma((2, Pn)),
        dma((8,)), dma((8,)),
        *chan,
        dma((3, Pn)), dma((3, Pn)),
        dma((M,)), dma((M,)),
        dma((B,)), dma((B,)),
        dma((M,)), dma((M,)),
    ]
    act, ig, wg, bg = pl.pallas_call(
        functools.partial(kernel, g),
        out_shape=(
            sds((SHARE, g.H, LANES), bf16),
            sds((SHARE, g.H, LANES), bf16),
            sds((27, SHARE, C), f32),
            sds((1, SHARE), f32),
        ),
        in_specs=[hbm] * 4,
        out_specs=(pl.BlockSpec(memory_space=pltpu.VMEM),) * 4,
        scratch_shapes=scratch,
        compiler_params=pltpu.CompilerParams(
            collective_id=0, has_side_effects=True, vmem_limit_bytes=40 << 20
        ),
    )(*(pltpu.with_memory_space_constraint(x, pltpu.HBM) for x in (vol, up, wl, bias[None])))
    act, ig, wg, bg = pl.pallas_call(
        deliver,
        out_shape=(
            sds((SHARE, g.H, LANES), bf16),
            sds((SHARE, g.H, LANES), bf16),
            sds((27, SHARE, C), f32),
            sds((1, SHARE), f32),
        ),
        in_specs=[pl.BlockSpec(memory_space=pl.ANY)] * 4,
        out_specs=(hbm,) * 4,
        scratch_shapes=[dma((4,))],
        compiler_params=pltpu.CompilerParams(vmem_limit_bytes=1 << 20),
    )(act, ig, wg, bg)
    wgrad = jnp.transpose(wg.reshape(3, 3, 3, SHARE, C), (3, 4, 0, 1, 2))
    return act[:, None], ig[:, None], wgrad, bg[0]


def solution(mesh, rows=48, halves=2, blocks=8):
    planes, ranks = mesh.shape["space"], mesh.shape["chan"]
    factor = 1.0 / math.sqrt(planes * rows * LANES)
    g = Plan(planes, ranks, rows, halves, blocks, factor)
    field = P("chan", "space", None, None)
    filters = P("chan", None, None, None, None)
    return jax.shard_map(
        functools.partial(shards, g),
        mesh=mesh,
        in_specs=(field, filters, P("chan"), field),
        out_specs=(field, field, filters, P("chan")),
        check_vma=False,
    )
```

```python
import functools
import math

import jax
import jax.numpy as jnp
from jax import lax
from jax.experimental import pallas as pl
from jax.experimental.pallas import tpu as pltpu
from jax.sharding import PartitionSpec as P

MESH = pl.DeviceIdType.MESH
f32 = jnp.float32
bf16 = jnp.bfloat16
leakage = 0.1
LANES = 128
SHARE = 8


class Plan:
    def __init__(self, planes, ranks, rows, halves, blocks, factor):
        self.N = planes
        self.P = ranks
        self.R = rows // ranks
        self.H = rows
        self.C = SHARE * ranks
        self.X = halves
        self.B = blocks
        self.U = planes // (halves * blocks)
        self.M = self.U * self.X
        self.KW = 9 * self.C
        self.NJ = self.KW // LANES + 1
        self.KP = self.NJ * LANES
        self.T = -(-3 * self.NJ // self.M)
        self.factor = factor


def kernel(
    g, vol, up, wl, bias,
    act_o, ig_o, wg_o, bg_o,
    RAW, RAWW, RAWB, TALL, SENDV, SENDU, SENDW, RCVV, RCVU, RCVW, HV, XL, DX, DL, W1, WA, W2, PRE, DB, AIS, AIR,
    GT, GS, GR, SB, Q1, Q2, FIN,
    l_s, v_s, v_r, w_s, w_r, u_s, u_r, far, p_s, p_r, d_s, d_r, i_s, i_r,
    g_s, g_r, q1_s, q1_r, q2_s, q2_r, q3_s, q3_r,
):
    N, Pn, R, C, M, B, U = g.N, g.P, g.R, g.C, g.M, g.B, g.U
    s = lax.axis_index("space")
    r = lax.axis_index("chan")
    span = B * U
    x_lo, within = s // span, s % span
    block, unit = within // U, within % U
    member = x_lo * U + unit
    pending = []

    def chan_peer(k):
        return lax.rem(r + k, Pn)

    def group_peer(k):
        m = lax.rem(member + k, M)
        return m, (m // U) * span + block * U + m % U

    def block_peer(k):
        b = lax.rem(block + k, B)
        return x_lo * span + b * U + unit

    def copy(src, dst, ssem, rsem, to_s, to_r):
        return pltpu.make_async_remote_copy(
            src_ref=src, dst_ref=dst, send_sem=ssem, recv_sem=rsem,
            device_id=(to_s, to_r), device_id_type=MESH,
        )

    def start(c):
        c.start()
        pending.append((None, c))

    def sent_all(copies):
        for ok, c in copies:
            if ok is None:
                c.wait_send()
            else:
                pl.when(ok)(c.wait_send)

    around = [(ds, dr) for ds in (-1, 0, 1) for dr in (-1, 0, 1) if (ds, dr) != (0, 0)]

    def inside(ds, dr):
        ok = None
        for here, step, end in ((s, ds, N), (r, dr, Pn)):
            if step:
                near = here > 0 if step < 0 else here < end - 1
                ok = near if ok is None else jnp.logical_and(ok, near)
        return ok

    barrier = pltpu.get_barrier_semaphore()

    def greet(to_s, to_r):
        pl.semaphore_signal(barrier, inc=1, device_id=(to_s, to_r), device_id_type=MESH)

    for k in range(1, Pn):
        greet(s, chan_peer(k))
    for k in range(1, M):
        greet(group_peer(k)[1], r)
    near = sorted({1, B - 1} - {0})
    for k in near:
        greet(block_peer(k), r)
    for ds, dr in around:
        pl.when(inside(ds, dr))(functools.partial(greet, s + ds, r + dr))
    wide_s = 1 + jnp.where(s > 0, 1, 0) + jnp.where(s < N - 1, 1, 0)
    wide_r = 1 + jnp.where(r > 0, 1, 0) + jnp.where(r < Pn - 1, 1, 0)

    V = R + 2
    loads = [
        pltpu.make_async_copy(vol, RAW.at[0], l_s.at[0]),
        pltpu.make_async_copy(up, RAW.at[1], l_s.at[1]),
        pltpu.make_async_copy(wl, RAWW, l_s.at[2]),
        pltpu.make_async_copy(bias, RAWB, l_s.at[3]),
    ]
    for c in loads:
        c.start()
    tile = (SHARE, LANES)
    edge = g.KW % LANES
    for c in loads:
        c.wait()
    sub = lax.broadcasted_iota(jnp.int32, (SHARE, g.KP - g.KW), 0)
    col = lax.broadcasted_iota(jnp.int32, (SHARE, g.KP - g.KW), 1)
    b0 = jnp.zeros((SHARE, g.KP - g.KW), f32)
    for q in range(SHARE):
        b0 = jnp.where(sub == q, RAWB[0, q], b0)
    hi = b0.astype(bf16).astype(f32)
    mid = (b0 - hi).astype(bf16).astype(f32)
    low = (b0 - hi - mid).astype(bf16).astype(f32)
    tail = jnp.where(col == 0, hi, jnp.where(col == 1, mid, jnp.where(col == 2, low, 0.0)))
    for b in range(3):
        taps = [RAWW[(a * 3 + b) * 3 + c_].astype(f32) for a in range(3) for c_ in range(3)]
        whole = jnp.concatenate(taps + [tail], axis=1)
        for j in range(g.NJ):
            part = whole[:, j * LANES : (j + 1) * LANES].astype(bf16)
            for to in range(Pn):
                SENDW[to, b * g.NJ + j] = part
    for n in range(2):
        TALL[n] = RAW[n].astype(f32).reshape(SHARE * g.H, LANES)
    zero_tile = jnp.zeros(tile, bf16)
    SENDV[0, 0] = zero_tile
    SENDV[Pn - 1, R + 1] = zero_tile
    for h in range(g.H):
        row = TALL[0, pl.ds(h, SHARE, stride=g.H), :].astype(bf16)
        for to in range(Pn):
            if 0 <= h + 1 - R * to < V:
                SENDV[to, h + 1 - R * to] = row
        SENDU[h // R, h % R] = TALL[1, pl.ds(h, SHARE, stride=g.H), :].astype(bf16)

    pl.semaphore_wait(barrier, (Pn - 1) + (M - 1) + len(near) + wide_s * wide_r - 1)

    reach = [1 << i for i in range(8) if 1 << i < B // 2]

    def relay(i):
        if i < len(reach):
            for k in sorted({reach[i], B - reach[i]}):
                pl.semaphore_signal(
                    far.at[i], inc=1, device_id=(block_peer(k), r), device_id_type=MESH
                )

    def heard(i):
        if i < len(reach):
            pl.semaphore_wait(far.at[i], len({reach[i], B - reach[i]}))

    relay(0)

    RCVV[r] = SENDV[r]

    def nearness(k):
        return k % 2, min(k, Pn - k)

    vsend, wsend = [], []
    for k in sorted(range(1, Pn), key=nearness, reverse=True):
        to = chan_peer(k)
        c = copy(SENDV.at[to], RCVV.at[r], v_s.at[k], v_r.at[k], s, to)
        start(c)
        vsend.append((k, c))
    for k in range(1, Pn):
        to = chan_peer(k)
        c = copy(SENDW.at[to], RCVW.at[r], w_s.at[k], w_r.at[k], s, to)
        start(c)
        wsend.append(c)
    RCVW[r] = SENDW[r]
    RCVU[r] = SENDU[r]

    def clear(ref, a):
        def body(i, _):
            ref[a, i] = jnp.zeros(ref.shape[2:], bf16)
            return 0
        lax.fori_loop(0, R + 2, body, 0)

    def clear_rows(ref, a):
        def body(i, _):
            ref[a, i] = jnp.zeros(ref.shape[2:], bf16)
            return 0
        lax.fori_loop(0, Pn, body, 0)

    @pl.when(s == 0)
    def _():
        clear_rows(HV, 0)
        clear(DX, 0)

    @pl.when(s == N - 1)
    def _():
        clear_rows(HV, 1)
        clear(DX, 2)

    @pl.when(r == 0)
    def _():
        for a in range(3):
            DX[a, 0] = jnp.zeros((C, LANES), bf16)

    @pl.when(r == Pn - 1)
    def _():
        for a in range(3):
            DX[a, R + 1] = jnp.zeros((C, LANES), bf16)

    halo = [[], []]

    def forward(k):
        q = lax.rem(r + Pn - k, Pn)
        for n, (ok, to) in enumerate(((s > 0, s - 1), (s < N - 1, s + 1))):
            c = copy(RCVV.at[q], HV.at[1 - n, q], p_s.at[n, k], p_r.at[n, k], to, r)
            pl.when(ok)(c.start)
            pending.append((ok, c))
            halo[n].append(c)

    forward(0)
    for k, c in sorted(vsend, key=lambda kc: nearness(kc[0])):
        c.wait_recv()
        forward(k)

    usend = []
    for k in sorted(range(1, Pn), key=nearness, reverse=True):
        to = chan_peer(k)
        c = copy(SENDU.at[to], RCVU.at[r], u_s.at[k], u_r.at[k], s, to)
        start(c)
        usend.append(c)

    heard(0)
    relay(1)
    last = pl.ds((g.NJ - 1) * LANES, LANES)
    lane = lax.broadcasted_iota(jnp.int32, (C, LANES), 1)

    def spread(row, out, a):
        for i in range(R + 2):
            x = row(i).astype(f32).reshape(C, LANES)
            at = pl.ds(i * LANES, LANES)
            before = jnp.where(lane == 0, 0.0, pltpu.roll(x, 1, 1))
            after = jnp.where(lane == LANES - 1, 0.0, pltpu.roll(x, LANES - 1, 1))
            out[pl.ds((3 * a) * C, C), at] = before.astype(bf16)
            out[pl.ds((3 * a + 1) * C, C), at] = x.astype(bf16)
            out[pl.ds((3 * a + 2) * C, C), at] = after.astype(bf16)

    spread(lambda i: RCVV[:, i], XL, 1)

    for c in wsend:
        c.wait_recv()
    for b in range(3):
        whole = jnp.concatenate(
            [RCVW[:, b * g.NJ + j].astype(f32).reshape(C, LANES) for j in range(g.NJ)], axis=1
        )
        W1[b] = whole[:, : g.KW].astype(bf16)
        for a in range(3):
            WA[a, b] = whole[:, a * 3 * C : (a + 1) * 3 * C].astype(bf16)
        if b == 0:
            end = whole[:, g.KP - LANES :]
            own = jnp.logical_and(lane >= edge, lane < edge + 3)
            bcol = jnp.sum(jnp.where(own, end, 0.0), axis=1, keepdims=True)

    def conv(w, x):
        acc = None
        for b in range(3):
            part = jnp.dot(w[b], x[:, pl.ds(b * LANES, R * LANES)], preferred_element_type=f32)
            acc = part if acc is None else acc + part
        return acc

    def third(a):
        acc = None
        for b in range(3):
            x = XL[pl.ds(a * 3 * C, 3 * C), pl.ds(b * LANES, R * LANES)]
            part = jnp.dot(WA[a, b], x, preferred_element_type=f32)
            acc = part if acc is None else acc + part
        return acc

    PRE[...] = third(1)
    for n, ok in enumerate((s < N - 1, s > 0)):
        @pl.when(ok)
        def _(n=n):
            for c in halo[n]:
                c.wait_recv()

    spread(lambda i: HV[0, :, i], XL, 0)
    spread(lambda i: HV[1, :, i], XL, 2)

    PRE[...] = PRE[...] + third(0) + third(2)

    for c in usend:
        c.wait_recv()
    dsum = jnp.zeros((C, LANES), f32)
    for j in range(R):
        p = PRE[:, pl.ds(j * LANES, LANES)] + bcol
        e = jnp.exp(-jnp.abs(p))
        gate = jnp.where(p >= 0.0, 1.0, e) / (1.0 + e)
        u = RCVU[:, j].astype(f32).reshape(C, LANES)
        d = (u * (leakage + (1.0 - leakage) * gate)).astype(bf16)
        DX[1, 1 + j] = d
        DB[:, pl.ds(j * LANES, LANES)] = d
        dsum = dsum + d.astype(f32)

    dcol = jnp.sum(dsum, axis=1, keepdims=True)
    gsend = []
    for b in range(3):
        GT[b, :, pl.ds(0, g.KW)] = lax.dot_general(
            DB[...], XL[:, pl.ds(b * LANES, R * LANES)],
            (((1,), (1,)), ((), ())), preferred_element_type=f32,
        )
        cur = GT[b, :, last]
        cur = jnp.where(lane < edge, cur, 0.0)
        if b == 0:
            cur = jnp.where(lane == edge, dcol, cur)
        GT[b, :, last] = cur
        for to in range(Pn):
            GS[b, to] = GT[b, pl.ds(SHARE * to, SHARE), :].astype(GS.dtype)
        sent = []
        for k in sorted(range(1, Pn), key=nearness, reverse=True):
            to = chan_peer(k)
            c = copy(GS.at[b, to], GR.at[b, r], g_s.at[b, k], g_r.at[b, k], s, to)
            start(c)
            sent.append(c)
        gsend.append(sent)
        GR[b, r] = GS[b, r]

    dcopies = []
    for e, (ds, dr) in enumerate(around):
        if dr == 0:
            src, dst = DX.at[1, pl.ds(1, R)], DX.at[1 - ds, pl.ds(1, R)]
        elif dr < 0:
            src, dst = DX.at[1, 1], DX.at[1 - ds, R + 1]
        else:
            src, dst = DX.at[1, R], DX.at[1 - ds, 0]
        c = copy(src, dst, d_s.at[e], d_r.at[e], s + ds, r + dr)
        pl.when(inside(ds, dr))(c.start)
        pending.append((inside(ds, dr), c))
        dcopies.append((inside(-ds, -dr), c))

    for j in range(R):
        p = PRE[:, pl.ds(j * LANES, LANES)] + bcol
        soft = jnp.maximum(p, 0.0) + jnp.log(1.0 + jnp.exp(-jnp.abs(p)))
        act = leakage * p + (1.0 - leakage) * soft
        AIS[:, 0, j] = act.reshape(Pn, SHARE, LANES).astype(bf16)

    for b in range(3):
        whole = W1[2 - b].astype(f32).T
        blocks = []
        for a in range(3):
            for c_ in range(3):
                at = ((2 - a) * 3 + (2 - c_)) * C
                blocks.append(whole[at : at + C])
        W2[b] = jnp.concatenate(blocks, axis=1).astype(bf16)

    for b in range(3):
        for c in gsend[b]:
            c.wait_recv()
        acc = GR[b, 0].astype(f32)
        for q in range(1, Pn):
            acc = acc + GR[b, q].astype(f32)
        for j in range(g.NJ):
            t = b * g.NJ + j
            SB[t // g.T, t % g.T] = acc[:, j * LANES : (j + 1) * LANES].astype(bf16)
    for t in range(3 * g.NJ, M * g.T):
        SB[t // g.T, t % g.T] = jnp.zeros(tile, bf16)
    q1send = []
    for k in range(1, M):
        m, to_s = group_peer(k)
        c = copy(SB.at[m], Q1.at[member], q1_s.at[k], q1_r.at[k], to_s, r)
        start(c)
        q1send.append(c)
    Q1[member] = SB[member]

    for ok, c in dcopies:
        pl.when(ok)(c.wait_recv)
    for a in range(3):
        spread(lambda i, a=a: DX[a, i], DL, a)
    for c in q1send:
        c.wait_recv()
    acc = Q1[0].astype(f32)
    for m in range(1, M):
        acc = acc + Q1[m].astype(f32)
    Q2[block] = acc.astype(bf16)
    heard(1)
    early = len(pending)
    q2send = []
    for k in sorted(range(1, B), key=lambda k: -min(k, B - k)):
        c = copy(Q2.at[block], Q2.at[block], q2_s.at[k], q2_r.at[k], block_peer(k), r)
        start(c)
        q2send.append(c)
    PRE[...] = conv(W2, DL)
    for j in range(R):
        v = PRE[:, pl.ds(j * LANES, LANES)]
        AIS[:, 1, j] = v.reshape(Pn, SHARE, LANES).astype(bf16)
    isend = []
    for k in range(1, Pn):
        to = chan_peer(k)
        c = copy(AIS.at[to], AIR.at[r], i_s.at[k], i_r.at[k], s, to)
        start(c)
        isend.append(c)
    AIR[r] = AIS[r]
    sent_all(pending[:early])
    del pending[:early]

    for c in q2send:
        c.wait_recv()
    acc = Q2[0].astype(f32)
    for m in range(1, B):
        acc = acc + Q2[m].astype(f32)
    FIN[member] = acc * g.factor
    q3send = []
    for k in range(1, M):
        c = copy(FIN.at[member], FIN.at[member], q3_s.at[k], q3_r.at[k], group_peer(k)[1], r)
        start(c)
        q3send.append(c)
    for c in isend:
        c.wait_recv()
    for n, out in enumerate((act_o, ig_o)):
        TALL[n] = AIR[:, n].astype(f32).reshape(g.H * SHARE, LANES)
        for q in range(SHARE):
            out[q] = TALL[n, pl.ds(q, g.H, stride=SHARE), :].astype(bf16)
    for c in q3send:
        c.wait_recv()
    for a in range(3):
        for b in range(3):
            for c_ in range(3):
                at = (a * 3 + c_) * C
                t = b * g.NJ + at // LANES
                off = at % LANES
                wg_o[(a * 3 + b) * 3 + c_] = FIN[t // g.T, t % g.T][:, off : off + C]
    t = g.NJ - 1
    sums = FIN[t // g.T, t % g.T][:, edge : edge + 1]
    spot = lax.broadcasted_iota(jnp.int32, tile, 0) == lax.broadcasted_iota(jnp.int32, tile, 1)
    bg_o[...] = jnp.sum(jnp.where(spot, sums, 0.0), axis=0, keepdims=True)[:, :SHARE]

    sent_all(pending)


def deliver(act, ig, wg, bg, act_o, ig_o, wg_o, bg_o, sems):
    pairs = ((act, act_o), (ig, ig_o), (wg, wg_o), (bg, bg_o))
    moves = [pltpu.make_async_copy(a, b, sems.at[n]) for n, (a, b) in enumerate(pairs)]
    for c in moves:
        c.start()
    for c in moves:
        c.wait()


def shards(g, volume, weight, bias, upstream):
    Pn, R, C, M, B = g.P, g.R, g.C, g.M, g.B
    vol, up = volume[:, 0], upstream[:, 0]
    wl = jnp.transpose(weight, (2, 3, 4, 0, 1)).reshape(27, SHARE, C)
    sds = jax.ShapeDtypeStruct
    hbm = pl.BlockSpec(memory_space=pltpu.HBM)
    rows = (R + 2) * LANES
    dma = pltpu.SemaphoreType.DMA
    V = pltpu.VMEM
    chan = [dma((Pn,)), dma((Pn,))]
    scratch = [
        V((2, SHARE, g.H, LANES), bf16),
        V((27, SHARE, C), bf16),
        pltpu.SMEM((1, SHARE), f32),
        V((2, SHARE * g.H, LANES), f32),
        V((Pn, R + 2, SHARE, LANES), bf16),
        V((Pn, R, SHARE, LANES), bf16),
        V((Pn, 3 * g.NJ, SHARE, LANES), bf16),
        V((Pn, R + 2, SHARE, LANES), bf16),
        V((Pn, R, SHARE, LANES), bf16),
        V((Pn, 3 * g.NJ, SHARE, LANES), bf16),
        V((2, Pn, R + 2, SHARE, LANES), bf16),
        V((9 * C, rows), bf16),
        V((3, R + 2, C, LANES), bf16),
        V((9 * C, rows), bf16),
        V((3, C, g.KW), bf16),
        V((3, 3, C, 3 * C), bf16),
        V((3, C, g.KW), bf16),
        V((C, R * LANES), f32),
        V((C, R * LANES), bf16),
        V((Pn, 2, R, SHARE, LANES), bf16),
        V((Pn, 2, R, SHARE, LANES), bf16),
        V((3, C, g.KP), f32),
        V((3, Pn, SHARE, g.KP), bf16),
        V((3, Pn, SHARE, g.KP), bf16),
        V((M, g.T, SHARE, LANES), bf16),
        V((M, g.T, SHARE, LANES), bf16),
        V((B, g.T, SHARE, LANES), bf16),
        V((M, g.T, SHARE, LANES), f32),
        dma((4,)),
        *chan, *chan, *chan,
        pltpu.SemaphoreType.REGULAR((2,)),
        dma((2, Pn)), dma((2, Pn)),
        dma((8,)), dma((8,)),
        *chan,
        dma((3, Pn)), dma((3, Pn)),
        dma((M,)), dma((M,)),
        dma((B,)), dma((B,)),
        dma((M,)), dma((M,)),
    ]
    act, ig, wg, bg = pl.pallas_call(
        functools.partial(kernel, g),
        out_shape=(
            sds((SHARE, g.H, LANES), bf16),
            sds((SHARE, g.H, LANES), bf16),
            sds((27, SHARE, C), f32),
            sds((1, SHARE), f32),
        ),
        in_specs=[hbm] * 4,
        out_specs=(pl.BlockSpec(memory_space=pltpu.VMEM),) * 4,
        scratch_shapes=scratch,
        compiler_params=pltpu.CompilerParams(
            collective_id=0, has_side_effects=True, vmem_limit_bytes=40 << 20
        ),
    )(*(pltpu.with_memory_space_constraint(x, pltpu.HBM) for x in (vol, up, wl, bias[None])))
    act, ig, wg, bg = pl.pallas_call(
        deliver,
        out_shape=(
            sds((SHARE, g.H, LANES), bf16),
            sds((SHARE, g.H, LANES), bf16),
            sds((27, SHARE, C), f32),
            sds((1, SHARE), f32),
        ),
        in_specs=[pl.BlockSpec(memory_space=pl.ANY)] * 4,
        out_specs=(hbm,) * 4,
        scratch_shapes=[dma((4,))],
        compiler_params=pltpu.CompilerParams(vmem_limit_bytes=1 << 20),
    )(act, ig, wg, bg)
    wgrad = jnp.transpose(wg.reshape(3, 3, 3, SHARE, C), (3, 4, 0, 1, 2))
    return act[:, None], ig[:, None], wgrad, bg[0]


def solution(mesh, rows=48, halves=2, blocks=8):
    planes, ranks = mesh.shape["space"], mesh.shape["chan"]
    factor = 1.0 / math.sqrt(planes * rows * LANES)
    g = Plan(planes, ranks, rows, halves, blocks, factor)
    field = P("chan", "space", None, None)
    filters = P("chan", None, None, None, None)
    return jax.shard_map(
        functools.partial(shards, g),
        mesh=mesh,
        in_specs=(field, filters, P("chan"), field),
        out_specs=(field, field, filters, P("chan")),
        check_vma=False,
    )
```
